32 devices in a mesh: dp: 8 (over y, x, core), tp: 4 (over z).
Axes of the slice: x: 2, y: 2, z: 4, core: 2. Of those that a mesh axis runs over, the one named last changes fastest.
Arguments:
- tokens: bfloat16 [8, 512, 768], P('dp', 'tp'), may hold values from -6 to 6
- seg_ids: int32 [8, 512], P('dp'), may hold values from 0 to 2, never falling along the last dimension, each value on 1 to 256 neighbouring positions
- time_embed: float32 [8, 3, 768], P('dp'), may hold values from -6 to 6
- text_states: bfloat16 [8, 3, 64, 768], P('dp', None, 'tp'), may hold values from -6 to 6
- text_lengths: int32 [8, 3], P('dp'), may hold values from 16 to 64, as said below
- out_grad: bfloat16 [8, 512, 768], P('dp', 'tp'), may hold values from -6 to 6
- w_qkv: bfloat16 [768, 2304], P(None, 'tp'), may hold values from -0.21875 to 0.21875
- w_attn_out: bfloat16 [768, 768], P('tp'), may hold values from -3 to 3
- b_attn_out: bfloat16 [768], replicated, may hold values from -3 to 3
- w_cross_q: bfloat16 [768, 768], P(None, 'tp'), may hold values from -0.21875 to 0.21875
- w_cross_kv: bfloat16 [768, 1536], P(None, 'tp'), may hold values from -0.21875 to 0.21875
- w_cross_out: bfloat16 [768, 768], P('tp'), may hold values from -0.875 to 0.875
- b_cross_out: bfloat16 [768], replicated, may hold values from -3 to 3
- w_up: bfloat16 [768, 3072], P(None, 'tp'), may hold values from -0.21875 to 0.21875
- b_up: bfloat16 [3072], P('tp'), may hold values from -3 to 3
- w_down: bfloat16 [3072, 768], P('tp'), may hold values from -0.109375 to 0.109375
- w_mod: bfloat16 [768, 4608], P(None, 'tp'), may hold values from -0.21875 to 0.21875
- b_mod: bfloat16 [4608], P('tp'), may hold values from -3 to 3
Outputs:
- d_tokens: bfloat16 [8, 512, 768], P('dp', 'tp')
- d_time: float32 [8, 3, 768], P('dp')
- d_text: bfloat16 [8, 3, 64, 768], P('dp', None, 'tp')
- g_qkv: float32 [768, 2304], P(None, 'tp')
- g_attn_out: float32 [768, 768], P('tp')
- gb_attn_out: float32 [768], replicated
- g_cross_q: float32 [768, 768], P(None, 'tp')
- g_cross_kv: float32 [768, 1536], P(None, 'tp')
- g_cross_out: float32 [768, 768], P('tp')
- gb_cross_out: float32 [768], replicated
- g_up: float32 [768, 3072], P(None, 'tp')
- gb_up: float32 [3072], P('tp')
- g_down: float32 [3072, 768], P('tp')
- g_mod: float32 [768, 4608], P(None, 'tp')
- gb_mod: float32 [4608], P('tp')
The draws below stay inside these ranges and needn't reach their ends.
Inputs may be any that keep to these rules, and one draw needn't show every extreme that they name: `seg_ids`: along a group's row item numbers never fall and every item of 0 to 2 has 1 to 256 frames. `text_lengths`: in every group one item has all 64 text tokens valid.
All inputs are finite; a program needn't handle non-finite values.
Results may differ from the reference program's by a relative error of at most 0.02.
Values may be sent and summed in bfloat16 or wider, within the bound.
A program may use at most 128 MiB of HBM per device.

```python
import math
import jax
import jax.numpy as jnp
import numpy as np
from jax import lax

D = 768
H = 12
DH = 64
FF = 3072
TOK_DEV = 512
ITEMS_DEV = 3
TXT = 64
MAXLEN = 256
GROUPS = 8


def draw_text_lengths(key, part):
    first, second = jax.random.split(jax.random.fold_in(key, 7))
    lengths = jax.random.randint(first, (GROUPS, ITEMS_DEV), TXT // 4, TXT + 1)
    picked = jax.random.randint(second, (GROUPS, 1), 0, ITEMS_DEV)
    slots = jnp.arange(ITEMS_DEV, dtype=jnp.int32)[None, :]
    return jnp.where(slots == picked, TXT, lengths).astype(jnp.int32)


def block_scale(own_key, dims, pieces, low, largest):
    gain, own = 1.0, jax.random.fold_in(own_key, 6)
    for axis_at, parts in pieces:
        draws = jnp.exp(jax.random.uniform(jax.random.fold_in(own, axis_at), (parts,), jnp.float32, low / len(pieces), largest / len(pieces)))
        gain = gain * jnp.repeat(draws, dims[axis_at] // parts).reshape([-1 if axis == axis_at else 1 for axis in range(len(dims))])
    return gain


def length_profile(amount, total, bound, skew):
    weights = [(1 << 20) // math.isqrt(rank ** skew) + 1 for rank in range(2, amount + 1)]
    rest, holding = total - bound - (amount - 1), [1] * (amount - 1)
    while rest > 0:
        free = [i for i in range(amount - 1) if holding[i] < bound]
        mass, remaining = sum([weights[i] for i in free]), rest
        for i in free:
            more = min(bound - holding[i], max(1, remaining * weights[i] // mass), rest)
            holding[i] = holding[i] + more
            rest = rest - more
    return np.array([bound] + holding)


def ragged(rng, amount, total, reach, lean):
    if amount == 2:
        one = jax.random.randint(rng, (), max(1, total - reach), min(reach, total - 1) + 1)
        return jnp.stack([one, total - one])
    sizes = jnp.asarray(length_profile(amount, total, reach, lean), jnp.int32)
    twos = (amount - 1) // 2
    source_of, sink = sizes[1:1 + 2 * twos:2], sizes[2:2 + 2 * twos:2]
    room = jnp.minimum(source_of - 1, reach - sink)
    passed = jax.random.randint(jax.random.fold_in(rng, 1), (twos,), 0, 1 << 20) % (room + 1)
    sizes = sizes.at[1:1 + 2 * twos:2].set(source_of - passed).at[2:2 + 2 * twos:2].set(sink + passed)
    return sizes[jax.random.permutation(jax.random.fold_in(rng, 2), amount)]


def centred(stream_key, shape, width, reach, cuts=(), kind=jnp.bfloat16):
    values = width * jax.random.normal(stream_key, shape, jnp.float32)
    if cuts:
        values = values * block_scale(stream_key, shape, cuts, -0.22, 0.18)
    return jnp.clip(values, -reach, reach).astype(kind)


def setup_inputs(seed: int = 0) -> dict:
    key_of = jax.random.split(jax.random.key(seed), 19)
    tokens = centred(key_of[0], (GROUPS, TOK_DEV, D), 1.0, 6.0, ((0, 8), (1, 4)))
    seg_ids = jax.vmap(lambda own: jnp.searchsorted(jnp.cumsum(ragged(own, ITEMS_DEV, TOK_DEV, MAXLEN, 2)), jnp.arange(TOK_DEV), side="right"))(jax.random.split(key_of[1], GROUPS)).reshape((GROUPS, TOK_DEV)).astype(jnp.int32)
    time_embed = centred(key_of[2], (GROUPS, ITEMS_DEV, D), 1.0, 6.0, ((0, 8),), jnp.float32)
    text_states = centred(key_of[3], (GROUPS, ITEMS_DEV, TXT, D), 1.0, 6.0, ((0, 8), (2, 4)))
    text_lengths = draw_text_lengths(jax.random.fold_in(key_of[18], 71), 0)
    out_grad = centred(key_of[5], (GROUPS, TOK_DEV, D), 1.0, 6.0, ((0, 8), (1, 4)))
    w_qkv = centred(key_of[6], (D, 3 * D), D ** -0.5, 0.21875, ((1, 4),))
    w_attn_out = centred(key_of[7], (D, D), (max(D // 192, 1)) ** -0.5, 3.0, ((0, 4),))
    b_attn_out = centred(key_of[8], (D,), 0.5, 3.0)
    w_cross_q = centred(key_of[9], (D, D), D ** -0.5, 0.21875, ((1, 4),))
    w_cross_kv = centred(key_of[10], (D, 2 * D), D ** -0.5, 0.21875, ((1, 4),))
    w_cross_out = centred(key_of[11], (D, D), (max(D // 16, 1)) ** -0.5, 0.875, ((0, 4),))
    b_cross_out = centred(key_of[12], (D,), 0.5, 3.0)
    w_up = centred(key_of[13], (D, FF), D ** -0.5, 0.21875, ((1, 4),))
    b_up = centred(key_of[14], (FF,), 0.5, 3.0, ((0, 4),))
    w_down = centred(key_of[15], (FF, D), FF ** -0.5, 0.109375, ((0, 4),))
    w_mod = centred(key_of[16], (D, 6 * D), D ** -0.5, 0.21875, ((1, 4),))
    b_mod = centred(key_of[17], (6 * D,), 0.5, 3.0, ((0, 4),))
    return {"tokens": tokens, "seg_ids": seg_ids, "time_embed": time_embed, "text_states": text_states, "text_lengths": text_lengths, "out_grad": out_grad, "w_qkv": w_qkv, "w_attn_out": w_attn_out, "b_attn_out": b_attn_out, "w_cross_q": w_cross_q, "w_cross_kv": w_cross_kv, "w_cross_out": w_cross_out, "b_cross_out": b_cross_out, "w_up": w_up, "b_up": b_up, "w_down": w_down, "w_mod": w_mod, "b_mod": b_mod}


@jax.custom_vjp
def low(v):
    return lax.optimization_barrier(v.astype(jnp.bfloat16)).astype(jnp.float32)

@jax.custom_vjp
def low_back(v):
    return v

def low_keep(v):
    return (low(v), None)

def low_pass(kept, grad):
    return (grad,)

def back_keep(v):
    return (v, None)

def back_low(kept, grad):
    return (low(grad),)
low.defvjp(low_keep, low_pass)
low_back.defvjp(back_keep, back_low)

def matmul_high(left, right):
    return jnp.dot(left, right, precision=lax.Precision.HIGHEST)

def layer_norm(values):
    center = values - lax.optimization_barrier(jnp.mean(values, axis=-1, keepdims=True))
    return center * lax.rsqrt(lax.optimization_barrier(jnp.mean(center * center, axis=-1, keepdims=True)) + 1e-06)

def attention(query, keys, values, row_tag, key_tag):
    rows = query.shape[0]
    block_rows = min(512, rows)
    scaling = 1.0 / math.sqrt(DH)

    def one_block(inputs):
        query_block, tag_block = inputs
        scores = low_back(scaling * jnp.einsum('rhd,khd->hrk', query_block, keys, precision=lax.Precision.HIGHEST))
        allowed = (tag_block[:, None] == key_tag[None, :])[None]
        scores = jnp.where(allowed, scores, -1000000000.0)
        peak = lax.optimization_barrier(jnp.max(scores, axis=-1, keepdims=True))
        exponent = jnp.exp(scores - peak)
        probs = low(exponent / lax.optimization_barrier(jnp.sum(exponent, axis=-1, keepdims=True)))
        return jnp.einsum('hrk,khd->rhd', probs, values, precision=lax.Precision.HIGHEST)
    blocks = lax.map(jax.checkpoint(one_block), (query.reshape(rows // block_rows, block_rows, query.shape[1], DH), row_tag.reshape(rows // block_rows, block_rows)))
    return blocks.reshape(rows, -1)

def group_forward(stream_in, time_embed, text_states, w_qkv, w_attn_out, b_attn_out, w_cross_q, w_cross_kv, w_cross_out, b_cross_out, w_up, b_up, w_down, w_mod, b_mod, segment, lengths):
    frames = stream_in.shape[0]
    silu_low = low(jax.nn.silu(time_embed))
    modulation = low_back(matmul_high(silu_low, w_mod) + b_mod)
    item_ids = jnp.arange(ITEMS_DEV, dtype=jnp.int32)
    onehot = (segment[:, None] == item_ids[None, :]).astype(stream_in.dtype)
    per_frame = matmul_high(onehot, modulation)
    shift_a, scale_a, gate_a, shift_m, scale_m, gate_m = jnp.split(per_frame, 6, axis=1)
    attn_in = low(layer_norm(stream_in) * (1.0 + scale_a) + shift_a)
    qkv = low(low_back(matmul_high(attn_in, w_qkv))).reshape(frames, H, 3, DH)
    attended = low(low_back(attention(qkv[:, :, 0], qkv[:, :, 1], qkv[:, :, 2], segment, segment)))
    branch_a = low_back(matmul_high(attended, w_attn_out) + b_attn_out)
    stream_a = stream_in + gate_a * branch_a
    cross_in = low(layer_norm(stream_a))
    cross_query = low(low_back(matmul_high(cross_in, w_cross_q))).reshape(frames, H, DH)
    cross_kv = low(low_back(matmul_high(text_states.reshape(ITEMS_DEV * TXT, D), w_cross_kv))).reshape(ITEMS_DEV * TXT, H, 2, DH)
    key_index = jnp.arange(ITEMS_DEV * TXT, dtype=jnp.int32)
    key_item = key_index // TXT
    key_tag = jnp.where(key_index % TXT < lengths[key_item], key_item, -1).astype(jnp.int32)
    cross_attended = low(low_back(attention(cross_query, cross_kv[:, :, 0], cross_kv[:, :, 1], segment, key_tag)))
    branch_c = low_back(matmul_high(cross_attended, w_cross_out) + b_cross_out)
    stream_c = stream_a + branch_c
    mlp_in = low(layer_norm(stream_c) * (1.0 + scale_m) + shift_m)
    pre = low_back(matmul_high(mlp_in, w_up) + b_up)
    act = low(jax.nn.gelu(pre, approximate=True))
    branch_m = low_back(matmul_high(act, w_down))
    return stream_c + gate_m * branch_m

def reference(tokens, seg_ids, time_embed, text_states, text_lengths, out_grad, w_qkv, w_attn_out, b_attn_out, w_cross_q, w_cross_kv, w_cross_out, b_cross_out, w_up, b_up, w_down, w_mod, b_mod):
    weights = tuple((w.astype(jnp.float32) for w in (w_qkv, w_attn_out, b_attn_out, w_cross_q, w_cross_kv, w_cross_out, b_cross_out, w_up, b_up, w_down, w_mod, b_mod)))

    def one_group(totals, inputs):
        frames, segment, embed, text, lengths, cotangent = inputs

        def forward(stream_in, embed_in, text_in, *params):
            return group_forward(stream_in, embed_in, text_in, *params, segment, lengths)
        output, pull = jax.vjp(forward, frames.astype(jnp.float32), embed.astype(jnp.float32), text.astype(jnp.float32), *weights)
        grads = pull(cotangent.astype(jnp.float32))
        totals = tuple((a + b for a, b in zip(totals, grads[3:])))
        return (totals, (grads[0].astype(jnp.bfloat16), grads[1], grads[2].astype(jnp.bfloat16)))
    start = tuple((jnp.zeros_like(w) for w in weights))
    totals, outputs = lax.scan(one_group, start, (tokens, seg_ids, time_embed, text_states, text_lengths, out_grad))
    d_tokens, d_time, d_text = outputs
    return (d_tokens, d_time, d_text, totals[0], totals[1], totals[2], totals[3], totals[4], totals[5], totals[6], totals[7], totals[8], totals[9], totals[10], totals[11])
```

```python
import functools
import math

import jax
import jax.numpy as jnp
from jax import lax
from jax.experimental import pallas as pl
from jax.experimental.pallas import tpu as pltpu
from jax.sharding import PartitionSpec as P

DH = 64
TP = 4
MESH = pl.DeviceIdType.MESH
BF = jnp.bfloat16
F32 = jnp.float32
GELU_C = math.sqrt(2.0 / math.pi)


def dot_nn(left, right):
    return jnp.dot(left, right, preferred_element_type=F32)


def dot_tn(left, right):
    return lax.dot_general(left, right, (((0,), (0,)), ((), ())), preferred_element_type=F32)


def dot_nt(left, right):
    return lax.dot_general(left, right, (((1,), (1,)), ((), ())), preferred_element_type=F32)


def normalize(values):
    center = values - jnp.mean(values, axis=-1, keepdims=True)
    inverse = lax.rsqrt(jnp.mean(center * center, axis=-1, keepdims=True) + 1e-06)
    return center * inverse, inverse


def normalize_back(grad, normed, inverse):
    return inverse * (
        grad
        - jnp.mean(grad, axis=-1, keepdims=True)
        - normed * jnp.mean(grad * normed, axis=-1, keepdims=True)
    )


def bucket_rows(hidden, heads_width):
    sizes = [
        ("up", hidden),
        ("down", hidden),
        ("cross_out", heads_width),
        ("cross_q", heads_width),
        ("cross_kv", 2 * heads_width),
        ("attn_out", heads_width),
        ("qkv", 3 * heads_width),
    ]
    at, place = 0, {}
    for name, rows in sizes:
        place[name] = (at, rows)
        at += rows
    return place, at


def layer_kernel(
    dims,
    tok_h, og_h, text_h, wqkv_h, wo_h, wcq_h, wckv_h, wco_h, wup_h, wdn_h, wmod_h,
    seg_ref, time_ref, small_ref, tlen_ref,
    dtok_o, dtime_o, dtext_o, grads_o, early_o, late_o,
    tok, og, text, att, gc,
    wqkv, wqkvT, wcq, wckv, wfull, wup, wdn, wmod,
    modbuf, mods, segrow, segcol, onehot, ktag,
    attn_in, na, qkvT, kvx, pself,
    stream_a, inv_c, cross_in, cqT, ckvT, kx, vx, pcross, catT, branch_own,
    mlp_in, nm_own, invm_own, inva_own, act, dpre, dbm, rs_send, rs_recv,
    gc_own, dcT, dcqT, dckv, dckvT, grad_own, dba, dOT, dqkvT,
    rs2_send, rs2_recv, dm, dmp, dmr, dsil, dsr, early, late, eall, lall,
    grads, rbuf,
    lsem, ssem, rsem, wsem_s, wsem_r, gsem_s, gsem_r, esem_s, esem_r, osem,
):
    dp_count, place, items, txt = dims
    tp = lax.axis_index("tp")
    dp = lax.axis_index("dp")
    R = tok.shape[1]
    D = tok.shape[2]
    T = TP * R
    HW = att.shape[1]
    HL = HW // DH
    TK = TP * text.shape[1]
    TL = text.shape[1]
    HEADS = TP * HL
    MB = modbuf.shape[2]
    scale = 1.0 / math.sqrt(DH)
    sub = lax.rem(dp, 8)
    base8 = dp - sub
    core = lax.rem(sub, 2)
    chip = sub // 2

    def tp_peer(k):
        return {"tp": lax.rem(tp + k, TP)}

    def remote(src, dst, send, recv, peer):
        return pltpu.make_async_remote_copy(
            src_ref=src, dst_ref=dst, send_sem=send, recv_sem=recv, device_id=peer, device_id_type=MESH
        )

    loads = [
        (wmod_h, wmod),
        (tok_h, tok.at[0]),
        (text_h, text.at[0]),
        (wqkv_h, wqkv),
        (wcq_h, wcq),
        (wo_h, wfull.at[0, 0]),
        (wco_h, wfull.at[0, 2]),
        (wckv_h, wckv),
        (og_h, og.at[0]),
        (wup_h, wup),
        (wdn_h, wdn),
    ]
    local = [pltpu.make_async_copy(src, dst, lsem.at[i]) for i, (src, dst) in enumerate(loads)]
    for copy in local:
        copy.start()

    barrier = pltpu.get_barrier_semaphore()
    for k in range(1, TP):
        pl.semaphore_signal(barrier, inc=1, device_id=tp_peer(k), device_id_type=MESH)

    def greet(k, carry):
        pl.semaphore_signal(
            barrier, inc=1, device_id={"dp": lax.rem(dp + k, dp_count)}, device_id_type=MESH
        )
        return carry

    lax.fori_loop(1, dp_count, greet, 0)

    time = time_ref[...]
    sig = 1.0 / (1.0 + jnp.exp(-time))
    silu_low = (time * sig).astype(BF)
    early[...] = jnp.zeros(early.shape, F32)
    early[0:items, :] = silu_low.astype(F32)
    silu_pad = early[...].astype(BF)
    local[0].wait()
    b_mod = small_ref[:, 3 * D : 3 * D + MB]
    modbuf[tp] = dot_nn(silu_pad, wmod[...]) + b_mod

    pl.semaphore_wait(barrier, TP - 1 + dp_count - 1)

    pending = []

    def direct(tag, src_of, dst_of):
        copies = []
        for k in range(1, TP):
            copy = remote(src_of(k), dst_of(k), ssem.at[tag, k], rsem.at[tag, TP - k], tp_peer(k))
            copy.start()
            copies.append(copy)
        pending.extend(copies)
        return copies

    local[1].wait()
    tok_copies = direct(0, lambda k: tok.at[0], lambda k: tok.at[TP - k])
    mod_copies = direct(1, lambda k: modbuf.at[tp], lambda k: modbuf.at[tp])
    local[2].wait()
    text_copies = direct(2, lambda k: text.at[0], lambda k: text.at[TP - k])

    def arrived(copies, slot):
        copies[TP - 1 - slot].wait_recv()

    eye = lax.broadcasted_iota(jnp.int32, (R, R), 0) == lax.broadcasted_iota(jnp.int32, (R, R), 1)
    for slot in range(TP):
        owner = lax.rem(tp + slot, TP)
        row = seg_ref[:, pl.ds(pl.multiple_of(owner * R, R), R)].astype(F32)
        segrow[:, slot * R : (slot + 1) * R] = row
        col = jnp.sum(jnp.where(eye, row, 0.0), axis=1, keepdims=True)
        segcol[slot * R : (slot + 1) * R, :] = col
    kinds = lax.broadcasted_iota(jnp.int32, (16, T), 0)
    matches = (segrow[...] == kinds.astype(F32)) & (kinds < items)
    onehot[...] = jnp.where(matches | (kinds == items), 1.0, 0.0).astype(BF)
    key_at = lax.broadcasted_iota(jnp.int32, (TK, 1), 0)
    key_slot = key_at // TL
    key_item = lax.rem(key_at, TL) // (TL // items)
    key_pos = lax.rem(key_slot + tp, TP) * (TL // items) + lax.rem(key_at, TL // items)
    tag = jnp.full((TK, 1), -1.0, F32)
    for item in range(items):
        inside = (key_item == item) & (key_pos < tlen_ref[0, item])
        tag = jnp.where(inside, float(item), tag)
    ktag[...] = tag

    ident = jnp.where(
        lax.broadcasted_iota(jnp.int32, (D, D), 0) == lax.broadcasted_iota(jnp.int32, (D, D), 1), 1.0, 0.0
    ).astype(BF)
    local[3].wait()
    wqkvT[...] = dot_tn(wqkv[...], ident).astype(BF)
    local[4].wait()
    wfull[0, 1] = dot_tn(wcq[...], ident).astype(BF)
    local[7].wait()
    wckvT = dot_tn(wckv[...], ident).astype(BF)
    wfull[0, 3] = wckvT[:HW]
    wfull[0, 4] = wckvT[HW:]
    local[5].wait()
    local[6].wait()

    for k in range(1, TP):
        arrived(mod_copies, k)
    for j in range(6):
        lo, hi = j * D, (j + 1) * D
        at = lo
        while at < hi:
            block = at // MB
            end = min(hi, (block + 1) * MB)
            mods[j, :, at - lo : end - lo] = modbuf[block, :, at - block * MB : end - block * MB]
            at = end

    def per_frame(j, slot):
        col = segcol[slot * R : (slot + 1) * R, :]
        out = mods[j, items - 1 : items, :]
        for item in range(items - 2, -1, -1):
            out = jnp.where(col == float(item), mods[j, item : item + 1, :], out)
        return out

    def item_sums(slot, values):
        return dot_nn(onehot[:, slot * R : (slot + 1) * R], values.astype(BF))

    order = (0, 1, 3, 2)
    for slot in order:
        if slot:
            arrived(tok_copies, slot)
        rows = slice(slot * R, (slot + 1) * R)
        normed, inverse = normalize(tok[slot].astype(F32))
        na[rows, :] = normed.astype(BF)
        if slot == 0:
            inva_own[...] = inverse
        x = (normed * (1.0 + per_frame(1, slot)) + per_frame(0, slot)).astype(BF)
        attn_in[rows, :] = x
        qkvT[:, rows] = dot_nt(wqkvT[...], x).astype(BF)

    WR, WC = HW // 4, D // 2
    wrow = pl.multiple_of(chip * WR, 16)
    wcol = pl.multiple_of(core * WC, 128)
    wz = []
    for k in range(1, TP):
        copy = remote(
            wfull.at[0, :, pl.ds(wrow, WR), pl.ds(wcol, WC)],
            wfull.at[TP - k, :, pl.ds(wrow, WR), pl.ds(wcol, WC)],
            wsem_s.at[k], wsem_r.at[TP - k], tp_peer(k),
        )
        copy.start()
        wz.append(copy)
    pending.extend(wz)

    att_copies = []
    for h in range(HL):
        q0 = h * 3 * DH
        kT = qkvT[q0 + DH : q0 + 2 * DH, :]
        keys = (kT.astype(F32).T * scale).astype(BF)
        kvx[2 * h] = keys
        kvx[2 * h + 1] = qkvT[q0 + 2 * DH : q0 + 3 * DH, :].astype(F32).T.astype(BF)
        vT = qkvT[q0 + 2 * DH : q0 + 3 * DH, :]
        for b in range(TP):
            cols = slice(b * R, (b + 1) * R)
            scores = dot_nn(keys, qkvT[q0 : q0 + DH, cols])
            scores = jnp.where(segcol[...] == segrow[:, cols], scores, -1000000000.0)
            peak = jnp.max(scores, axis=0, keepdims=True)
            exponent = jnp.exp(scores - peak)
            probs = exponent * (1.0 / jnp.sum(exponent, axis=0, keepdims=True))
            pself[h, :, cols] = probs
            att[0, h * DH : (h + 1) * DH, cols] = dot_nn(vT, probs.astype(BF)).astype(BF)
        hr = slice(h * DH, (h + 1) * DH)
        att_copies.append(
            direct(3 + h, lambda k: att.at[0, hr], lambda k: att.at[TP - k, hr])
        )
    local[8].wait()
    og_copies = direct(3 + HL, lambda k: og.at[0], lambda k: og.at[TP - k])

    for copy in wz:
        copy.wait_recv()
    wx = []
    for m in range(1, 4):
        peer = {"dp": base8 + jnp.bitwise_xor(sub, 2 * m)}
        copy = remote(
            wfull.at[1:TP, :, pl.ds(wrow, WR), pl.ds(wcol, WC)],
            wfull.at[1:TP, :, pl.ds(wrow, WR), pl.ds(wcol, WC)],
            wsem_s.at[3 + m], wsem_r.at[3 + m], peer,
        )
        copy.start()
        wx.append(copy)
    for copy in wx:
        copy.wait_recv()
    wlast = remote(
        wfull.at[1:TP, :, :, pl.ds(wcol, WC)],
        wfull.at[1:TP, :, :, pl.ds(wcol, WC)],
        wsem_s.at[7], wsem_r.at[7], {"dp": base8 + jnp.bitwise_xor(sub, 1)},
    )
    wlast.start()
    pending.extend(wx + [wlast])
    for k in range(1, TP):
        arrived(text_copies, k)
    wlast.wait_recv()

    def full(i):
        return wfull[:, i].reshape(TP * HW, D)

    text_flat = text[...].reshape(TK, D)
    for s in range(TP):
        for part in range(2):
            ckvT[(2 * s + part) * HW : (2 * s + part + 1) * HW, :] = dot_nt(wfull[s, 3 + part], text_flat).astype(BF)
    for h in range(HEADS):
        pair = ckvT[h * 2 * DH : (h + 1) * 2 * DH, :].astype(F32).T
        kx[h] = (pair[:, :DH] * scale).astype(BF)
        vx[h] = pair[:, DH:].astype(BF)

    b_attn_out = small_ref[:, 0:D]
    b_cross_out = small_ref[:, D : 2 * D]
    b_up = small_ref[:, 2 * D : 3 * D]
    for copies in att_copies:
        for k in range(1, TP):
            arrived(copies, k)
    for b in range(TP):
        rows = slice(b * R, (b + 1) * R)
        gathered = jnp.concatenate(
            [att[k, :, ((b - k) % TP) * R : ((b - k) % TP + 1) * R] for k in range(TP)], axis=0
        )
        branch = dot_tn(gathered, full(0)) + b_attn_out
        if b == 0:
            branch_own[...] = branch
        stream = tok[b].astype(F32) + per_frame(2, b) * branch
        stream_a[rows, :] = stream
        normed, inverse = normalize(stream)
        inv_c[rows, :] = inverse
        x = normed.astype(BF)
        cross_in[rows, :] = x
        cqT[:, rows] = dot_nt(full(1), x).astype(BF)
        allowed = ktag[...] == segrow[:, rows]
        for h in range(HEADS):
            hr = slice(h * DH, (h + 1) * DH)
            scores = dot_nn(kx[h], cqT[hr, rows])
            scores = jnp.where(allowed, scores, -1000000000.0)
            peak = jnp.max(scores, axis=0, keepdims=True)
            exponent = jnp.exp(scores - peak)
            probs = exponent * (1.0 / jnp.sum(exponent, axis=0, keepdims=True))
            pcross[h, :, rows] = probs
            vT = ckvT[h * 2 * DH + DH : (h + 1) * 2 * DH, :]
            catT[hr, rows] = dot_nn(vT, probs.astype(BF)).astype(BF)
        stream = stream_a[rows, :] + dot_tn(catT[:, rows], full(2)) + b_cross_out
        normed, inverse = normalize(stream)
        if b == 0:
            nm_own[...] = normed
            invm_own[...] = inverse
        mlp_in[rows, :] = (normed * (1.0 + per_frame(4, b)) + per_frame(3, b)).astype(BF)

    local[9].wait()
    local[10].wait()
    gate_sum = jnp.zeros((16, D), F32)
    gb_up = jnp.zeros((16, D), F32)
    rs_copies = {}
    for b in (2, 1, 3, 0):
        rows = slice(b * R, (b + 1) * R)
        if b:
            arrived(og_copies, b)
        pre = dot_nn(mlp_in[rows, :], wup[...]) + b_up
        square = pre * pre
        inner = jnp.tanh(GELU_C * pre * (1.0 + 0.044715 * square))
        low = (0.5 * pre * (1.0 + inner)).astype(BF)
        act[rows, :] = low
        slope = 0.5 * (1.0 + inner) + 0.5 * pre * (1.0 - inner * inner) * (
            GELU_C * (1.0 + 3.0 * 0.044715 * square)
        )
        grad = og[b].astype(F32)
        gate_sum = gate_sum + item_sums(b, grad * dot_nn(low, wdn[...]))
        d_branch = (grad * per_frame(5, b)).astype(BF)
        dbm[rows, :] = d_branch
        d_pre = (dot_nt(d_branch, wdn[...]) * slope).astype(BF)
        dpre[rows, :] = d_pre
        gb_up = gb_up + item_sums(b, d_pre)
        rs_send[b] = dot_nt(d_pre, wup[...]).astype(BF)
        if b:
            copy = remote(
                rs_send.at[b], rs_recv.at[TP - 1 - b], ssem.at[4 + HL, b], rsem.at[4 + HL, TP - b], tp_peer(b)
            )
            copy.start()
            rs_copies[b] = copy
    pending.extend(rs_copies.values())
    dm[5] = gate_sum
    early[3:4, :] = gb_up[items : items + 1, :]

    bits = []
    step = 8
    while step < dp_count:
        bits.append(step)
        step *= 2

    class Reduce:
        def __init__(self, index, start, rows, room):
            self.parts = []
            half = rows // 2
            for part in range(2):
                chain = (1, 2, 4) if part == 0 else (1, 4, 2)
                self.parts.append((start + part * half, half, chain, part * half))
            self.index, self.room = index, room
            self.open, self.own = [], []

        def sem(self, part, step):
            return gsem_s.at[self.index, part, step], gsem_r.at[self.index, part, step]

        def launch(self, src, dst, part, step, bit):
            send, recv = self.sem(part, step)
            copy = remote(src, dst, send, recv, {"dp": jnp.bitwise_xor(dp, bit)})
            copy.start()
            pending.append(copy)
            return copy

        def bounds(self, part, level):
            start, rows, chain, _ = self.parts[part]
            at, size = start, rows
            for bit in chain[:level]:
                size //= 2
                at = at + jnp.bitwise_and(dp // bit, 1) * size
            return at, size

        def scatter_start(self, level):
            self.open = []
            for part in range(2):
                at, size = self.bounds(part, level)
                bit = self.parts[part][2][level]
                half = size // 2
                mine = jnp.bitwise_and(dp // bit, 1)
                other = pl.multiple_of(at + (1 - mine) * half, 16)
                rows = self.parts[part][1]
                room = self.room + 2 * (rows - (rows >> level)) + part * half
                copy = self.launch(
                    grads.at[pl.ds(other, half)], rbuf.at[room : room + half], part, level, bit
                )
                self.open.append((copy, room, half))

        def scatter_end(self, level):
            for part in range(2):
                copy, room, half = self.open[part]
                copy.wait_recv()
                at, size = self.bounds(part, level + 1)
                mine = pl.ds(pl.multiple_of(at, 16), half)
                grads[mine, :] = (grads[mine, :].astype(F32) + rbuf[room : room + half, :].astype(F32)).astype(BF)

        def widen(self):
            for i, bit in enumerate(bits):
                for part in range(2):
                    at, size = self.bounds(part, 3)
                    rows = self.parts[part][1]
                    mine = pl.ds(pl.multiple_of(at, 16), size)
                    room = self.room + 2 * (rows - rows // 8) + (2 * i + part) * size
                    copy = self.launch(grads.at[mine], rbuf.at[room : room + size], part, 6 + i, bit)
                    copy.wait_recv()
                    grads[mine, :] = (
                        grads[mine, :].astype(F32) + rbuf[room : room + size, :].astype(F32)
                    ).astype(BF)

        def gather_start(self, level):
            self.open = []
            source = grads if level == 2 else grads_o
            if level == 1:
                for copy in self.own:
                    copy.wait()
            for part in range(2):
                at, size = self.bounds(part, level + 1)
                bit = self.parts[part][2][level]
                mine = pl.ds(pl.multiple_of(at, 16), size)
                self.open.append(
                    self.launch(source.at[mine], grads_o.at[mine], part, 3 + (2 - level), bit)
                )
                if level == 2:
                    copy = pltpu.make_async_copy(grads.at[mine], grads_o.at[mine], osem.at[self.index, part])
                    copy.start()
                    self.own.append(copy)

        def gather_end(self):
            for copy in self.open:
                copy.wait_recv()

    mid0 = place["cross_out"][0]
    mid1 = place["attn_out"][0]
    total_rows = grads.shape[0]
    extra = 2 * len(bits)
    rooms, at = [], 0
    for rows in (mid0, mid1 - mid0, total_rows - mid1):
        rooms.append(at)
        at += rows - rows // 8 + extra * (rows // 16)
    reduce_mlp = Reduce(0, 0, mid0, rooms[0])
    reduce_cross = Reduce(1, mid0, mid1 - mid0, rooms[1])
    reduce_self = Reduce(2, mid1, total_rows - mid1, rooms[2])

    def put(name, values):
        at, rows = place[name]
        grads[at : at + rows, :] = values.astype(BF)

    put("up", dot_tn(mlp_in[...], dpre[...]))
    put("down", dot_tn(act[...], dbm[...]))
    reduce_mlp.scatter_start(0)

    d_mlp = rs_send[0].astype(F32)
    reduce_mlp.scatter_end(0)
    reduce_mlp.scatter_start(1)
    for k in (1, 3, 2):
        rs_copies[TP - k].wait_recv()
        d_mlp = d_mlp + rs_recv[k - 1].astype(F32)
    normed = nm_own[...]
    dm[3] = item_sums(0, d_mlp)
    dm[4] = item_sums(0, d_mlp * normed)
    grad_c = og[0].astype(F32) + normalize_back(d_mlp * (1.0 + per_frame(4, 0)), normed, invm_own[...])
    gc_own[...] = grad_c
    gc[0] = grad_c.astype(BF)
    gc_copies = direct(5 + HL, lambda k: gc.at[0], lambda k: gc.at[TP - k])

    dckv[...] = jnp.zeros(dckv.shape, F32)
    for slot in order:
        rows = slice(slot * R, (slot + 1) * R)
        if slot:
            arrived(gc_copies, slot)
        if slot == 1:
            reduce_mlp.scatter_end(1)
            reduce_mlp.scatter_start(2)
        if slot == 3:
            reduce_mlp.scatter_end(2)
            reduce_mlp.widen()
            reduce_mlp.gather_start(2)
        if slot == 2:
            reduce_mlp.gather_end()
            reduce_mlp.gather_start(1)
        grad_low = gc[slot]
        dcT[:, rows] = dot_nt(full(2), grad_low).astype(BF)
        for h in range(HEADS):
            hr = slice(h * DH, (h + 1) * DH)
            d_out = dcT[hr, rows]
            probs = pcross[h, :, rows]
            d_probs = dot_nn(vx[h], d_out)
            d_scores = (probs * (d_probs - jnp.sum(probs * d_probs, axis=0, keepdims=True))).astype(BF)
            kT = ckvT[h * 2 * DH : h * 2 * DH + DH, :]
            dcqT[hr, rows] = (dot_nn(kT, d_scores) * scale).astype(BF)
            dckv[h * 2 * DH : h * 2 * DH + DH, :] += dot_nt(cqT[hr, rows], d_scores) * scale
            dckv[h * 2 * DH + DH : (h + 1) * 2 * DH, :] += dot_nt(d_out, probs.astype(BF))
        d_cross = dot_tn(dcqT[:, rows], full(1))
        grad = gc_own[...] if slot == 0 else grad_low.astype(F32)
        grad = grad + normalize_back(d_cross, cross_in[rows, :].astype(F32), inv_c[rows, :])
        if slot == 0:
            grad_own[...] = grad
            dm[2] = item_sums(0, grad * branch_own[...])
        low = (grad * per_frame(2, slot)).astype(BF)
        dba[rows, :] = low
        dOT[:, rows] = dot_nt(wfull[0, 0], low).astype(BF)

    gc_flat = gc[...].reshape(T, D)
    dckvT[...] = dckv[...].astype(BF)
    put("cross_out", dot_nn(catT[0:HW, :], gc_flat))
    put("cross_q", dot_nn(dcqT[0:HW, :], cross_in[...]))
    put("cross_kv", dot_nn(dckvT[0 : 2 * HW, :], text_flat))
    put("attn_out", dot_nn(att[0], dba[...]))
    reduce_cross.scatter_start(0)
    early[4:5, :] = dot_nn(onehot[...], gc_flat)[items : items + 1, :]
    early[5:6, :] = dot_nn(onehot[...], dba[...])[items : items + 1, :]
    eall[dp] = early[...]

    def dp_send(src, dst, index):
        def one(k, carry):
            peer = lax.rem(dp + k, dp_count)
            remote(
                src, dst, esem_s.at[index, k], esem_r.at[index, dp_count - k], {"dp": peer}
            ).start()
            return carry

        lax.fori_loop(1, dp_count, one, 0)

    def dp_wait(src, dst, index):
        def one(k, carry):
            remote(
                src, dst, esem_s.at[index, k], esem_r.at[index, k], {"dp": lax.rem(dp + k, dp_count)}
            ).wait()
            return carry

        lax.fori_loop(1, dp_count, one, 0)

    dp_send(eall.at[dp], eall.at[dp], 0)

    for h in range(HL):
        q0 = h * 3 * DH
        hr = slice(h * DH, (h + 1) * DH)
        d_keys = jnp.zeros((DH, T), F32)
        d_values = jnp.zeros((DH, T), F32)
        for b in range(TP):
            cols = slice(b * R, (b + 1) * R)
            d_out = dOT[hr, cols]
            probs = pself[h, :, cols]
            d_probs = dot_nn(kvx[2 * h + 1], d_out)
            d_scores = (probs * (d_probs - jnp.sum(probs * d_probs, axis=0, keepdims=True))).astype(BF)
            dqkvT[q0 : q0 + DH, cols] = (dot_nn(qkvT[q0 + DH : q0 + 2 * DH, :], d_scores) * scale).astype(BF)
            d_keys = d_keys + dot_nt(qkvT[q0 : q0 + DH, cols], d_scores)
            d_values = d_values + dot_nt(d_out, probs.astype(BF))
        dqkvT[q0 + DH : q0 + 2 * DH, :] = (d_keys * scale).astype(BF)
        dqkvT[q0 + 2 * DH : q0 + 3 * DH, :] = d_values.astype(BF)
        if h == 0:
            reduce_cross.scatter_end(0)
            reduce_cross.scatter_start(1)
            reduce_mlp.gather_end()
            reduce_mlp.gather_start(0)

    shift_sum = jnp.zeros((16, D), F32)
    scale_sum = jnp.zeros((16, D), F32)
    rs2_copies = {}
    for b in (2, 1, 3, 0):
        rows = slice(b * R, (b + 1) * R)
        part = dot_tn(dqkvT[:, rows], wqkvT[...])
        rs2_send[b] = part.astype(BF)
        if b:
            copy = remote(
                rs2_send.at[b], rs2_recv.at[TP - 1 - b], ssem.at[6 + HL, b], rsem.at[6 + HL, TP - b], tp_peer(b)
            )
            copy.start()
            rs2_copies[b] = copy
        shift_sum = shift_sum + item_sums(b, part)
        scale_sum = scale_sum + item_sums(b, part * na[rows, :].astype(F32))
    pending.extend(rs2_copies.values())
    dm[0] = shift_sum
    dm[1] = scale_sum

    put("qkv", dot_nn(dqkvT[...], attn_in[...]))
    reduce_self.scatter_start(0)

    for j in range(6):
        lo, hi = j * D, (j + 1) * D
        at = lo
        while at < hi:
            block = at // MB
            end = min(hi, (block + 1) * MB)
            dmp[block, :, at - block * MB : end - block * MB] = dm[j, 0:8, at - lo : end - lo]
            at = end
    dm_copies = direct(
        7 + HL, lambda k: dmp.at[lax.rem(tp + k, TP)], lambda k: dmr.at[TP - 1 - k]
    )
    reduce_cross.scatter_end(1)
    reduce_cross.scatter_start(2)
    reduce_self.scatter_end(0)
    reduce_self.scatter_start(1)
    d_mod = dmp[tp]
    for k in range(1, TP):
        arrived(dm_copies, k)
        d_mod = d_mod + dmr[k - 1]
    low = d_mod.astype(BF)
    lall[dp] = low.astype(F32)
    dp_send(lall.at[dp], lall.at[dp], 1)
    dsil[...] = dot_nt(low, wmod[...])
    ds_copies = direct(8 + HL, lambda k: dsil, lambda k: dsr.at[TP - 1 - k])

    dtext_o[...] = dot_tn(dckvT[:, 0:TL], wfull_kv(wfull, HW, D)).astype(BF)

    reduce_cross.scatter_end(2)
    reduce_cross.widen()
    reduce_cross.gather_start(2)
    reduce_self.scatter_end(1)
    reduce_self.scatter_start(2)
    reduce_mlp.gather_end()
    reduce_cross.gather_end()
    reduce_cross.gather_start(1)
    reduce_self.scatter_end(2)
    reduce_self.widen()
    reduce_self.gather_start(2)

    d_in = rs2_send[0].astype(F32)
    for k in (1, 3, 2):
        rs2_copies[TP - k].wait_recv()
        d_in = d_in + rs2_recv[k - 1].astype(F32)
    normed, inverse = normalize(tok[0].astype(F32))
    dtok_o[...] = (
        grad_own[...] + normalize_back(d_in * (1.0 + per_frame(1, 0)), normed, inverse)
    ).astype(BF)

    reduce_cross.gather_end()
    reduce_cross.gather_start(0)
    reduce_self.gather_end()
    reduce_self.gather_start(1)
    d_silu = dsil[...]
    for k in range(1, TP):
        arrived(ds_copies, k)
        d_silu = d_silu + dsr[k - 1]
    dtime_o[...] = d_silu[0:items, :] * (sig * (1.0 + time * (1.0 - sig)))
    reduce_cross.gather_end()
    dp_wait(eall.at[dp], eall.at[dp], 0)
    dp_wait(lall.at[dp], lall.at[dp], 1)
    out_copies = [
        pltpu.make_async_copy(eall, early_o, osem.at[3, 0]),
        pltpu.make_async_copy(lall, late_o, osem.at[3, 1]),
    ]
    for copy in out_copies:
        copy.start()
    reduce_self.gather_end()
    reduce_self.gather_start(0)
    reduce_self.gather_end()
    for copy in pending:
        copy.wait_send()
    for copy in out_copies:
        copy.wait()


def wfull_kv(wfull, HW, D):
    return wfull[:, 3:5].reshape(TP * 2 * HW, D)


def body(
    dp_count,
    tokens,
    seg_ids,
    time_embed,
    text_states,
    text_lengths,
    out_grad,
    w_qkv,
    w_attn_out,
    b_attn_out,
    w_cross_q,
    w_cross_kv,
    w_cross_out,
    b_cross_out,
    w_up,
    b_up,
    w_down,
    w_mod,
    b_mod,
):
    _, R, D = tokens.shape
    T = R * TP
    items = time_embed.shape[1]
    shard_txt = text_states.shape[2]
    TL = items * shard_txt
    TK = TP * TL
    HW = w_cross_q.shape[1]
    HL = HW // DH
    HEADS = TP * HL
    FF = w_up.shape[1]
    MB = w_mod.shape[1]
    place, total_rows = bucket_rows(FF, HW)
    small = jnp.concatenate([b_attn_out, b_cross_out, b_up, b_mod]).astype(F32)[None]
    text = text_states[0].reshape(TL, D)

    extra = 0
    step = 8
    while step < dp_count:
        extra += 1
        step *= 2
    room = total_rows - total_rows // 8 + 2 * extra * (total_rows // 16)

    hbm = pl.BlockSpec(memory_space=pl.ANY)
    vmem = pl.BlockSpec(memory_space=pltpu.VMEM)
    smem = pl.BlockSpec(memory_space=pltpu.SMEM)
    V = pltpu.VMEM
    DMA = pltpu.SemaphoreType.DMA
    scratch = [
        V((TP, R, D), BF), V((TP, R, D), BF), V((TP, TL, D), BF), V((TP, HW, T), BF), V((TP, R, D), BF),
        V((D, 3 * HW), BF), V((3 * HW, D), BF), V((D, HW), BF), V((D, 2 * HW), BF), V((TP, 5, HW, D), BF),
        V((D, FF), BF), V((FF, D), BF), V((D, MB), BF),
        V((TP, 8, MB), F32), V((6, 8, D), F32), V((1, T), F32), V((T, 1), F32), V((16, T), BF), V((TK, 1), F32),
        V((T, D), BF), V((T, D), BF), V((3 * HW, T), BF), V((2 * HL, T, DH), BF), V((HL, T, T), F32),
        V((T, D), F32), V((T, 1), F32), V((T, D), BF), V((TP * HW, T), BF), V((TP * 2 * HW, TK), BF),
        V((HEADS, TK, DH), BF), V((HEADS, TK, DH), BF), V((HEADS, TK, T), F32), V((TP * HW, T), BF), V((R, D), F32),
        V((T, D), BF), V((R, D), F32), V((R, 1), F32), V((R, 1), F32), V((T, FF), BF), V((T, FF), BF), V((T, D), BF),
        V((TP, R, D), BF), V((TP - 1, R, D), BF),
        V((R, D), F32), V((TP * HW, T), BF), V((TP * HW, T), BF), V((TP * 2 * HW, TK), F32),
        V((TP * 2 * HW, TK), BF), V((R, D), F32), V((T, D), BF), V((HW, T), BF), V((3 * HW, T), BF),
        V((TP, R, D), BF), V((TP - 1, R, D), BF),
        V((6, 16, D), F32), V((TP, 8, MB), F32), V((TP - 1, 8, MB), F32), V((8, D), F32), V((TP - 1, 8, D), F32),
        V((8, D), F32), V((8, MB), F32), V((dp_count, 8, D), F32), V((dp_count, 8, MB), F32),
        V((total_rows, D), BF), V((room, D), BF),
        DMA((11,)), DMA((9 + HL, TP)), DMA((9 + HL, TP)), DMA((8,)), DMA((8,)),
        DMA((3, 2, 6 + extra)), DMA((3, 2, 6 + extra)), DMA((2, dp_count)), DMA((2, dp_count)), DMA((4, 2)),
    ]
    d_tokens, d_time, d_text, grads, early, late = pl.pallas_call(
        functools.partial(layer_kernel, (dp_count, place, items, shard_txt)),
        out_shape=(
            jax.ShapeDtypeStruct((R, D), BF),
            jax.ShapeDtypeStruct((items, D), F32),
            jax.ShapeDtypeStruct((TL, D), BF),
            jax.ShapeDtypeStruct((total_rows, D), BF),
            jax.ShapeDtypeStruct((dp_count, 8, D), F32),
            jax.ShapeDtypeStruct((dp_count, 8, MB), F32),
        ),
        in_specs=[hbm] * 11 + [vmem] * 3 + [smem],
        out_specs=(vmem, vmem, vmem, hbm, hbm, hbm),
        scratch_shapes=scratch,
        name="layer",
        compiler_params=pltpu.CompilerParams(
            collective_id=0, has_side_effects=True, vmem_limit_bytes=63 * 1024 * 1024
        ),
    )(
        tokens[0], out_grad[0], text, w_qkv, w_attn_out, w_cross_q, w_cross_kv, w_cross_out,
        w_up, w_down, w_mod, seg_ids, time_embed[0], small, text_lengths,
    )

    def grad(name, transpose=False):
        at, rows = place[name]
        piece = grads[at : at + rows].astype(F32)
        return piece.T if transpose else piece

    silu_all = early[:, 0:items].astype(BF).reshape(dp_count * items, D)
    mod_all = late[:, 0:items].reshape(dp_count * items, MB)
    g_mod = dot_tn(silu_all, mod_all.astype(BF))
    gb_mod = jnp.sum(mod_all, axis=0)
    biases = jnp.sum(early[:, 3:6], axis=0)
    return (
        d_tokens[None],
        d_time[None],
        d_text.reshape(1, items, shard_txt, D),
        grad("qkv", True),
        grad("attn_out"),
        biases[2],
        grad("cross_q", True),
        grad("cross_kv", True),
        grad("cross_out"),
        biases[1],
        grad("up"),
        biases[0],
        grad("down"),
        g_mod,
        gb_mod,
    )


def solution(mesh):
    placed = (
        P("dp", "tp", None),
        P("dp", None),
        P("dp", None, None),
        P("dp", None, "tp", None),
        P("dp", None),
        P("dp", "tp", None),
        P(None, "tp"),
        P("tp", None),
        P(),
        P(None, "tp"),
        P(None, "tp"),
        P("tp", None),
        P(),
        P(None, "tp"),
        P("tp"),
        P("tp", None),
        P(None, "tp"),
        P("tp"),
    )
    return jax.shard_map(
        functools.partial(body, mesh.shape["dp"]),
        mesh=mesh,
        in_specs=placed,
        out_specs=(
            P("dp", "tp", None),
            P("dp", None, None),
            P("dp", None, "tp", None),
            P(None, "tp"),
            P("tp", None),
            P(),
            P(None, "tp"),
            P(None, "tp"),
            P("tp", None),
            P(),
            P(None, "tp"),
            P("tp"),
            P("tp", None),
            P(None, "tp"),
            P("tp"),
        ),
        check_vma=False,
    )
```

```python
import functools
import math

import jax
import jax.numpy as jnp
from jax import lax
from jax.experimental import pallas as pl
from jax.experimental.pallas import tpu as pltpu
from jax.sharding import PartitionSpec as P

DH = 64
TP = 4
MESH = pl.DeviceIdType.MESH
BF = jnp.bfloat16
F32 = jnp.float32
GELU_C = math.sqrt(2.0 / math.pi)


def dot_nn(left, right):
    return jnp.dot(left, right, preferred_element_type=F32)


def dot_tn(left, right):
    return lax.dot_general(left, right, (((0,), (0,)), ((), ())), preferred_element_type=F32)


def dot_nt(left, right):
    return lax.dot_general(left, right, (((1,), (1,)), ((), ())), preferred_element_type=F32)


def normalize(values):
    center = values - jnp.mean(values, axis=-1, keepdims=True)
    inverse = lax.rsqrt(jnp.mean(center * center, axis=-1, keepdims=True) + 1e-06)
    return center * inverse, inverse


def normalize_back(grad, normed, inverse):
    return inverse * (
        grad
        - jnp.mean(grad, axis=-1, keepdims=True)
        - normed * jnp.mean(grad * normed, axis=-1, keepdims=True)
    )


def bucket_rows(hidden, heads_width):
    sizes = [
        ("up", hidden),
        ("down", hidden),
        ("cross_out", heads_width),
        ("cross_q", heads_width),
        ("cross_kv", 2 * heads_width),
        ("attn_out", heads_width),
        ("qkv", 3 * heads_width),
    ]
    at, place = 0, {}
    for name, rows in sizes:
        place[name] = (at, rows)
        at += rows
    return place, at


def layer_kernel(
    dims,
    tok_h, og_h, text_h, wqkvT_h, wo_h, wcqT_h, wckv_h, wco_h, wup_h, wdn_h, wmod_h,
    seg_ref, time_ref, b_attn_out_ref, b_cross_out_ref, b_up_ref, b_mod_ref, tlen_ref,
    dtok_o, dtime_o, dtext_o, grads_o, early_o, late_o,
    tok, og, text, att, gc,
    wqkvT, wckv, wfull, wup, wdn, wmod,
    modbuf, mods, segrow, segcol, onehot, ktag,
    attn_in, na, qkvT, kvx, pself,
    stream_a, inv_c, cross_in, cqT, ckvT, kx, vx, pcross, catT, branch_own,
    mlp_in, nm_own, invm_own, act, dpre, dbm, rs_send, rs_recv,
    gc_own, dcT, dcqT, dckv, dckvT, grad_own, dba, dOT, dqkvT, dkv_acc,
    rs2_send, rs2_recv, dm, dmp, dmr, dsil, dsr, early, eall, lall,
    grads, rbuf,
    lsem, ssem, rsem, csem_s, csem_r, wsem_s, wsem_r, gsem_s, gsem_r, esem_s, esem_r, osem,
):
    dp_count, place, items = dims
    tp = lax.axis_index("tp")
    dp = lax.axis_index("dp")
    R = tok.shape[1]
    D = tok.shape[2]
    T = TP * R
    HW = att.shape[1]
    HL = HW // DH
    TK = TP * text.shape[1]
    TL = text.shape[1]
    HEADS = TP * HL
    MB = modbuf.shape[2]
    QB = 2 * R
    scale = 1.0 / math.sqrt(DH)
    sub = lax.rem(dp, 8)
    base8 = dp - sub
    core = lax.rem(sub, 2)
    chip = sub // 2

    def tp_peer(k):
        return {"tp": lax.rem(tp + k, TP)}

    def remote(src, dst, send, recv, peer):
        return pltpu.make_async_remote_copy(
            src_ref=src, dst_ref=dst, send_sem=send, recv_sem=recv, device_id=peer, device_id_type=MESH
        )

    def span(at, size, unit):
        return pl.ds(pl.multiple_of(at, unit), size)

    loads = [
        (tok_h, tok.at[0]),
        (wmod_h, wmod),
        (text_h, text.at[0]),
        (wqkvT_h, wqkvT),
        (wcqT_h, wfull.at[0, 1]),
        (wo_h, wfull.at[0, 0]),
        (wco_h, wfull.at[0, 2]),
        (wckv_h, wckv),
        (og_h, og.at[0]),
        (wup_h, wup),
        (wdn_h, wdn),
    ]
    local = [pltpu.make_async_copy(src, dst, lsem.at[i]) for i, (src, dst) in enumerate(loads)]
    for copy in local:
        copy.start()

    barrier = pltpu.get_barrier_semaphore()
    for k in range(1, TP):
        pl.semaphore_signal(barrier, inc=1, device_id=tp_peer(k), device_id_type=MESH)

    def greet(k, carry):
        pl.semaphore_signal(
            barrier, inc=1, device_id={"dp": lax.rem(dp + k, dp_count)}, device_id_type=MESH
        )
        return carry

    lax.fori_loop(1, dp_count, greet, 0)

    early[...] = jnp.zeros(early.shape, F32)
    for item in range(items):
        early[item : item + 1, :] = time_ref[item]
    time = early[...]
    sig = 1.0 / (1.0 + jnp.exp(-time))
    silu_low = (time * sig).astype(BF)
    early[...] = silu_low.astype(F32)
    local[1].wait()
    modbuf[tp] = dot_nn(silu_low, wmod[...]) + b_mod_ref[...].astype(F32).reshape(1, MB)
    local[0].wait()

    pl.semaphore_wait(barrier, TP - 1 + dp_count - 1)

    pending, chains = [], []
    inner = (tp > 0) & (tp < TP - 1)
    slot_a = jnp.where(tp == 3, 3, 1)
    slot_b = jnp.where((tp == 0) | (tp == 3), 2, 3)
    slot_c = jnp.where(tp == 0, 3, jnp.where(tp == 3, 1, 2))
    right, left = {"tp": lax.rem(tp + 1, TP)}, {"tp": lax.rem(tp + TP - 1, TP)}
    onward = {"tp": jnp.where(tp == 1, 0, TP - 1)}
    onward_slot = jnp.where(tp == 1, 3, 1)

    class Chain:
        def __init__(self, index, view):
            self.index, self.view, self.started = index, view, []
            chains.append(self)

        def copy(self, src, dst, send, chunk, peer):
            return remote(
                self.view(src, chunk), self.view(dst, chunk),
                csem_s.at[self.index, send, chunk], csem_r.at[self.index, dst, chunk], peer,
            )

        def start(self, chunk):
            self.started.append(chunk)

            @pl.when(tp < TP - 1)
            def _():
                self.copy(0, 3, 0, chunk, right).start()

            @pl.when(tp > 0)
            def _():
                self.copy(0, 1, 1, chunk, left).start()

        def step(self, which, chunk):
            slot = (slot_a, slot_b, slot_c)[which]
            self.copy(slot, slot, 2 + which, chunk, right).wait_recv()

            @pl.when(inner)
            def _():
                if which == 0:
                    self.copy(slot, 2, 2, chunk, left).start()
                elif which == 1:
                    self.copy(slot, 2, 3, chunk, right).start()
                else:
                    self.copy(slot, onward_slot, 4, chunk, onward).start()

        def finish(self):
            for chunk in self.started:

                @pl.when(tp < TP - 1)
                def _():
                    self.copy(0, 3, 0, chunk, right).wait_send()

                @pl.when(tp > 0)
                def _():
                    self.copy(0, 1, 1, chunk, left).wait_send()

                @pl.when(inner)
                def _():
                    self.copy(slot_a, 2, 2, chunk, left).wait_send()
                    self.copy(slot_b, 2, 3, chunk, right).wait_send()
                    self.copy(slot_c, onward_slot, 4, chunk, onward).wait_send()

    half = R // 2
    tok_chain = Chain(0, lambda slot, c: tok.at[slot, c * half : (c + 1) * half])
    text_chain = Chain(1, lambda slot, c: text.at[slot])
    WR, WC = HW // 4, D // 2
    wrow = pl.multiple_of(chip * WR, 16)
    wcol = pl.multiple_of(core * WC, 128)
    pieces = (slice(0, 3), slice(3, 5))
    w_chain = Chain(2, lambda slot, c: wfull.at[slot, pieces[c], pl.ds(wrow, WR), pl.ds(wcol, WC)])
    att_chain = Chain(3, lambda slot, c: att.at[slot, c * DH : (c + 1) * DH])
    og_chain = Chain(4, lambda slot, c: og.at[slot, c * half : (c + 1) * half])
    gc_chain = Chain(5, lambda slot, c: gc.at[slot, c * half : (c + 1) * half])

    def direct(tag, src_of, dst_of):
        copies = []
        for k in range(1, TP):
            copy = remote(src_of(k), dst_of(k), ssem.at[tag, k], rsem.at[tag, TP - k], tp_peer(k))
            copy.start()
            copies.append(copy)
        pending.extend(copies)
        return copies

    def arrived(copies, slot):
        copies[TP - 1 - slot].wait_recv()

    tok_chain.start(0)
    tok_chain.start(1)
    mod_copies = direct(0, lambda k: modbuf.at[tp], lambda k: modbuf.at[tp])

    eye = lax.broadcasted_iota(jnp.int32, (R, R), 0) == lax.broadcasted_iota(jnp.int32, (R, R), 1)
    for slot in range(TP):
        owner = lax.rem(tp + slot, TP)
        row = seg_ref[:, pl.ds(pl.multiple_of(owner * R, R), R)].astype(F32)
        segrow[:, slot * R : (slot + 1) * R] = row
        col = jnp.sum(jnp.where(eye, row, 0.0), axis=1, keepdims=True)
        segcol[slot * R : (slot + 1) * R, :] = col
    kinds = lax.broadcasted_iota(jnp.int32, (16, T), 0)
    matches = (segrow[...] == kinds.astype(F32)) & (kinds < items)
    onehot[...] = jnp.where(matches | (kinds == items), 1.0, 0.0).astype(BF)
    key_at = lax.broadcasted_iota(jnp.int32, (TK, 1), 0)
    key_slot = key_at // TL
    key_item = lax.rem(key_at, TL) // (TL // items)
    key_pos = lax.rem(key_slot + tp, TP) * (TL // items) + lax.rem(key_at, TL // items)
    tag = jnp.full((TK, 1), -1.0, F32)
    for item in range(items):
        inside = (key_item == item) & (key_pos < tlen_ref[0, item])
        tag = jnp.where(inside, float(item), tag)
    ktag[...] = tag

    for k in range(1, TP):
        arrived(mod_copies, k)
    for j in range(6):
        lo, hi = j * D, (j + 1) * D
        at = lo
        while at < hi:
            block = at // MB
            end = min(hi, (block + 1) * MB)
            mods[j, :, at - lo : end - lo] = modbuf[block, :, at - block * MB : end - block * MB]
            at = end

    def per_frame(j, rows):
        col = segcol[rows, :]
        out = mods[j, items - 1 : items, :]
        for item in range(items - 2, -1, -1):
            out = jnp.where(col == float(item), mods[j, item : item + 1, :], out)
        return out

    def item_sums(rows, values):
        return dot_nn(onehot[:, rows], values.astype(BF))

    own = slice(0, R)
    local[3].wait()

    def project(slot):
        rows = span(slot * R, R, R)
        normed, inverse = normalize(tok[slot].astype(F32))
        na[rows, :] = normed.astype(BF)
        x = (normed * (1.0 + per_frame(1, rows)) + per_frame(0, rows)).astype(BF)
        attn_in[rows, :] = x
        qkvT[:, rows] = dot_nt(wqkvT[...], x).astype(BF)

    project(0)
    for which, slot in enumerate((slot_a, slot_b, slot_c)):
        tok_chain.step(which, 0)
        tok_chain.step(which, 1)
        if which == 0:
            local[2].wait()
            local[7].wait()
            ident = (
                lax.broadcasted_iota(jnp.int32, (D, D), 0) == lax.broadcasted_iota(jnp.int32, (D, D), 1)
            ).astype(F32).astype(BF)
            wckvT = dot_tn(wckv[...], ident).astype(BF)
            wfull[0, 3] = wckvT[:HW]
            wfull[0, 4] = wckvT[HW:]
            for copy in local[4:7]:
                copy.wait()
        if which == 2:
            text_chain.start(0)
            w_chain.start(0)
            w_chain.start(1)
        project(slot)

    for h in range(HL):
        q0 = h * 3 * DH
        keys = (qkvT[q0 + DH : q0 + 2 * DH, :].astype(F32).T * scale).astype(BF)
        kvx[2 * h] = keys
        kvx[2 * h + 1] = qkvT[q0 + 2 * DH : q0 + 3 * DH, :].astype(F32).T.astype(BF)

        def attend(b, carry, h=h, q0=q0):
            cols = span(b * R, R, R)
            scores = dot_nn(kvx[2 * h], qkvT[q0 : q0 + DH, cols])
            scores = jnp.where(segcol[...] == segrow[:, cols], scores, -1000000000.0)
            peak = jnp.max(scores, axis=0, keepdims=True)
            exponent = jnp.exp(scores - peak)
            probs = exponent * (1.0 / jnp.sum(exponent, axis=0, keepdims=True))
            pself[h, :, cols] = probs
            att[0, h * DH : (h + 1) * DH, cols] = dot_nn(
                qkvT[q0 + 2 * DH : q0 + 3 * DH, :], probs.astype(BF)
            ).astype(BF)
            return carry

        lax.fori_loop(0, TP, attend, 0)
        att_chain.start(h)
        if h == 0:
            text_chain.step(0, 0)
        if h == 1:
            w_chain.step(0, 0)
            text_chain.step(1, 0)
        if h == 2:
            w_chain.step(0, 1)
    w_chain.step(1, 0)
    w_chain.step(1, 1)
    text_chain.step(2, 0)
    for h in range(HL):
        att_chain.step(0, h)
    w_chain.step(2, 0)
    w_chain.step(2, 1)
    local[8].wait()

    wx = []
    for m in range(1, 4):
        peer = {"dp": base8 + jnp.bitwise_xor(sub, 2 * m)}
        copy = remote(
            wfull.at[1:TP, :, pl.ds(wrow, WR), pl.ds(wcol, WC)],
            wfull.at[1:TP, :, pl.ds(wrow, WR), pl.ds(wcol, WC)],
            wsem_s.at[m], wsem_r.at[m], peer,
        )
        copy.start()
        wx.append(copy)
    for h in range(HL):
        att_chain.step(1, h)
    og_chain.start(0)
    og_chain.start(1)
    for copy in wx:
        copy.wait_recv()
    wlast = remote(
        wfull.at[1:TP, :, :, pl.ds(wcol, WC)],
        wfull.at[1:TP, :, :, pl.ds(wcol, WC)],
        wsem_s.at[0], wsem_r.at[0], {"dp": base8 + jnp.bitwise_xor(sub, 1)},
    )
    wlast.start()
    pending.extend(wx + [wlast])
    wlast.wait_recv()

    def full(i):
        return wfull[:, i].reshape(TP * HW, D)

    text_flat = text[...].reshape(TK, D)
    for s in range(TP):
        for part in range(2):
            ckvT[(2 * s + part) * HW : (2 * s + part + 1) * HW, :] = dot_nt(wfull[s, 3 + part], text_flat).astype(BF)
    for h in range(HEADS):
        pair = ckvT[h * 2 * DH : (h + 1) * 2 * DH, :].astype(F32).T
        kx[h] = (pair[:, :DH] * scale).astype(BF)
        vx[h] = pair[:, DH:].astype(BF)
    for h in range(HL):
        att_chain.step(2, h)

    b_attn_out = b_attn_out_ref[...].astype(F32).reshape(1, D)
    b_cross_out = b_cross_out_ref[...].astype(F32).reshape(1, D)
    b_up = b_up_ref[...].astype(F32).reshape(1, wup.shape[1])

    def forward(i, carry):
        rows = span(i * QB, QB, QB)
        parts = []
        for b in range(QB // R):
            at = i * (QB // R) + b
            parts.append(
                jnp.concatenate(
                    [att[k, :, span(lax.rem(at + TP - k, TP) * R, R, R)] for k in range(TP)], axis=0
                )
            )
        branch = dot_tn(jnp.concatenate(parts, axis=1), full(0)) + b_attn_out

        @pl.when(i == 0)
        def _():
            branch_own[...] = branch[:R]

        frames = tok[span(i * (QB // R), QB // R, 1)].reshape(QB, D)
        stream_a[rows, :] = frames.astype(F32) + per_frame(2, rows) * branch
        normed, inverse = normalize(stream_a[rows, :])
        inv_c[rows, :] = inverse
        x = normed.astype(BF)
        cross_in[rows, :] = x
        cqT[:, rows] = dot_nt(full(1), x).astype(BF)
        allowed = ktag[...] == segrow[:, rows]
        for h in range(HEADS):
            hr = slice(h * DH, (h + 1) * DH)
            scores = dot_nn(kx[h], cqT[hr, rows])
            scores = jnp.where(allowed, scores, -1000000000.0)
            peak = jnp.max(scores, axis=0, keepdims=True)
            exponent = jnp.exp(scores - peak)
            probs = exponent * (1.0 / jnp.sum(exponent, axis=0, keepdims=True))
            pcross[h, :, rows] = probs
            vT = ckvT[h * 2 * DH + DH : (h + 1) * 2 * DH, :]
            catT[hr, rows] = dot_nn(vT, probs.astype(BF)).astype(BF)
        stream = stream_a[rows, :] + dot_tn(catT[:, rows], full(2)) + b_cross_out
        normed, inverse = normalize(stream)

        @pl.when(i == 0)
        def _():
            nm_own[...] = normed[:R]
            invm_own[...] = inverse[:R]

        mlp_in[rows, :] = (normed * (1.0 + per_frame(4, rows)) + per_frame(3, rows)).astype(BF)
        for which in range(2):

            @pl.when(i == which)
            def _():
                og_chain.step(which, 0)
                og_chain.step(which, 1)

        return carry

    lax.fori_loop(0, T // QB, forward, 0)
    og_chain.step(2, 0)
    og_chain.step(2, 1)

    local[9].wait()
    local[10].wait()
    dm[5] = jnp.zeros((16, D), F32)

    def rs_copy(b):
        return remote(
            rs_send.at[b], rs_recv.at[TP - 1 - b], ssem.at[1, b], rsem.at[1, TP - b], tp_peer(b)
        )

    def feed(i, carry):
        b = jnp.where(i == 0, 2, jnp.where(i == 3, 0, 2 * i - 1))
        rows = span(b * R, R, R)
        pre = dot_nn(mlp_in[rows, :], wup[...]) + b_up
        square = pre * pre
        bend = jnp.tanh(GELU_C * pre * (1.0 + 0.044715 * square))
        low = (0.5 * pre * (1.0 + bend)).astype(BF)
        act[rows, :] = low
        slope = 0.5 * (1.0 + bend) + 0.5 * pre * (1.0 - bend * bend) * (
            GELU_C * (1.0 + 3.0 * 0.044715 * square)
        )
        grad = og[b].astype(F32)
        d_branch = (grad * per_frame(5, rows)).astype(BF)
        dbm[rows, :] = d_branch
        d_pre = (dot_nt(d_branch, wdn[...]) * slope).astype(BF)
        dpre[rows, :] = d_pre
        rs_send[b] = dot_nt(d_pre, wup[...]).astype(BF)

        @pl.when(i < 3)
        def _():
            rs_copy(b).start()

        dm[5] += item_sums(rows, grad * dot_nn(low, wdn[...]))
        return carry

    lax.fori_loop(0, TP, feed, 0)
    rs_copies = {b: rs_copy(b) for b in range(1, TP)}
    pending.extend(rs_copies.values())
    early[3:4, :] = dot_nn(onehot[...], dpre[...])[items : items + 1, :]

    bits = []
    step = 8
    while step < dp_count:
        bits.append(step)
        step *= 2

    class Reduce:
        def __init__(self, index, start, rows, room):
            self.parts = []
            half = rows // 2
            for part in range(2):
                chain = (1, 2, 4) if part == 0 else (1, 4, 2)
                self.parts.append((start + part * half, half, chain, part * half))
            self.index, self.room = index, room
            self.open, self.own = [], []

        def sem(self, part, step):
            return gsem_s.at[self.index, part, step], gsem_r.at[self.index, part, step]

        def launch(self, src, dst, part, step, bit):
            send, recv = self.sem(part, step)
            copy = remote(src, dst, send, recv, {"dp": jnp.bitwise_xor(dp, bit)})
            copy.start()
            pending.append(copy)
            return copy

        def bounds(self, part, level):
            start, rows, chain, _ = self.parts[part]
            at, size = start, rows
            for bit in chain[:level]:
                size //= 2
                at = at + jnp.bitwise_and(dp // bit, 1) * size
            return at, size

        def scatter_start(self, level):
            self.open = []
            for part in range(2):
                at, size = self.bounds(part, level)
                bit = self.parts[part][2][level]
                half = size // 2
                mine = jnp.bitwise_and(dp // bit, 1)
                other = pl.multiple_of(at + (1 - mine) * half, 16)
                rows = self.parts[part][1]
                room = self.room + 2 * (rows - (rows >> level)) + part * half
                copy = self.launch(
                    grads.at[pl.ds(other, half)], rbuf.at[room : room + half], part, level, bit
                )
                self.open.append((copy, room, half))

        def scatter_end(self, level):
            for part in range(2):
                copy, room, half = self.open[part]
                copy.wait_recv()
                at, size = self.bounds(part, level + 1)
                mine = pl.ds(pl.multiple_of(at, 16), half)
                grads[mine, :] = (grads[mine, :].astype(F32) + rbuf[room : room + half, :].astype(F32)).astype(BF)

        def widen(self):
            for i, bit in enumerate(bits):
                for part in range(2):
                    at, size = self.bounds(part, 3)
                    rows = self.parts[part][1]
                    mine = pl.ds(pl.multiple_of(at, 16), size)
                    room = self.room + 2 * (rows - rows // 8) + (2 * i + part) * size
                    copy = self.launch(grads.at[mine], rbuf.at[room : room + size], part, 6 + i, bit)
                    copy.wait_recv()
                    grads[mine, :] = (
                        grads[mine, :].astype(F32) + rbuf[room : room + size, :].astype(F32)
                    ).astype(BF)

        def gather_start(self, level):
            self.open = []
            source = grads if level == 2 else grads_o
            if level == 1:
                for copy in self.own:
                    copy.wait()
            for part in range(2):
                at, size = self.bounds(part, level + 1)
                bit = self.parts[part][2][level]
                mine = pl.ds(pl.multiple_of(at, 16), size)
                self.open.append(
                    self.launch(source.at[mine], grads_o.at[mine], part, 3 + (2 - level), bit)
                )
                if level == 2:
                    copy = pltpu.make_async_copy(grads.at[mine], grads_o.at[mine], osem.at[self.index, part])
                    copy.start()
                    self.own.append(copy)

        def gather_end(self):
            for copy in self.open:
                copy.wait_recv()

    mid0 = place["cross_out"][0]
    mid1 = place["attn_out"][0]
    total_rows = grads.shape[0]
    extra = 2 * len(bits)
    rooms, at = [], 0
    for rows in (mid0, mid1 - mid0, total_rows - mid1):
        rooms.append(at)
        at += rows - rows // 8 + extra * (rows // 16)
    reduce_mlp = Reduce(0, 0, mid0, rooms[0])
    reduce_cross = Reduce(1, mid0, mid1 - mid0, rooms[1])
    reduce_self = Reduce(2, mid1, total_rows - mid1, rooms[2])

    def put(name, values):
        at, rows = place[name]
        grads[at : at + rows, :] = values.astype(BF)

    put("up", dot_tn(mlp_in[...], dpre[...]))
    put("down", dot_tn(act[...], dbm[...]))
    reduce_mlp.scatter_start(0)

    d_mlp = rs_send[0].astype(F32)
    reduce_mlp.scatter_end(0)
    reduce_mlp.scatter_start(1)
    for k in (1, 3, 2):
        rs_copies[TP - k].wait_recv()
        d_mlp = d_mlp + rs_recv[k - 1].astype(F32)
    normed = nm_own[...]
    grad_c = og[0].astype(F32) + normalize_back(d_mlp * (1.0 + per_frame(4, own)), normed, invm_own[...])
    gc_own[...] = grad_c
    gc[0] = grad_c.astype(BF)
    gc_chain.start(0)
    gc_chain.start(1)
    dm[3] = item_sums(own, d_mlp)
    dm[4] = item_sums(own, d_mlp * normed)

    dckv[...] = jnp.zeros(dckv.shape, F32)
    GROUP = 4

    def backward(slot, first):
        rows = span(slot * R, R, R)
        grad_low = gc[slot]
        dcT[:, rows] = dot_nt(full(2), grad_low).astype(BF)

        def heads(g, carry):
            for j in range(GROUP):
                h = g * GROUP + j
                hr = span(h * DH, DH, DH)
                kr, vr = span(h * 2 * DH, DH, DH), span(h * 2 * DH + DH, DH, DH)
                d_out = dcT[hr, rows]
                probs = pcross[h, :, rows]
                d_probs = dot_nn(vx[h], d_out)
                d_scores = (probs * (d_probs - jnp.sum(probs * d_probs, axis=0, keepdims=True))).astype(BF)
                dcqT[hr, rows] = (dot_nn(ckvT[kr, :], d_scores) * scale).astype(BF)
                dckv[kr, :] += dot_nt(cqT[hr, rows], d_scores) * scale
                dckv[vr, :] += dot_nt(d_out, probs.astype(BF))
            return carry

        lax.fori_loop(0, HEADS // GROUP, heads, 0)
        d_cross = dot_tn(dcqT[:, rows], full(1))
        grad = gc_own[...] if first else grad_low.astype(F32)
        grad = grad + normalize_back(d_cross, cross_in[rows, :].astype(F32), inv_c[rows, :])
        if first:
            grad_own[...] = grad
            dm[2] = item_sums(own, grad * branch_own[...])
        low = (grad * per_frame(2, rows)).astype(BF)
        dba[rows, :] = low
        dOT[:, rows] = dot_nt(wfull[0, 0], low).astype(BF)

    backward(0, True)
    gc_chain.step(0, 0)
    gc_chain.step(0, 1)
    gc_chain.step(1, 0)
    gc_chain.step(1, 1)
    reduce_mlp.scatter_end(1)
    reduce_mlp.scatter_start(2)
    backward(slot_a, False)
    gc_chain.step(2, 0)
    gc_chain.step(2, 1)
    reduce_mlp.scatter_end(2)
    reduce_mlp.widen()
    reduce_mlp.gather_start(2)
    backward(slot_b, False)
    reduce_mlp.gather_end()
    reduce_mlp.gather_start(1)
    backward(slot_c, False)

    gc_flat = gc[...].reshape(T, D)
    dckvT[...] = dckv[...].astype(BF)
    put("cross_out", dot_nn(catT[0:HW, :], gc_flat))
    put("cross_q", dot_nn(dcqT[0:HW, :], cross_in[...]))
    put("cross_kv", dot_nn(dckvT[0 : 2 * HW, :], text_flat))
    put("attn_out", dot_nn(att[0], dba[...]))
    reduce_cross.scatter_start(0)
    early[4:5, :] = dot_nn(onehot[...], gc_flat)[items : items + 1, :]
    early[5:6, :] = dot_nn(onehot[...], dba[...])[items : items + 1, :]
    eall[dp] = early[...]

    def dp_send(src, dst, index):
        def one(k, carry):
            peer = lax.rem(dp + k, dp_count)
            remote(
                src, dst, esem_s.at[index, k], esem_r.at[index, dp_count - k], {"dp": peer}
            ).start()
            return carry

        lax.fori_loop(1, dp_count, one, 0)

    def dp_wait(src, dst, index):
        def one(k, carry):
            remote(
                src, dst, esem_s.at[index, k], esem_r.at[index, k], {"dp": lax.rem(dp + k, dp_count)}
            ).wait()
            return carry

        lax.fori_loop(1, dp_count, one, 0)

    dp_send(eall.at[dp], eall.at[dp], 0)

    for h in range(HL):
        q0 = h * 3 * DH
        hr = slice(h * DH, (h + 1) * DH)
        dkv_acc[...] = jnp.zeros(dkv_acc.shape, F32)

        def attend_back(b, carry, h=h, q0=q0, hr=hr):
            cols = span(b * R, R, R)
            d_out = dOT[hr, cols]
            probs = pself[h, :, cols]
            d_probs = dot_nn(kvx[2 * h + 1], d_out)
            d_scores = (probs * (d_probs - jnp.sum(probs * d_probs, axis=0, keepdims=True))).astype(BF)
            dqkvT[q0 : q0 + DH, cols] = (dot_nn(qkvT[q0 + DH : q0 + 2 * DH, :], d_scores) * scale).astype(BF)
            dkv_acc[0:DH, :] += dot_nt(qkvT[q0 : q0 + DH, cols], d_scores) * scale
            dkv_acc[DH : 2 * DH, :] += dot_nt(d_out, probs.astype(BF))
            return carry

        lax.fori_loop(0, TP, attend_back, 0)
        dqkvT[q0 + DH : q0 + 3 * DH, :] = dkv_acc[...].astype(BF)
        if h == 0:
            reduce_cross.scatter_end(0)
            reduce_cross.scatter_start(1)
            reduce_mlp.gather_end()
            reduce_mlp.gather_start(0)

    dm[0] = jnp.zeros((16, D), F32)
    dm[1] = jnp.zeros((16, D), F32)

    def rs2_copy(b):
        return remote(
            rs2_send.at[b], rs2_recv.at[TP - 1 - b], ssem.at[2, b], rsem.at[2, TP - b], tp_peer(b)
        )

    def entry(i, carry):
        b = jnp.where(i == 0, 2, jnp.where(i == 3, 0, 2 * i - 1))
        rows = span(b * R, R, R)
        part = dot_tn(dqkvT[:, rows], wqkvT[...])
        rs2_send[b] = part.astype(BF)

        @pl.when(i < 3)
        def _():
            rs2_copy(b).start()

        dm[0] += item_sums(rows, part)
        dm[1] += item_sums(rows, part * na[rows, :].astype(F32))
        return carry

    lax.fori_loop(0, TP, entry, 0)
    rs2_copies = {b: rs2_copy(b) for b in range(1, TP)}
    pending.extend(rs2_copies.values())

    put("qkv", dot_nn(dqkvT[...], attn_in[...]))
    reduce_self.scatter_start(0)

    for j in range(6):
        lo, hi = j * D, (j + 1) * D
        at = lo
        while at < hi:
            block = at // MB
            end = min(hi, (block + 1) * MB)
            dmp[block, :, at - block * MB : end - block * MB] = dm[j, 0:8, at - lo : end - lo]
            at = end
    dm_copies = direct(
        3, lambda k: dmp.at[lax.rem(tp + k, TP)], lambda k: dmr.at[TP - 1 - k]
    )
    reduce_self.scatter_end(0)
    reduce_self.scatter_start(1)
    reduce_cross.scatter_end(1)
    reduce_cross.scatter_start(2)

    dtext_o[...] = dot_tn(dckvT[:, 0:TL], wfull[:, 3:5].reshape(TP * 2 * HW, D)).astype(BF)

    d_mod = dmp[tp]
    for k in range(1, TP):
        arrived(dm_copies, k)
        d_mod = d_mod + dmr[k - 1]
    low = d_mod.astype(BF)
    lall[dp] = low.astype(F32)
    dp_send(lall.at[dp], lall.at[dp], 1)
    dsil[...] = dot_nt(low, wmod[...])
    ds_copies = direct(4, lambda k: dsil, lambda k: dsr.at[TP - 1 - k])

    reduce_self.scatter_end(1)
    reduce_self.scatter_start(2)
    reduce_cross.scatter_end(2)
    reduce_cross.widen()
    reduce_cross.gather_start(2)
    reduce_mlp.gather_end()
    reduce_self.scatter_end(2)
    reduce_self.widen()
    reduce_self.gather_start(2)
    reduce_cross.gather_end()
    reduce_cross.gather_start(1)
    reduce_self.gather_end()
    reduce_self.gather_start(1)

    d_in = rs2_send[0].astype(F32)
    for k in (1, 3, 2):
        rs2_copies[TP - k].wait_recv()
        d_in = d_in + rs2_recv[k - 1].astype(F32)
    normed, inverse = normalize(tok[0].astype(F32))
    dtok_o[...] = (
        grad_own[...] + normalize_back(d_in * (1.0 + per_frame(1, own)), normed, inverse)
    ).astype(BF)
    reduce_cross.gather_end()
    reduce_cross.gather_start(0)

    d_silu = dsil[...]
    for k in range(1, TP):
        arrived(ds_copies, k)
        d_silu = d_silu + dsr[k - 1]
    for item in range(items):
        value = time_ref[item]
        gate = 1.0 / (1.0 + jnp.exp(-value))
        dtime_o[item] = d_silu[item : item + 1, :] * (gate * (1.0 + value * (1.0 - gate)))
    dp_wait(eall.at[dp], eall.at[dp], 0)
    dp_wait(lall.at[dp], lall.at[dp], 1)
    out_copies = [
        pltpu.make_async_copy(eall, early_o, osem.at[3, 0]),
        pltpu.make_async_copy(lall, late_o, osem.at[3, 1]),
    ]
    for copy in out_copies:
        copy.start()
    reduce_self.gather_end()
    reduce_self.gather_start(0)
    for chain in chains:
        chain.finish()
    reduce_cross.gather_end()
    reduce_self.gather_end()
    for copy in pending:
        copy.wait_send()
    for copy in out_copies:
        copy.wait()


def finish_kernel(
    place, items, grads_h, early_ref, late_ref,
    qkv_o, attn_out_o, cross_q_o, cross_kv_o, cross_out_o, up_o, down_o, mod_o,
    gb_attn_o, gb_cross_o, gb_up_o, gb_mod_o,
    low, full_v, kv_v, mod_v, isem, osem,
):
    names = ("up", "down", "qkv", "cross_kv", "attn_out", "cross_out", "cross_q")
    outs = {
        "up": up_o, "down": down_o, "qkv": qkv_o, "attn_out": attn_out_o, "cross_out": cross_out_o,
        "cross_q": cross_q_o, "cross_kv": cross_kv_o,
    }
    loads = {}
    for i, name in enumerate(names):
        at, rows = place[name]
        loads[name] = pltpu.make_async_copy(
            grads_h.at[at : at + rows], low.at[at : at + rows], isem.at[i]
        )
        loads[name].start()
    stores = []

    def store(src, dst, i):
        copy = pltpu.make_async_copy(src, dst, osem.at[i])
        copy.start()
        stores.append(copy)

    dp_count, slots, D = early_ref.shape
    MB = late_ref.shape[2]
    keep = lax.rem(lax.broadcasted_iota(jnp.int32, (dp_count * slots, MB), 0), slots) < items
    late = jnp.where(keep, late_ref[...].reshape(dp_count * slots, MB), 0.0)
    early = early_ref[...]
    mod_v[...] = dot_tn(early.reshape(dp_count * slots, D).astype(BF), late.astype(BF))
    store(mod_v, mod_o, 7)
    gb_mod_o[...] = jnp.sum(late, axis=0)
    sums = jnp.sum(early, axis=0)
    gb_up_o[...] = sums[3]
    gb_cross_o[...] = sums[4]
    gb_attn_o[...] = sums[5]
    for i, name in enumerate(names):
        at, rows = place[name]
        loads[name].wait()
        if name == "cross_kv":
            ident = (
                lax.broadcasted_iota(jnp.int32, (rows, rows), 0)
                == lax.broadcasted_iota(jnp.int32, (rows, rows), 1)
            ).astype(F32).astype(BF)
            kv_v[...] = dot_tn(low[at : at + rows, :], ident)
            store(kv_v, outs[name], i)
        else:
            full_v[at : at + rows, :] = low[at : at + rows, :].astype(F32)
            store(full_v.at[at : at + rows], outs[name], i)
    for copy in stores:
        copy.wait()


def body(
    dp_count,
    tokens,
    seg_ids,
    time_embed,
    text_states,
    text_lengths,
    out_grad,
    w_qkv,
    w_attn_out,
    b_attn_out,
    w_cross_q,
    w_cross_kv,
    w_cross_out,
    b_cross_out,
    w_up,
    b_up,
    w_down,
    w_mod,
    b_mod,
):
    _, R, D = tokens.shape
    T = R * TP
    items = time_embed.shape[1]
    shard_txt = text_states.shape[2]
    TL = items * shard_txt
    TK = TP * TL
    HW = w_cross_q.shape[1]
    HL = HW // DH
    HEADS = TP * HL
    FF = w_up.shape[1]
    MB = w_mod.shape[1]
    place, total_rows = bucket_rows(FF, HW)
    text = text_states[0].reshape(TL, D)

    extra = 0
    step = 8
    while step < dp_count:
        extra += 1
        step *= 2
    room = total_rows - total_rows // 8 + 2 * extra * (total_rows // 16)

    hbm = pl.BlockSpec(memory_space=pl.ANY)
    vmem = pl.BlockSpec(memory_space=pltpu.VMEM)
    smem = pl.BlockSpec(memory_space=pltpu.SMEM)
    V = pltpu.VMEM
    DMA = pltpu.SemaphoreType.DMA
    chunks = max(HL, 2)
    scratch = [
        V((TP, R, D), BF), V((TP, R, D), BF), V((TP, TL, D), BF), V((TP, HW, T), BF), V((TP, R, D), BF),
        V((3 * HW, D), BF), V((D, 2 * HW), BF), V((TP, 5, HW, D), BF),
        V((D, FF), BF), V((FF, D), BF), V((D, MB), BF),
        V((TP, 8, MB), F32), V((6, 8, D), F32), V((1, T), F32), V((T, 1), F32), V((16, T), BF), V((TK, 1), F32),
        V((T, D), BF), V((T, D), BF), V((3 * HW, T), BF), V((2 * HL, T, DH), BF), V((HL, T, T), F32),
        V((T, D), F32), V((T, 1), F32), V((T, D), BF), V((TP * HW, T), BF), V((TP * 2 * HW, TK), BF),
        V((HEADS, TK, DH), BF), V((HEADS, TK, DH), BF), V((HEADS, TK, T), F32), V((TP * HW, T), BF), V((R, D), F32),
        V((T, D), BF), V((R, D), F32), V((R, 1), F32), V((T, FF), BF), V((T, FF), BF), V((T, D), BF),
        V((TP, R, D), BF), V((TP - 1, R, D), BF),
        V((R, D), F32), V((TP * HW, T), BF), V((TP * HW, T), BF), V((TP * 2 * HW, TK), F32),
        V((TP * 2 * HW, TK), BF), V((R, D), F32), V((T, D), BF), V((HW, T), BF), V((3 * HW, T), BF),
        V((2 * DH, T), F32),
        V((TP, R, D), BF), V((TP - 1, R, D), BF),
        V((6, 16, D), F32), V((TP, 8, MB), F32), V((TP - 1, 8, MB), F32), V((8, D), F32), V((TP - 1, 8, D), F32),
        V((8, D), F32), V((dp_count, 8, D), F32), V((dp_count, 8, MB), F32),
        V((total_rows, D), BF), V((room, D), BF),
        DMA((11,)), DMA((5, TP)), DMA((5, TP)), DMA((6, 5, chunks)), DMA((6, TP, chunks)), DMA((4,)), DMA((4,)),
        DMA((3, 2, 6 + extra)), DMA((3, 2, 6 + extra)), DMA((2, dp_count)), DMA((2, dp_count)), DMA((4, 2)),
    ]
    d_tokens, d_time, d_text, grads, early, late = pl.pallas_call(
        functools.partial(layer_kernel, (dp_count, place, items)),
        out_shape=(
            jax.ShapeDtypeStruct((R, D), BF),
            jax.ShapeDtypeStruct((items, 1, D), F32),
            jax.ShapeDtypeStruct((TL, D), BF),
            jax.ShapeDtypeStruct((total_rows, D), BF),
            jax.ShapeDtypeStruct((dp_count, 8, D), F32),
            jax.ShapeDtypeStruct((dp_count, 8, MB), F32),
        ),
        in_specs=[hbm] * 11 + [vmem] * 6 + [smem],
        out_specs=(vmem, vmem, vmem, hbm, hbm, hbm),
        scratch_shapes=scratch,
        name="layer",
        compiler_params=pltpu.CompilerParams(
            collective_id=0, has_side_effects=True, vmem_limit_bytes=63 * 1024 * 1024
        ),
    )(
        tokens[0], out_grad[0], text, w_qkv.T, w_attn_out, w_cross_q.T, w_cross_kv, w_cross_out,
        w_up, w_down, w_mod, seg_ids, jnp.transpose(time_embed, (1, 0, 2)),
        b_attn_out, b_cross_out, b_up, b_mod, text_lengths,
    )

    f32 = lambda *shape: jax.ShapeDtypeStruct(shape, F32)
    g_qkv, g_attn, g_cq, g_ckv, g_co, g_up, g_down, g_mod, gb_attn, gb_cross, gb_up, gb_mod = pl.pallas_call(
        functools.partial(finish_kernel, place, items),
        out_shape=(
            f32(3 * HW, D), f32(HW, D), f32(HW, D), f32(D, 2 * HW), f32(HW, D), f32(FF, D), f32(FF, D),
            f32(D, MB), f32(D), f32(D), f32(FF), f32(MB),
        ),
        in_specs=[hbm, vmem, vmem],
        out_specs=(hbm,) * 8 + (vmem,) * 4,
        scratch_shapes=[
            V((total_rows, D), BF), V((total_rows, D), F32), V((D, 2 * HW), F32), V((D, MB), F32), DMA((7,)), DMA((8,)),
        ],
        name="finish",
        compiler_params=pltpu.CompilerParams(vmem_limit_bytes=40 * 1024 * 1024),
    )(grads, early, late)
    return (
        d_tokens[None],
        jnp.transpose(d_time, (1, 0, 2)),
        d_text.reshape(1, items, shard_txt, D),
        g_qkv.T,
        g_attn,
        gb_attn,
        g_cq.T,
        g_ckv,
        g_co,
        gb_cross,
        g_up,
        gb_up,
        g_down,
        g_mod,
        gb_mod,
    )


def solution(mesh):
    placed = (
        P("dp", "tp", None),
        P("dp", None),
        P("dp", None, None),
        P("dp", None, "tp", None),
        P("dp", None),
        P("dp", "tp", None),
        P(None, "tp"),
        P("tp", None),
        P(),
        P(None, "tp"),
        P(None, "tp"),
        P("tp", None),
        P(),
        P(None, "tp"),
        P("tp"),
        P("tp", None),
        P(None, "tp"),
        P("tp"),
    )
    return jax.shard_map(
        functools.partial(body, mesh.shape["dp"]),
        mesh=mesh,
        in_specs=placed,
        out_specs=(
            P("dp", "tp", None),
            P("dp", None, None),
            P("dp", None, "tp", None),
            P(None, "tp"),
            P("tp", None),
            P(),
            P(None, "tp"),
            P(None, "tp"),
            P("tp", None),
            P(),
            P(None, "tp"),
            P("tp"),
            P("tp", None),
            P(None, "tp"),
            P("tp"),
        ),
        check_vma=False,
    )
```

```python
import functools
import math

import jax
import jax.numpy as jnp
from jax import lax
from jax.experimental import pallas as pl
from jax.experimental.pallas import tpu as pltpu
from jax.sharding import PartitionSpec as P

DH = 64
TP = 4
MESH = pl.DeviceIdType.MESH
BF = jnp.bfloat16
F32 = jnp.float32
GELU_C = math.sqrt(2.0 / math.pi)


def dot_nn(left, right):
    return jnp.dot(left, right, preferred_element_type=F32)


def dot_tn(left, right):
    return lax.dot_general(left, right, (((0,), (0,)), ((), ())), preferred_element_type=F32)


def dot_nt(left, right):
    return lax.dot_general(left, right, (((1,), (1,)), ((), ())), preferred_element_type=F32)


def normalize(values):
    center = values - jnp.mean(values, axis=-1, keepdims=True)
    inverse = lax.rsqrt(jnp.mean(center * center, axis=-1, keepdims=True) + 1e-06)
    return center * inverse, inverse


def normalize_back(grad, normed, inverse):
    return inverse * (
        grad
        - jnp.mean(grad, axis=-1, keepdims=True)
        - normed * jnp.mean(grad * normed, axis=-1, keepdims=True)
    )


def bucket_rows(hidden, heads_width):
    sizes = [
        ("up", hidden),
        ("down", hidden),
        ("cross_out", heads_width),
        ("cross_q", heads_width),
        ("cross_kv", 2 * heads_width),
        ("attn_out", heads_width),
        ("qkv", 3 * heads_width),
    ]
    at, place = 0, {}
    for name, rows in sizes:
        place[name] = (at, rows)
        at += rows
    return place, at


def layer_kernel(
    dims,
    tok_h, og_h, text_h, wqkvT_h, wo_h, wcqT_h, wckv_h, wco_h, wup_h, wdn_h, wmod_h,
    seg_ref, time_ref, b_attn_out_ref, b_cross_out_ref, b_up_ref, b_mod_ref, tlen_ref,
    dtok_o, dtime_o, dtext_o, grads_o, early_o, late_o,
    tok, og, text, att, gc,
    wqkvT, wckv, wfull, wup, wdn, wmod,
    modbuf, mods, segrow, segcol, onehot, ktag,
    attn_in, na, qkvT, kvx, pself,
    stream_a, inv_c, cross_in, cqT, ckvT, kblk, vblk, pcross, catT, branch_own,
    mlp_in, nm_own, invm_own, act, slope, dpre, dbm, rs_send, rs_recv,
    gc_own, dcT, dcqT, dckvT, grad_own, dba, dOT, dqkvT,
    rs2_send, rs2_recv, dm, dmp, dmr, dsil, dsr, early, eall, lall,
    grads, rbuf,
    lsem, ssem, rsem, csem_s, csem_r, wsem_s, wsem_r, gsem_s, gsem_r, esem_s, esem_r, osem,
):
    dp_count, place, items = dims
    tp = lax.axis_index("tp")
    dp = lax.axis_index("dp")
    R = tok.shape[1]
    D = tok.shape[2]
    T = TP * R
    HW = att.shape[1]
    HL = HW // DH
    TK = TP * text.shape[1]
    TL = text.shape[1]
    HEADS = TP * HL
    MB = modbuf.shape[2]
    scale = 1.0 / math.sqrt(DH)
    sub = lax.rem(dp, 8)
    base8 = dp - sub
    core = lax.rem(sub, 2)
    chip = sub // 2

    def tp_peer(k):
        return {"tp": lax.rem(tp + k, TP)}

    def remote(src, dst, send, recv, peer):
        return pltpu.make_async_remote_copy(
            src_ref=src, dst_ref=dst, send_sem=send, recv_sem=recv, device_id=peer, device_id_type=MESH
        )

    def span(at, size, unit):
        return pl.ds(pl.multiple_of(at, unit), size)

    loads = [
        (tok_h, tok.at[0]),
        (wmod_h, wmod),
        (text_h, text.at[0]),
        (wqkvT_h, wqkvT),
        (wcqT_h, wfull.at[0, 1]),
        (wo_h, wfull.at[0, 0]),
        (wco_h, wfull.at[0, 2]),
        (wckv_h, wckv),
        (og_h, og.at[0]),
        (wup_h, wup),
        (wdn_h, wdn),
    ]
    local = [pltpu.make_async_copy(src, dst, lsem.at[i]) for i, (src, dst) in enumerate(loads)]
    for copy in local:
        copy.start()

    barrier = pltpu.get_barrier_semaphore()
    for k in range(1, TP):
        pl.semaphore_signal(barrier, inc=1, device_id=tp_peer(k), device_id_type=MESH)

    def greet(k, carry):
        pl.semaphore_signal(
            barrier, inc=1, device_id={"dp": lax.rem(dp + k, dp_count)}, device_id_type=MESH
        )
        return carry

    lax.fori_loop(1, dp_count, greet, 0)

    early[...] = jnp.zeros(early.shape, F32)
    for item in range(items):
        early[item : item + 1, :] = time_ref[item]
    time = early[...]
    sig = 1.0 / (1.0 + jnp.exp(-time))
    silu_low = (time * sig).astype(BF)
    early[...] = silu_low.astype(F32)
    local[1].wait()
    modbuf[tp] = dot_nn(silu_low, wmod[...]) + b_mod_ref[...].astype(F32).reshape(1, MB)
    local[0].wait()

    pl.semaphore_wait(barrier, TP - 1 + dp_count - 1)

    pending, chains = [], []
    inner = (tp > 0) & (tp < TP - 1)
    slot_a = jnp.where(tp == 3, 3, 1)
    slot_b = jnp.where((tp == 0) | (tp == 3), 2, 3)
    slot_c = jnp.where(tp == 0, 3, jnp.where(tp == 3, 1, 2))
    right, left = {"tp": lax.rem(tp + 1, TP)}, {"tp": lax.rem(tp + TP - 1, TP)}
    onward = {"tp": jnp.where(tp == 1, 0, TP - 1)}
    onward_slot = jnp.where(tp == 1, 3, 1)

    class Chain:
        def __init__(self, index, view):
            self.index, self.view, self.started = index, view, []
            chains.append(self)

        def copy(self, src, dst, send, chunk, peer):
            return remote(
                self.view(src, chunk), self.view(dst, chunk),
                csem_s.at[self.index, send, chunk], csem_r.at[self.index, dst, chunk], peer,
            )

        def start(self, chunk):
            self.started.append(chunk)

            @pl.when(tp < TP - 1)
            def _():
                self.copy(0, 3, 0, chunk, right).start()

            @pl.when(tp > 0)
            def _():
                self.copy(0, 1, 1, chunk, left).start()

        def step(self, which, chunk):
            slot = (slot_a, slot_b, slot_c)[which]
            self.copy(slot, slot, 2 + which, chunk, right).wait_recv()

            @pl.when(inner)
            def _():
                if which == 0:
                    self.copy(slot, 2, 2, chunk, left).start()
                elif which == 1:
                    self.copy(slot, 2, 3, chunk, right).start()
                else:
                    self.copy(slot, onward_slot, 4, chunk, onward).start()

        def finish(self):
            for chunk in self.started:

                @pl.when(tp < TP - 1)
                def _():
                    self.copy(0, 3, 0, chunk, right).wait_send()

                @pl.when(tp > 0)
                def _():
                    self.copy(0, 1, 1, chunk, left).wait_send()

                @pl.when(inner)
                def _():
                    self.copy(slot_a, 2, 2, chunk, left).wait_send()
                    self.copy(slot_b, 2, 3, chunk, right).wait_send()
                    self.copy(slot_c, onward_slot, 4, chunk, onward).wait_send()

    half = R // 2
    tok_chain = Chain(0, lambda slot, c: tok.at[slot, c * half : (c + 1) * half])
    text_chain = Chain(1, lambda slot, c: text.at[slot])
    WR, WC = HW // 4, D // 2
    wcol = pl.multiple_of(core * WC, 128)
    pieces = (slice(0, 3), slice(3, 5))
    swapped = lax.rem(chip, 2) * 2 + chip // 2
    places = (chip, swapped)
    w_chain = Chain(2, lambda slot, c: wfull.at[slot, pieces[c], span(places[c] * WR, WR, 16), pl.ds(wcol, WC)])
    att_chain = Chain(3, lambda slot, c: att.at[slot, c * DH : (c + 1) * DH])
    og_chain = Chain(4, lambda slot, c: og.at[slot, c * half : (c + 1) * half])
    gc_chain = Chain(5, lambda slot, c: gc.at[slot, c * half : (c + 1) * half])

    def direct(tag, src_of, dst_of):
        copies = []
        for k in range(1, TP):
            copy = remote(src_of(k), dst_of(k), ssem.at[tag, k], rsem.at[tag, TP - k], tp_peer(k))
            copy.start()
            copies.append(copy)
        pending.extend(copies)
        return copies

    def arrived(copies, slot):
        copies[TP - 1 - slot].wait_recv()

    tok_chain.start(0)
    tok_chain.start(1)
    mod_copies = direct(0, lambda k: modbuf.at[tp], lambda k: modbuf.at[tp])

    eye = lax.broadcasted_iota(jnp.int32, (R, R), 0) == lax.broadcasted_iota(jnp.int32, (R, R), 1)
    for slot in range(TP):
        owner = lax.rem(tp + slot, TP)
        row = seg_ref[:, pl.ds(pl.multiple_of(owner * R, R), R)].astype(F32)
        segrow[:, slot * R : (slot + 1) * R] = row
        col = jnp.sum(jnp.where(eye, row, 0.0), axis=1, keepdims=True)
        segcol[slot * R : (slot + 1) * R, :] = col
    kinds = lax.broadcasted_iota(jnp.int32, (16, T), 0)
    matches = (segrow[...] == kinds.astype(F32)) & (kinds < items)
    onehot[...] = jnp.where(matches | (kinds == items), 1.0, 0.0).astype(BF)
    key_at = lax.broadcasted_iota(jnp.int32, (TK, 1), 0)
    key_slot = key_at // TL
    key_item = lax.rem(key_at, TL) // (TL // items)
    key_pos = lax.rem(key_slot + tp, TP) * (TL // items) + lax.rem(key_at, TL // items)
    tag = jnp.full((TK, 1), -1.0, F32)
    for item in range(items):
        inside = (key_item == item) & (key_pos < tlen_ref[0, item])
        tag = jnp.where(inside, float(item), tag)
    ktag[...] = tag

    for k in range(1, TP):
        arrived(mod_copies, k)
    for j in range(6):
        lo, hi = j * D, (j + 1) * D
        at = lo
        while at < hi:
            block = at // MB
            end = min(hi, (block + 1) * MB)
            mods[j, :, at - lo : end - lo] = modbuf[block, :, at - block * MB : end - block * MB]
            at = end

    def per_frame(j, rows):
        col = segcol[rows, :]
        out = mods[j, items - 1 : items, :]
        for item in range(items - 2, -1, -1):
            out = jnp.where(col == float(item), mods[j, item : item + 1, :], out)
        return out

    def item_sums(rows, values):
        return dot_nn(onehot[:, rows], values.astype(BF))

    own, every = slice(0, R), slice(0, T)
    local[3].wait()

    def project(slot):
        rows = span(slot * R, R, R)
        normed, inverse = normalize(tok[slot].astype(F32))
        na[rows, :] = normed.astype(BF)
        x = (normed * (1.0 + per_frame(1, rows)) + per_frame(0, rows)).astype(BF)
        attn_in[rows, :] = x
        qkvT[:, rows] = dot_nt(wqkvT[...], x).astype(BF)

    project(0)
    tok_chain.step(0, 0)
    tok_chain.step(0, 1)
    local[2].wait()
    text_chain.start(0)
    local[7].wait()
    ident = (
        lax.broadcasted_iota(jnp.int32, (D, D), 0) == lax.broadcasted_iota(jnp.int32, (D, D), 1)
    ).astype(F32).astype(BF)
    wckvT = dot_tn(wckv[...], ident).astype(BF)
    wfull[0, 3] = wckvT[:HW]
    wfull[0, 4] = wckvT[HW:]
    for copy in local[4:7]:
        copy.wait()
    tok_chain.step(1, 0)
    tok_chain.step(1, 1)
    w_chain.start(0)
    w_chain.start(1)
    project(slot_a)
    text_chain.step(0, 0)
    tok_chain.step(2, 0)
    tok_chain.step(2, 1)
    project(slot_b)
    w_chain.step(0, 0)
    project(slot_c)

    for h in range(HL):
        q0 = h * 3 * DH
        kvx[2 * h] = (qkvT[q0 + DH : q0 + 2 * DH, :].astype(F32).T * scale).astype(BF)
        kvx[2 * h + 1] = qkvT[q0 + 2 * DH : q0 + 3 * DH, :].astype(F32).T.astype(BF)
        scores = dot_nn(kvx[2 * h], qkvT[q0 : q0 + DH, :])
        scores = jnp.where(segcol[...] == segrow[...], scores, -1000000000.0)
        peak = jnp.max(scores, axis=0, keepdims=True)
        exponent = jnp.exp(scores - peak)
        probs = exponent * (1.0 / jnp.sum(exponent, axis=0, keepdims=True))
        pself[h] = probs
        att[0, h * DH : (h + 1) * DH, :] = dot_nn(qkvT[q0 + 2 * DH : q0 + 3 * DH, :], probs.astype(BF)).astype(BF)

    class Plane:
        def __init__(self, index, bits):
            self.index, self.bits, self.open = index, bits, None

        def send(self, step, rows, bit):
            at = wfull.at[1:TP, pieces[self.index], rows, pl.ds(wcol, WC)]
            copy = remote(
                at, at, wsem_s.at[self.index, step], wsem_r.at[self.index, step],
                {"dp": base8 + jnp.bitwise_xor(sub, bit)},
            )
            copy.start()
            pending.append(copy)
            self.open = copy

        def step(self, step):
            if step:
                self.open.wait_recv()
            place = places[self.index]
            if step == 0:
                self.send(0, span(place * WR, WR, 16), self.bits[0])
            elif step == 1:
                self.send(1, span(place // 2 * (2 * WR), 2 * WR, 16), self.bits[1])
            elif step == 2:
                self.send(2, slice(0, HW), 1)

    planes = (Plane(0, (2, 4)), Plane(1, (4, 2)))
    w_chain.step(0, 1)
    text_chain.step(1, 0)
    w_chain.step(1, 0)
    for h in range(HL):
        att_chain.start(h)
    w_chain.step(1, 1)
    w_chain.step(2, 0)
    planes[0].step(0)
    w_chain.step(2, 1)
    planes[1].step(0)
    text_chain.step(2, 0)
    for h in range(HL):
        att_chain.step(0, h)
    local[8].wait()
    planes[0].step(1)
    planes[1].step(1)
    for h in range(HL):
        att_chain.step(1, h)
    og_chain.start(0)
    og_chain.start(1)
    for h in range(HL):
        att_chain.step(2, h)
    planes[0].step(2)
    planes[1].step(2)
    og_chain.step(0, 0)
    og_chain.step(0, 1)
    planes[1].step(3)

    def full(i):
        return wfull[:, i].reshape(TP * HW, D)

    text_flat = text[...].reshape(TK, D)
    for s in range(TP):
        for part in range(2):
            ckvT[(2 * s + part) * HW : (2 * s + part + 1) * HW, :] = dot_nt(wfull[s, 3 + part], text_flat).astype(BF)
    quad = 4 * DH
    lane_head = lax.broadcasted_iota(jnp.int32, (TK, quad), 1) // DH
    for g in range(HEADS // 4):
        heads_at = [(4 * g + j) * 2 * DH for j in range(4)]
        for blocks, offset, factor in ((kblk, 0, scale), (vblk, DH, 1.0)):
            turned = jnp.concatenate(
                [ckvT[at + offset : at + offset + DH, :] for at in heads_at], axis=0
            ).astype(F32).T * factor
            for j in range(4):
                blocks[g, j * TK : (j + 1) * TK, :] = jnp.where(lane_head == j, turned, 0.0).astype(BF)
    og_chain.step(1, 0)
    og_chain.step(1, 1)
    planes[0].step(3)

    b_attn_out = b_attn_out_ref[...].astype(F32).reshape(1, D)
    b_cross_out = b_cross_out_ref[...].astype(F32).reshape(1, D)
    b_up = b_up_ref[...].astype(F32).reshape(1, wup.shape[1])

    gathered = jnp.concatenate(
        [
            jnp.concatenate([att[k, :, (b - k) % TP * R : ((b - k) % TP + 1) * R] for b in range(TP)], axis=1)
            for k in range(TP)
        ],
        axis=0,
    )
    stream_a[...] = dot_tn(gathered, full(0)) + b_attn_out
    branch_own[...] = stream_a[own, :]
    stream_a[...] = tok[...].reshape(T, D).astype(F32) + per_frame(2, every) * stream_a[...]
    normed, inverse = normalize(stream_a[...])
    inv_c[...] = inverse
    cross_in[...] = normed.astype(BF)
    cqT[...] = dot_nt(full(1), cross_in[...]).astype(BF)
    allowed = ktag[...] == segrow[...]

    def cross_forward(g, carry):
        scores_all = dot_nn(kblk[g], cqT[span(g * quad, quad, quad), :])
        for j in range(4):
            h = 4 * g + j
            scores = jnp.where(allowed, scores_all[j * TK : (j + 1) * TK], -1000000000.0)
            peak = jnp.max(scores, axis=0, keepdims=True)
            exponent = jnp.exp(scores - peak)
            probs = exponent * (1.0 / jnp.sum(exponent, axis=0, keepdims=True))
            pcross[h] = probs
            vT = ckvT[span(h * 2 * DH + DH, DH, DH), :]
            catT[span(h * DH, DH, DH), :] = dot_nn(vT, probs.astype(BF)).astype(BF)
        return carry

    lax.fori_loop(0, HEADS // 4, cross_forward, 0)
    og_chain.step(2, 0)
    og_chain.step(2, 1)
    normed, inverse = normalize(stream_a[...] + dot_tn(catT[...], full(2)) + b_cross_out)
    nm_own[...] = normed[:R]
    invm_own[...] = inverse[:R]
    mlp_in[...] = (normed * (1.0 + per_frame(4, every)) + per_frame(3, every)).astype(BF)

    local[9].wait()
    local[10].wait()
    pre = dot_nn(mlp_in[...], wup[...]) + b_up
    square = pre * pre
    bend = jnp.tanh(GELU_C * pre * (1.0 + 0.044715 * square))
    act[...] = (0.5 * pre * (1.0 + bend)).astype(BF)
    slope[...] = 0.5 * (1.0 + bend) + 0.5 * pre * (1.0 - bend * bend) * (
        GELU_C * (1.0 + 3.0 * 0.044715 * square)
    )
    dbm[...] = (og[...].reshape(T, D).astype(F32) * per_frame(5, every)).astype(BF)
    dpre[...] = (dot_nt(dbm[...], wdn[...]) * slope[...]).astype(BF)
    rs_send[...] = dot_nt(dpre[...], wup[...]).astype(BF).reshape(TP, R, D)

    def to_owners(source, target, tag):
        copies = {}
        for b in (2, 1, 3):
            copies[b] = remote(
                source.at[b], target.at[TP - 1 - b], ssem.at[tag, b], rsem.at[tag, TP - b], tp_peer(b)
            )
            copies[b].start()
        pending.extend(copies.values())
        return copies

    rs_copies = to_owners(rs_send, rs_recv, 1)
    early[3:4, :] = dot_nn(onehot[...], dpre[...])[items : items + 1, :]

    bits = []
    step = 8
    while step < dp_count:
        bits.append(step)
        step *= 2

    class Reduce:
        def __init__(self, index, start, rows, room):
            self.parts = []
            half = rows // 2
            for part in range(2):
                chain = (1, 2, 4) if part == 0 else (1, 4, 2)
                self.parts.append((start + part * half, half, chain, part * half))
            self.index, self.room = index, room
            self.open, self.own = [], []

        def sem(self, part, step):
            return gsem_s.at[self.index, part, step], gsem_r.at[self.index, part, step]

        def launch(self, src, dst, part, step, bit):
            send, recv = self.sem(part, step)
            copy = remote(src, dst, send, recv, {"dp": jnp.bitwise_xor(dp, bit)})
            copy.start()
            pending.append(copy)
            return copy

        def bounds(self, part, level):
            start, rows, chain, _ = self.parts[part]
            at, size = start, rows
            for bit in chain[:level]:
                size //= 2
                at = at + jnp.bitwise_and(dp // bit, 1) * size
            return at, size

        def scatter_start(self, level):
            self.open = []
            for part in range(2):
                at, size = self.bounds(part, level)
                bit = self.parts[part][2][level]
                half = size // 2
                mine = jnp.bitwise_and(dp // bit, 1)
                other = pl.multiple_of(at + (1 - mine) * half, 16)
                rows = self.parts[part][1]
                room = self.room + 2 * (rows - (rows >> level)) + part * half
                copy = self.launch(
                    grads.at[pl.ds(other, half)], rbuf.at[room : room + half], part, level, bit
                )
                self.open.append((copy, room, half))

        def scatter_end(self, level):
            for part in range(2):
                copy, room, half = self.open[part]
                copy.wait_recv()
                at, size = self.bounds(part, level + 1)
                mine = pl.ds(pl.multiple_of(at, 16), half)
                grads[mine, :] = (grads[mine, :].astype(F32) + rbuf[room : room + half, :].astype(F32)).astype(BF)

        def widen(self):
            for i, bit in enumerate(bits):
                for part in range(2):
                    at, size = self.bounds(part, 3)
                    rows = self.parts[part][1]
                    mine = pl.ds(pl.multiple_of(at, 16), size)
                    room = self.room + 2 * (rows - rows // 8) + (2 * i + part) * size
                    copy = self.launch(grads.at[mine], rbuf.at[room : room + size], part, 6 + i, bit)
                    copy.wait_recv()
                    grads[mine, :] = (
                        grads[mine, :].astype(F32) + rbuf[room : room + size, :].astype(F32)
                    ).astype(BF)

        def gather_start(self, level):
            self.open = []
            source = grads if level == 2 else grads_o
            if level == 1:
                for copy in self.own:
                    copy.wait()
            for part in range(2):
                at, size = self.bounds(part, level + 1)
                bit = self.parts[part][2][level]
                mine = pl.ds(pl.multiple_of(at, 16), size)
                self.open.append(
                    self.launch(source.at[mine], grads_o.at[mine], part, 3 + (2 - level), bit)
                )
                if level == 2:
                    copy = pltpu.make_async_copy(grads.at[mine], grads_o.at[mine], osem.at[self.index, part])
                    copy.start()
                    self.own.append(copy)

        def gather_end(self):
            for copy in self.open:
                copy.wait_recv()

    mid0 = place["cross_out"][0]
    mid1 = place["attn_out"][0]
    total_rows = grads.shape[0]
    extra = 2 * len(bits)
    rooms, at = [], 0
    for rows in (mid0, mid1 - mid0, total_rows - mid1):
        rooms.append(at)
        at += rows - rows // 8 + extra * (rows // 16)
    reduce_mlp = Reduce(0, 0, mid0, rooms[0])
    reduce_cross = Reduce(1, mid0, mid1 - mid0, rooms[1])
    reduce_self = Reduce(2, mid1, total_rows - mid1, rooms[2])

    def put(name, values):
        at, rows = place[name]
        grads[at : at + rows, :] = values.astype(BF)

    put("up", dot_tn(mlp_in[...], dpre[...]))
    put("down", dot_tn(act[...], dbm[...]))
    reduce_mlp.scatter_start(0)
    dm[5] = item_sums(every, og[...].reshape(T, D).astype(F32) * dot_nn(act[...], wdn[...]))

    d_mlp = rs_send[0].astype(F32)
    reduce_mlp.scatter_end(0)
    reduce_mlp.scatter_start(1)
    reduce_mlp.scatter_end(1)
    reduce_mlp.scatter_start(2)
    for k in (1, 3, 2):
        rs_copies[TP - k].wait_recv()
        d_mlp = d_mlp + rs_recv[k - 1].astype(F32)
    normed = nm_own[...]
    grad_c = og[0].astype(F32) + normalize_back(d_mlp * (1.0 + per_frame(4, own)), normed, invm_own[...])
    gc_own[...] = grad_c
    gc[0] = grad_c.astype(BF)
    gc_chain.start(0)
    gc_chain.start(1)
    dm[3] = item_sums(own, d_mlp)
    dm[4] = item_sums(own, d_mlp * normed)

    reduce_mlp.scatter_end(2)
    reduce_mlp.widen()
    reduce_mlp.gather_start(2)
    for which in range(3):
        gc_chain.step(which, 0)
        gc_chain.step(which, 1)
        if which == 1:
            reduce_mlp.gather_end()
            reduce_mlp.gather_start(1)
    gc_flat = gc[...].reshape(T, D)
    dcT[...] = dot_nt(full(2), gc_flat).astype(BF)

    def cross_backward(g, carry):
        d_probs_all = dot_nn(vblk[g], dcT[span(g * quad, quad, quad), :])
        for j in range(4):
            h = 4 * g + j
            hr = span(h * DH, DH, DH)
            kr, vr = span(h * 2 * DH, DH, DH), span(h * 2 * DH + DH, DH, DH)
            probs = pcross[h]
            d_probs = d_probs_all[j * TK : (j + 1) * TK]
            d_scores = (probs * (d_probs - jnp.sum(probs * d_probs, axis=0, keepdims=True))).astype(BF)
            dcqT[hr, :] = (dot_nn(ckvT[kr, :], d_scores) * scale).astype(BF)
            dckvT[kr, :] = (dot_nt(cqT[hr, :], d_scores) * scale).astype(BF)
            dckvT[vr, :] = dot_nt(dcT[hr, :], probs.astype(BF)).astype(BF)
        return carry

    lax.fori_loop(0, HEADS // 4, cross_backward, 0)
    d_cross = dot_tn(dcqT[...], full(1))
    back = normalize_back(d_cross, cross_in[...].astype(F32), inv_c[...])
    grad = gc_own[...] + back[:R]
    grad_own[...] = grad
    gate = per_frame(2, every)
    dba[own, :] = (grad * gate[:R]).astype(BF)
    rest = slice(R, T)
    dba[rest, :] = ((gc_flat[R:].astype(F32) + back[R:]) * gate[R:]).astype(BF)
    dOT[...] = dot_nt(wfull[0, 0], dba[...]).astype(BF)

    put("cross_out", dot_nn(catT[0:HW, :], gc_flat))
    put("cross_q", dot_nn(dcqT[0:HW, :], cross_in[...]))
    put("cross_kv", dot_nn(dckvT[0 : 2 * HW, :], text_flat))
    put("attn_out", dot_nn(att[0], dba[...]))
    reduce_cross.scatter_start(0)
    early[4:5, :] = dot_nn(onehot[...], gc_flat)[items : items + 1, :]
    early[5:6, :] = dot_nn(onehot[...], dba[...])[items : items + 1, :]
    eall[dp] = early[...]

    def dp_send(src, dst, index):
        def one(k, carry):
            peer = lax.rem(dp + k, dp_count)
            remote(
                src, dst, esem_s.at[index, k], esem_r.at[index, dp_count - k], {"dp": peer}
            ).start()
            return carry

        lax.fori_loop(1, dp_count, one, 0)

    def dp_wait(src, dst, index):
        def one(k, carry):
            remote(
                src, dst, esem_s.at[index, k], esem_r.at[index, k], {"dp": lax.rem(dp + k, dp_count)}
            ).wait()
            return carry

        lax.fori_loop(1, dp_count, one, 0)

    dp_send(eall.at[dp], eall.at[dp], 0)

    for h in range(HL):
        q0 = h * 3 * DH
        hr = slice(h * DH, (h + 1) * DH)
        probs = pself[h]
        d_probs = dot_nn(kvx[2 * h + 1], dOT[hr, :])
        d_scores = (probs * (d_probs - jnp.sum(probs * d_probs, axis=0, keepdims=True))).astype(BF)
        dqkvT[q0 : q0 + DH, :] = (dot_nn(qkvT[q0 + DH : q0 + 2 * DH, :], d_scores) * scale).astype(BF)
        dqkvT[q0 + DH : q0 + 2 * DH, :] = (dot_nt(qkvT[q0 : q0 + DH, :], d_scores) * scale).astype(BF)
        dqkvT[q0 + 2 * DH : q0 + 3 * DH, :] = dot_nt(dOT[hr, :], probs.astype(BF)).astype(BF)

    put("qkv", dot_nn(dqkvT[...], attn_in[...]))
    reduce_self.scatter_start(0)
    reduce_cross.scatter_end(0)
    reduce_cross.scatter_start(1)

    part = dot_tn(dqkvT[...], wqkvT[...])
    rs2_send[...] = part.astype(BF).reshape(TP, R, D)
    input_grad = rs2_send[...].reshape(T, D)
    dm[0] = dot_nn(onehot[...], input_grad)
    dm[1] = item_sums(every, input_grad.astype(F32) * na[...].astype(F32))
    dm[2] = item_sums(own, grad_own[...] * branch_own[...])

    for j in range(6):
        lo, hi = j * D, (j + 1) * D
        at = lo
        while at < hi:
            block = at // MB
            end = min(hi, (block + 1) * MB)
            dmp[block, :, at - block * MB : end - block * MB] = dm[j, 0:8, at - lo : end - lo]
            at = end
    dm_copies = direct(
        3, lambda k: dmp.at[lax.rem(tp + k, TP)], lambda k: dmr.at[TP - 1 - k]
    )
    rs2_copies = to_owners(rs2_send, rs2_recv, 2)
    reduce_self.scatter_end(0)
    reduce_self.scatter_start(1)
    reduce_mlp.gather_end()
    reduce_mlp.gather_start(0)

    dtext_o[...] = dot_tn(dckvT[:, 0:TL], wfull[:, 3:5].reshape(TP * 2 * HW, D)).astype(BF)
    reduce_cross.scatter_end(1)
    reduce_cross.scatter_start(2)

    d_mod = dmp[tp]
    for k in range(1, TP):
        arrived(dm_copies, k)
        d_mod = d_mod + dmr[k - 1]
    low = d_mod.astype(BF)
    lall[dp] = low.astype(F32)
    dsil[...] = dot_nt(low, wmod[...])
    ds_copies = direct(4, lambda k: dsil, lambda k: dsr.at[TP - 1 - k])

    reduce_self.scatter_end(1)
    reduce_self.scatter_start(2)
    dp_send(lall.at[dp], lall.at[dp], 1)
    reduce_cross.scatter_end(2)
    reduce_cross.widen()
    reduce_cross.gather_start(2)
    reduce_self.scatter_end(2)
    reduce_self.widen()
    reduce_self.gather_start(2)
    reduce_mlp.gather_end()
    reduce_cross.gather_end()
    reduce_cross.gather_start(1)
    reduce_self.gather_end()
    reduce_self.gather_start(1)

    d_in = rs2_send[0].astype(F32)
    for k in (1, 3, 2):
        rs2_copies[TP - k].wait_recv()
        d_in = d_in + rs2_recv[k - 1].astype(F32)
    normed, inverse = normalize(tok[0].astype(F32))
    dtok_o[...] = (
        grad_own[...] + normalize_back(d_in * (1.0 + per_frame(1, own)), normed, inverse)
    ).astype(BF)
    reduce_cross.gather_end()
    reduce_cross.gather_start(0)

    d_silu = dsil[...]
    for k in range(1, TP):
        arrived(ds_copies, k)
        d_silu = d_silu + dsr[k - 1]
    for item in range(items):
        value = time_ref[item]
        gate = 1.0 / (1.0 + jnp.exp(-value))
        dtime_o[item] = d_silu[item : item + 1, :] * (gate * (1.0 + value * (1.0 - gate)))
    dp_wait(eall.at[dp], eall.at[dp], 0)
    dp_wait(lall.at[dp], lall.at[dp], 1)
    out_copies = [
        pltpu.make_async_copy(eall, early_o, osem.at[3, 0]),
        pltpu.make_async_copy(lall, late_o, osem.at[3, 1]),
    ]
    for copy in out_copies:
        copy.start()
    reduce_self.gather_end()
    reduce_self.gather_start(0)
    for chain in chains:
        chain.finish()
    reduce_cross.gather_end()
    reduce_self.gather_end()
    for copy in pending:
        copy.wait_send()
    for copy in out_copies:
        copy.wait()


def finish_kernel(
    place, items, grads_h, early_h, late_h, dtok_h, dtime_h, dtext_h,
    dtok_o, dtime_o, dtext_o, qkv_o, attn_out_o, cross_q_o, cross_kv_o, cross_out_o, up_o, down_o, mod_o,
    gb_attn_o, gb_cross_o, gb_up_o, gb_mod_o,
    low, full_v, kv_v, mod_v, early_v, late_v, isem, osem,
):
    names = ("up", "down", "qkv", "cross_kv", "attn_out", "cross_out", "cross_q")
    outs = {
        "up": up_o, "down": down_o, "qkv": qkv_o, "attn_out": attn_out_o, "cross_out": cross_out_o,
        "cross_q": cross_q_o, "cross_kv": cross_kv_o,
    }
    loads = {}
    small = [
        pltpu.make_async_copy(early_h, early_v, isem.at[7]),
        pltpu.make_async_copy(late_h, late_v, isem.at[8]),
    ]
    stores = [
        pltpu.make_async_copy(dtok_h, dtok_o, osem.at[8]),
        pltpu.make_async_copy(dtime_h, dtime_o, osem.at[9]),
        pltpu.make_async_copy(dtext_h, dtext_o, osem.at[10]),
    ]
    for copy in small + stores:
        copy.start()
    for i, name in enumerate(names):
        at, rows = place[name]
        loads[name] = pltpu.make_async_copy(
            grads_h.at[at : at + rows], low.at[at : at + rows], isem.at[i]
        )
        loads[name].start()

    def store(src, dst, i):
        copy = pltpu.make_async_copy(src, dst, osem.at[i])
        copy.start()
        stores.append(copy)

    dp_count, slots, D = early_v.shape
    MB = late_v.shape[2]
    for copy in small:
        copy.wait()
    keep = lax.rem(lax.broadcasted_iota(jnp.int32, (dp_count * slots, MB), 0), slots) < items
    late = jnp.where(keep, late_v[...].reshape(dp_count * slots, MB), 0.0)
    early = early_v[...]
    mod_v[...] = dot_tn(early.reshape(dp_count * slots, D).astype(BF), late.astype(BF))
    store(mod_v, mod_o, 7)
    gb_mod_o[...] = jnp.sum(late, axis=0)
    sums = jnp.sum(early, axis=0)
    gb_up_o[...] = sums[3]
    gb_cross_o[...] = sums[4]
    gb_attn_o[...] = sums[5]
    for i, name in enumerate(names):
        at, rows = place[name]
        loads[name].wait()
        if name == "cross_kv":
            ident = (
                lax.broadcasted_iota(jnp.int32, (rows, rows), 0)
                == lax.broadcasted_iota(jnp.int32, (rows, rows), 1)
            ).astype(F32).astype(BF)
            kv_v[...] = dot_tn(low[at : at + rows, :], ident)
            store(kv_v, outs[name], i)
        else:
            full_v[at : at + rows, :] = low[at : at + rows, :].astype(F32)
            store(full_v.at[at : at + rows], outs[name], i)
    for copy in stores:
        copy.wait()


def body(
    dp_count,
    tokens,
    seg_ids,
    time_embed,
    text_states,
    text_lengths,
    out_grad,
    w_qkv,
    w_attn_out,
    b_attn_out,
    w_cross_q,
    w_cross_kv,
    w_cross_out,
    b_cross_out,
    w_up,
    b_up,
    w_down,
    w_mod,
    b_mod,
):
    _, R, D = tokens.shape
    T = R * TP
    items = time_embed.shape[1]
    shard_txt = text_states.shape[2]
    TL = items * shard_txt
    TK = TP * TL
    HW = w_cross_q.shape[1]
    HL = HW // DH
    HEADS = TP * HL
    FF = w_up.shape[1]
    MB = w_mod.shape[1]
    place, total_rows = bucket_rows(FF, HW)
    text = text_states[0].reshape(TL, D)

    extra = 0
    step = 8
    while step < dp_count:
        extra += 1
        step *= 2
    room = total_rows - total_rows // 8 + 2 * extra * (total_rows // 16)

    hbm = pl.BlockSpec(memory_space=pl.ANY)
    vmem = pl.BlockSpec(memory_space=pltpu.VMEM)
    smem = pl.BlockSpec(memory_space=pltpu.SMEM)
    V = pltpu.VMEM
    DMA = pltpu.SemaphoreType.DMA
    chunks = max(HL, 2)
    scratch = [
        V((TP, R, D), BF), V((TP, R, D), BF), V((TP, TL, D), BF), V((TP, HW, T), BF), V((TP, R, D), BF),
        V((3 * HW, D), BF), V((D, 2 * HW), BF), V((TP, 5, HW, D), BF),
        V((D, FF), BF), V((FF, D), BF), V((D, MB), BF),
        V((TP, 8, MB), F32), V((6, 8, D), F32), V((1, T), F32), V((T, 1), F32), V((16, T), BF), V((TK, 1), F32),
        V((T, D), BF), V((T, D), BF), V((3 * HW, T), BF), V((2 * HL, T, DH), BF), V((HL, T, T), F32),
        V((T, D), F32), V((T, 1), F32), V((T, D), BF), V((TP * HW, T), BF), V((TP * 2 * HW, TK), BF),
        V((HEADS // 4, 4 * TK, 4 * DH), BF), V((HEADS // 4, 4 * TK, 4 * DH), BF), V((HEADS, TK, T), F32), V((TP * HW, T), BF), V((R, D), F32),
        V((T, D), BF), V((R, D), F32), V((R, 1), F32), V((T, FF), BF), V((T, FF), F32), V((T, FF), BF), V((T, D), BF),
        V((TP, R, D), BF), V((TP - 1, R, D), BF),
        V((R, D), F32), V((TP * HW, T), BF), V((TP * HW, T), BF),
        V((TP * 2 * HW, TK), BF), V((R, D), F32), V((T, D), BF), V((HW, T), BF), V((3 * HW, T), BF),
        V((TP, R, D), BF), V((TP - 1, R, D), BF),
        V((6, 16, D), F32), V((TP, 8, MB), F32), V((TP - 1, 8, MB), F32), V((8, D), F32), V((TP - 1, 8, D), F32),
        V((8, D), F32), V((dp_count, 8, D), F32), V((dp_count, 8, MB), F32),
        V((total_rows, D), BF), V((room, D), BF),
        DMA((11,)), DMA((5, TP)), DMA((5, TP)), DMA((6, 5, chunks)), DMA((6, TP, chunks)), DMA((2, 3)), DMA((2, 3)),
        DMA((3, 2, 6 + extra)), DMA((3, 2, 6 + extra)), DMA((2, dp_count)), DMA((2, dp_count)), DMA((4, 2)),
    ]
    d_tokens, d_time, d_text, grads, early, late = pl.pallas_call(
        functools.partial(layer_kernel, (dp_count, place, items)),
        out_shape=(
            jax.ShapeDtypeStruct((R, D), BF),
            jax.ShapeDtypeStruct((items, 1, D), F32),
            jax.ShapeDtypeStruct((TL, D), BF),
            jax.ShapeDtypeStruct((total_rows, D), BF),
            jax.ShapeDtypeStruct((dp_count, 8, D), F32),
            jax.ShapeDtypeStruct((dp_count, 8, MB), F32),
        ),
        in_specs=[hbm] * 11 + [vmem] * 6 + [smem],
        out_specs=(vmem, vmem, vmem, hbm, hbm, hbm),
        scratch_shapes=scratch,
        name="layer",
        compiler_params=pltpu.CompilerParams(
            collective_id=0, has_side_effects=True, vmem_limit_bytes=63 * 1024 * 1024
        ),
    )(
        tokens[0], out_grad[0], text, w_qkv.T, w_attn_out, w_cross_q.T, w_cross_kv, w_cross_out,
        w_up, w_down, w_mod, seg_ids, jnp.transpose(time_embed, (1, 0, 2)),
        b_attn_out, b_cross_out, b_up, b_mod, text_lengths,
    )

    f32 = lambda *shape: jax.ShapeDtypeStruct(shape, F32)
    d_tokens, d_time, d_text, g_qkv, g_attn, g_cq, g_ckv, g_co, g_up, g_down, g_mod, gb_attn, gb_cross, gb_up, gb_mod = pl.pallas_call(
        functools.partial(finish_kernel, place, items),
        out_shape=(
            jax.ShapeDtypeStruct((R, D), BF), f32(items, 1, D), jax.ShapeDtypeStruct((TL, D), BF),
            f32(3 * HW, D), f32(HW, D), f32(HW, D), f32(D, 2 * HW), f32(HW, D), f32(FF, D), f32(FF, D),
            f32(D, MB), f32(D), f32(D), f32(FF), f32(MB),
        ),
        in_specs=[hbm] * 6,
        out_specs=(hbm,) * 11 + (vmem,) * 4,
        scratch_shapes=[
            V((total_rows, D), BF), V((total_rows, D), F32), V((D, 2 * HW), F32), V((D, MB), F32),
            V((dp_count, 8, D), F32), V((dp_count, 8, MB), F32), DMA((9,)), DMA((11,)),
        ],
        name="finish",
        compiler_params=pltpu.CompilerParams(vmem_limit_bytes=63 * 1024 * 1024),
    )(grads, early, late, d_tokens, d_time, d_text)
    return (
        d_tokens[None],
        jnp.transpose(d_time, (1, 0, 2)),
        d_text.reshape(1, items, shard_txt, D),
        g_qkv.T,
        g_attn,
        gb_attn,
        g_cq.T,
        g_ckv,
        g_co,
        gb_cross,
        g_up,
        gb_up,
        g_down,
        g_mod,
        gb_mod,
    )


def solution(mesh):
    placed = (
        P("dp", "tp", None),
        P("dp", None),
        P("dp", None, None),
        P("dp", None, "tp", None),
        P("dp", None),
        P("dp", "tp", None),
        P(None, "tp"),
        P("tp", None),
        P(),
        P(None, "tp"),
        P(None, "tp"),
        P("tp", None),
        P(),
        P(None, "tp"),
        P("tp"),
        P("tp", None),
        P(None, "tp"),
        P("tp"),
    )
    return jax.shard_map(
        functools.partial(body, mesh.shape["dp"]),
        mesh=mesh,
        in_specs=placed,
        out_specs=(
            P("dp", "tp", None),
            P("dp", None, None),
            P("dp", None, "tp", None),
            P(None, "tp"),
            P("tp", None),
            P(),
            P(None, "tp"),
            P(None, "tp"),
            P("tp", None),
            P(),
            P(None, "tp"),
            P("tp"),
            P("tp", None),
            P(None, "tp"),
            P("tp"),
        ),
        check_vma=False,
    )
```

```python
import functools
import math

import jax
import jax.numpy as jnp
from jax import lax
from jax.experimental import pallas as pl
from jax.experimental.pallas import tpu as pltpu
from jax.sharding import PartitionSpec as P

DH = 64
TP = 4
MESH = pl.DeviceIdType.MESH
BF = jnp.bfloat16
F32 = jnp.float32
GELU_C = math.sqrt(2.0 / math.pi)


def dot_nn(left, right):
    return jnp.dot(left, right, preferred_element_type=F32)


def dot_tn(left, right):
    return lax.dot_general(left, right, (((0,), (0,)), ((), ())), preferred_element_type=F32)


def dot_nt(left, right):
    return lax.dot_general(left, right, (((1,), (1,)), ((), ())), preferred_element_type=F32)


def normalize(values):
    center = values - jnp.mean(values, axis=-1, keepdims=True)
    inverse = lax.rsqrt(jnp.mean(center * center, axis=-1, keepdims=True) + 1e-06)
    return center * inverse, inverse


def normalize_back(grad, normed, inverse):
    return inverse * (
        grad
        - jnp.mean(grad, axis=-1, keepdims=True)
        - normed * jnp.mean(grad * normed, axis=-1, keepdims=True)
    )


def bucket_rows(hidden, heads_width):
    sizes = [
        ("up", hidden),
        ("down", hidden),
        ("cross_out", heads_width),
        ("cross_q", heads_width),
        ("cross_kv", 2 * heads_width),
        ("attn_out", heads_width),
        ("qkv", 3 * heads_width),
    ]
    at, place = 0, {}
    for name, rows in sizes:
        place[name] = (at, rows)
        at += rows
    return place, at


def layer_kernel(
    dims,
    tok_h, og_h, text_h, wqkvT_h, wo_h, wcqT_h, wckv_h, wco_h, wup_h, wdn_h, wmod_h,
    seg_ref, time_ref, b_attn_out_ref, b_cross_out_ref, b_up_ref, b_mod_ref, tlen_ref,
    dtok_o, dtime_o, dtext_o, grads_o, early_o, late_o,
    tok, og, text, att, gc,
    wqkvT, wckv, wfull, wup, wdn, wmod,
    modbuf, mods, segrow, segcol, onehot, ktag,
    attn_in, na, qkvT, kvx, pself,
    stream_a, inv_c, cross_in, cqT, ckvT, kblk, vblk, pcross, catT, branch_own,
    mlp_in, nm_own, invm_own, act, slope, dpre, dbm, rs_send, rs_recv,
    gc_own, dcT, dcqT, dckvT, grad_own, dba, dOT, dqkvT,
    rs2_send, rs2_recv, dm, dmp, dmr, dsil, dsr, early, eall, lall,
    grads, rbuf,
    lsem, ssem, rsem, csem_s, csem_r, wsem_s, wsem_r, gsem_s, gsem_r, esem_s, esem_r, osem,
):
    dp_count, place, items = dims
    tp = lax.axis_index("tp")
    dp = lax.axis_index("dp")
    R = tok.shape[1]
    D = tok.shape[2]
    T = TP * R
    HW = att.shape[1]
    HL = HW // DH
    TK = TP * text.shape[1]
    TL = text.shape[1]
    HEADS = TP * HL
    MB = modbuf.shape[2]
    scale = 1.0 / math.sqrt(DH)
    sub = lax.rem(dp, 8)
    base8 = dp - sub
    core = lax.rem(sub, 2)
    chip = sub // 2

    def tp_peer(k):
        return {"tp": lax.rem(tp + k, TP)}

    def remote(src, dst, send, recv, peer):
        return pltpu.make_async_remote_copy(
            src_ref=src, dst_ref=dst, send_sem=send, recv_sem=recv, device_id=peer, device_id_type=MESH
        )

    def span(at, size, unit):
        return pl.ds(pl.multiple_of(at, unit), size)

    loads = [
        (wckv_h, wckv),
        (wo_h, wfull.at[0, 0]),
        (wcqT_h, wfull.at[0, 1]),
        (wco_h, wfull.at[0, 2]),
        (tok_h, tok.at[0]),
        (wmod_h, wmod),
        (wqkvT_h, wqkvT),
        (text_h, text.at[0]),
        (og_h, og.at[0]),
        (wup_h, wup),
        (wdn_h, wdn),
    ]
    local = [pltpu.make_async_copy(src, dst, lsem.at[i]) for i, (src, dst) in enumerate(loads)]
    for copy in local:
        copy.start()

    barrier = pltpu.get_barrier_semaphore()
    for k in range(1, TP):
        pl.semaphore_signal(barrier, inc=1, device_id=tp_peer(k), device_id_type=MESH)

    def greet(k, carry):
        pl.semaphore_signal(
            barrier, inc=1, device_id={"dp": lax.rem(dp + k, dp_count)}, device_id_type=MESH
        )
        return carry

    lax.fori_loop(1, dp_count, greet, 0)

    early[...] = jnp.zeros(early.shape, F32)
    for item in range(items):
        early[item : item + 1, :] = time_ref[item]
    time = early[...]
    sig = 1.0 / (1.0 + jnp.exp(-time))
    silu_low = (time * sig).astype(BF)
    early[...] = silu_low.astype(F32)
    local[5].wait()
    modbuf[tp] = dot_nn(silu_low, wmod[...]) + b_mod_ref[...].astype(F32).reshape(1, MB)
    local[0].wait()
    ident = (
        lax.broadcasted_iota(jnp.int32, (D, D), 0) == lax.broadcasted_iota(jnp.int32, (D, D), 1)
    ).astype(F32).astype(BF)
    wckvT = dot_tn(wckv[...], ident).astype(BF)
    wfull[0, 3] = wckvT[:HW]
    wfull[0, 4] = wckvT[HW:]
    for copy in local[1:5]:
        copy.wait()

    pl.semaphore_wait(barrier, TP - 1 + dp_count - 1)

    pending, chains = [], []
    inner = (tp > 0) & (tp < TP - 1)
    slot_a = jnp.where(tp == 3, 3, 1)
    slot_b = jnp.where((tp == 0) | (tp == 3), 2, 3)
    slot_c = jnp.where(tp == 0, 3, jnp.where(tp == 3, 1, 2))
    right, left = {"tp": lax.rem(tp + 1, TP)}, {"tp": lax.rem(tp + TP - 1, TP)}
    onward = {"tp": jnp.where(tp == 1, 0, TP - 1)}
    onward_slot = jnp.where(tp == 1, 3, 1)

    class Chain:
        def __init__(self, index, view):
            self.index, self.view, self.started = index, view, []
            chains.append(self)

        def copy(self, src, dst, send, chunk, peer):
            return remote(
                self.view(src, chunk), self.view(dst, chunk),
                csem_s.at[self.index, send, chunk], csem_r.at[self.index, dst, chunk], peer,
            )

        def start(self, chunk):
            self.started.append(chunk)

            @pl.when(tp < TP - 1)
            def _():
                self.copy(0, 3, 0, chunk, right).start()

            @pl.when(tp > 0)
            def _():
                self.copy(0, 1, 1, chunk, left).start()

        def step(self, which, chunk):
            slot = (slot_a, slot_b, slot_c)[which]
            self.copy(slot, slot, 2 + which, chunk, right).wait_recv()

            @pl.when(inner)
            def _():
                if which == 0:
                    self.copy(slot, 2, 2, chunk, left).start()
                elif which == 1:
                    self.copy(slot, 2, 3, chunk, right).start()
                else:
                    self.copy(slot, onward_slot, 4, chunk, onward).start()

        def finish(self):
            for chunk in self.started:

                @pl.when(tp < TP - 1)
                def _():
                    self.copy(0, 3, 0, chunk, right).wait_send()

                @pl.when(tp > 0)
                def _():
                    self.copy(0, 1, 1, chunk, left).wait_send()

                @pl.when(inner)
                def _():
                    self.copy(slot_a, 2, 2, chunk, left).wait_send()
                    self.copy(slot_b, 2, 3, chunk, right).wait_send()
                    self.copy(slot_c, onward_slot, 4, chunk, onward).wait_send()

    half = R // 2
    tok_chain = Chain(0, lambda slot, c: tok.at[slot, c * half : (c + 1) * half])
    text_chain = Chain(1, lambda slot, c: text.at[slot])
    WR, WC = HW // 4, D // 2
    wcol = pl.multiple_of(core * WC, 128)
    mats = (3, 4, 0, 1, 2)
    swapped = lax.rem(chip, 2) * 2 + chip // 2
    places = (chip, swapped, chip, swapped, chip)
    w_chain = Chain(2, lambda slot, c: wfull.at[slot, mats[c], span(places[c] * WR, WR, 16), pl.ds(wcol, WC)])
    att_chain = Chain(3, lambda slot, c: att.at[slot, c * DH : (c + 1) * DH])
    og_chain = Chain(4, lambda slot, c: og.at[slot, c * half : (c + 1) * half])
    gc_chain = Chain(5, lambda slot, c: gc.at[slot, c * half : (c + 1) * half])

    class Plane:
        def __init__(self, index, bits):
            self.index, self.bits, self.open = index, bits, None

        def send(self, step, rows, bit):
            at = wfull.at[1:TP, mats[self.index], rows, pl.ds(wcol, WC)]
            copy = remote(
                at, at, wsem_s.at[self.index, step], wsem_r.at[self.index, step],
                {"dp": base8 + jnp.bitwise_xor(sub, bit)},
            )
            copy.start()
            pending.append(copy)
            self.open = copy

        def step(self, step):
            if step:
                self.open.wait_recv()
            place = places[self.index]
            if step == 0:
                self.send(0, span(place * WR, WR, 16), self.bits[0])
            elif step == 1:
                self.send(1, span(place // 2 * (2 * WR), 2 * WR, 16), self.bits[1])
            elif step == 2:
                self.send(2, slice(0, HW), 1)

    planes = [Plane(i, (4, 2) if i % 2 else (2, 4)) for i in range(5)]

    def direct(tag, src_of, dst_of):
        copies = []
        for k in range(1, TP):
            copy = remote(src_of(k), dst_of(k), ssem.at[tag, k], rsem.at[tag, TP - k], tp_peer(k))
            copy.start()
            copies.append(copy)
        pending.extend(copies)
        return copies

    def arrived(copies, slot):
        copies[TP - 1 - slot].wait_recv()

    w_chain.start(0)
    w_chain.start(1)
    tok_chain.start(0)
    tok_chain.start(1)
    mod_copies = direct(0, lambda k: modbuf.at[tp, 0:items], lambda k: modbuf.at[tp, 0:items])

    eye = lax.broadcasted_iota(jnp.int32, (R, R), 0) == lax.broadcasted_iota(jnp.int32, (R, R), 1)
    for slot in range(TP):
        owner = lax.rem(tp + slot, TP)
        row = seg_ref[:, pl.ds(pl.multiple_of(owner * R, R), R)].astype(F32)
        segrow[:, slot * R : (slot + 1) * R] = row
        col = jnp.sum(jnp.where(eye, row, 0.0), axis=1, keepdims=True)
        segcol[slot * R : (slot + 1) * R, :] = col
    kinds = lax.broadcasted_iota(jnp.int32, (16, T), 0)
    matches = (segrow[...] == kinds.astype(F32)) & (kinds < items)
    onehot[...] = jnp.where(matches | (kinds == items), 1.0, 0.0).astype(BF)
    key_at = lax.broadcasted_iota(jnp.int32, (TK, 1), 0)
    key_slot = key_at // TL
    key_item = lax.rem(key_at, TL) // (TL // items)
    key_pos = lax.rem(key_slot + tp, TP) * (TL // items) + lax.rem(key_at, TL // items)
    tag = jnp.full((TK, 1), -1.0, F32)
    for item in range(items):
        inside = (key_item == item) & (key_pos < tlen_ref[0, item])
        tag = jnp.where(inside, float(item), tag)
    ktag[...] = tag

    for k in range(1, TP):
        arrived(mod_copies, k)
    for j in range(6):
        lo, hi = j * D, (j + 1) * D
        at = lo
        while at < hi:
            block = at // MB
            end = min(hi, (block + 1) * MB)
            mods[j, 0:items, at - lo : end - lo] = modbuf[block, 0:items, at - block * MB : end - block * MB]
            at = end

    def per_frame(j, rows):
        col = segcol[rows, :]
        out = mods[j, items - 1 : items, :]
        for item in range(items - 2, -1, -1):
            out = jnp.where(col == float(item), mods[j, item : item + 1, :], out)
        return out

    def item_sums(rows, values):
        return dot_nn(onehot[:, rows], values.astype(BF))

    own, every = slice(0, R), slice(0, T)
    local[6].wait()

    def project(slot):
        rows = span(slot * R, R, R)
        normed, inverse = normalize(tok[slot].astype(F32))
        na[rows, :] = normed.astype(BF)
        x = (normed * (1.0 + per_frame(1, rows)) + per_frame(0, rows)).astype(BF)
        attn_in[rows, :] = x
        qkvT[:, rows] = dot_nt(wqkvT[...], x).astype(BF)

    def w_step(which, *chunks):
        for chunk in chunks:
            w_chain.step(which, chunk)
            if which == 2:
                planes[chunk].step(0)

    project(0)
    w_step(0, 0, 1)
    tok_chain.step(0, 0)
    tok_chain.step(0, 1)
    for chunk in (2, 3, 4):
        w_chain.start(chunk)
    local[7].wait()
    text_chain.start(0)
    w_step(1, 0, 1)
    tok_chain.step(1, 0)
    tok_chain.step(1, 1)
    w_step(2, 0, 1)
    project(slot_a)
    w_step(0, 2, 3, 4)
    planes[0].step(1)
    planes[1].step(1)
    project(slot_b)
    tok_chain.step(2, 0)
    tok_chain.step(2, 1)
    text_chain.step(0, 0)
    w_step(1, 2, 3, 4)
    project(slot_c)
    planes[0].step(2)
    planes[1].step(2)

    for h in range(HL):
        q0 = h * 3 * DH
        kvx[2 * h] = (qkvT[q0 + DH : q0 + 2 * DH, :].astype(F32).T * scale).astype(BF)
        kvx[2 * h + 1] = qkvT[q0 + 2 * DH : q0 + 3 * DH, :].astype(F32).T.astype(BF)
        scores = dot_nn(kvx[2 * h], qkvT[q0 : q0 + DH, :])
        scores = jnp.where(segcol[...] == segrow[...], scores, -1000000000.0)
        peak = jnp.max(scores, axis=0, keepdims=True)
        exponent = jnp.exp(scores - peak)
        probs = exponent * (1.0 / jnp.sum(exponent, axis=0, keepdims=True))
        pself[h] = probs
        att[0, h * DH : (h + 1) * DH, :] = dot_nn(qkvT[q0 + 2 * DH : q0 + 3 * DH, :], probs.astype(BF)).astype(BF)

    for h in range(HL):
        att_chain.start(h)
    w_step(2, 2, 3, 4)
    text_chain.step(1, 0)
    text_chain.step(2, 0)
    planes[0].step(3)
    planes[1].step(3)
    planes[2].step(1)
    planes[3].step(1)

    def full(i):
        return wfull[:, i].reshape(TP * HW, D)

    text_flat = text[...].reshape(TK, D)
    for s in range(TP):
        for part in range(2):
            ckvT[(2 * s + part) * HW : (2 * s + part + 1) * HW, :] = dot_nt(wfull[s, 3 + part], text_flat).astype(BF)
    quad = 4 * DH
    lane_head = lax.broadcasted_iota(jnp.int32, (TK, quad), 1) // DH
    for g in range(HEADS // 4):
        heads_at = [(4 * g + j) * 2 * DH for j in range(4)]
        for blocks, offset, factor in ((kblk, 0, scale), (vblk, DH, 1.0)):
            turned = jnp.concatenate(
                [ckvT[at + offset : at + offset + DH, :] for at in heads_at], axis=0
            ).astype(F32).T * factor
            for j in range(4):
                blocks[g, j * TK : (j + 1) * TK, :] = jnp.where(lane_head == j, turned, 0.0).astype(BF)
    planes[4].step(1)
    for h in range(HL):
        att_chain.step(0, h)
    planes[2].step(2)
    planes[3].step(2)
    for h in range(HL):
        att_chain.step(1, h)
    local[8].wait()
    og_chain.start(0)
    og_chain.start(1)
    planes[4].step(2)
    for h in range(HL):
        att_chain.step(2, h)
    for plane in planes[2:]:
        plane.step(3)
    og_chain.step(0, 0)
    og_chain.step(0, 1)

    b_attn_out = b_attn_out_ref[...].astype(F32).reshape(1, D)
    b_cross_out = b_cross_out_ref[...].astype(F32).reshape(1, D)
    b_up = b_up_ref[...].astype(F32).reshape(1, wup.shape[1])

    gathered = jnp.concatenate(
        [
            jnp.concatenate([att[k, :, (b - k) % TP * R : ((b - k) % TP + 1) * R] for b in range(TP)], axis=1)
            for k in range(TP)
        ],
        axis=0,
    )
    stream_a[...] = dot_tn(gathered, full(0)) + b_attn_out
    branch_own[...] = stream_a[own, :]
    stream_a[...] = tok[...].reshape(T, D).astype(F32) + per_frame(2, every) * stream_a[...]
    normed, inverse = normalize(stream_a[...])
    inv_c[...] = inverse
    cross_in[...] = normed.astype(BF)
    cqT[...] = dot_nt(full(1), cross_in[...]).astype(BF)
    allowed = ktag[...] == segrow[...]
    og_chain.step(1, 0)
    og_chain.step(1, 1)

    def cross_forward(g, carry):
        scores_all = dot_nn(kblk[g], cqT[span(g * quad, quad, quad), :])
        for j in range(4):
            h = 4 * g + j
            scores = jnp.where(allowed, scores_all[j * TK : (j + 1) * TK], -1000000000.0)
            peak = jnp.max(scores, axis=0, keepdims=True)
            exponent = jnp.exp(scores - peak)
            probs = exponent * (1.0 / jnp.sum(exponent, axis=0, keepdims=True))
            pcross[h] = probs
            vT = ckvT[span(h * 2 * DH + DH, DH, DH), :]
            catT[span(h * DH, DH, DH), :] = dot_nn(vT, probs.astype(BF)).astype(BF)
        return carry

    lax.fori_loop(0, HEADS // 4, cross_forward, 0)
    og_chain.step(2, 0)
    og_chain.step(2, 1)
    normed, inverse = normalize(stream_a[...] + dot_tn(catT[...], full(2)) + b_cross_out)
    nm_own[...] = normed[:R]
    invm_own[...] = inverse[:R]
    mlp_in[...] = (normed * (1.0 + per_frame(4, every)) + per_frame(3, every)).astype(BF)

    local[9].wait()
    local[10].wait()
    pre = dot_nn(mlp_in[...], wup[...]) + b_up
    square = pre * pre
    bend = jnp.tanh(GELU_C * pre * (1.0 + 0.044715 * square))
    act[...] = (0.5 * pre * (1.0 + bend)).astype(BF)
    slope[...] = 0.5 * (1.0 + bend) + 0.5 * pre * (1.0 - bend * bend) * (
        GELU_C * (1.0 + 3.0 * 0.044715 * square)
    )
    dbm[...] = (og[...].reshape(T, D).astype(F32) * per_frame(5, every)).astype(BF)
    dpre[...] = (dot_nt(dbm[...], wdn[...]) * slope[...]).astype(BF)
    rs_send[...] = dot_nt(dpre[...], wup[...]).astype(BF).reshape(TP, R, D)

    def to_owners(source, target, tag, rows):
        copies = {}
        for b in (2, 1, 3):
            copies[b] = remote(
                source.at[b, rows], target.at[TP - 1 - b, rows], ssem.at[tag, b], rsem.at[tag, TP - b], tp_peer(b)
            )
            copies[b].start()
        return copies

    halves = (slice(0, half), slice(half, R))
    rs_first = to_owners(rs_send, rs_recv, 1, halves[0])
    early[3:4, :] = dot_nn(onehot[...], dpre[...])[items : items + 1, :]

    bits = []
    step = 8
    while step < dp_count:
        bits.append(step)
        step *= 2

    class Reduce:
        def __init__(self, index, start, rows, room):
            self.parts = []
            half = rows // 2
            for part in range(2):
                chain = (1, 2, 4) if part == 0 else (1, 4, 2)
                self.parts.append((start + part * half, half, chain, part * half))
            self.index, self.room = index, room
            self.open, self.own = [], []

        def sem(self, part, step):
            return gsem_s.at[self.index, part, step], gsem_r.at[self.index, part, step]

        def launch(self, src, dst, part, step, bit):
            send, recv = self.sem(part, step)
            copy = remote(src, dst, send, recv, {"dp": jnp.bitwise_xor(dp, bit)})
            copy.start()
            pending.append(copy)
            return copy

        def bounds(self, part, level):
            start, rows, chain, _ = self.parts[part]
            at, size = start, rows
            for bit in chain[:level]:
                size //= 2
                at = at + jnp.bitwise_and(dp // bit, 1) * size
            return at, size

        def scatter_start(self, level):
            self.open = []
            for part in range(2):
                at, size = self.bounds(part, level)
                bit = self.parts[part][2][level]
                half = size // 2
                mine = jnp.bitwise_and(dp // bit, 1)
                other = pl.multiple_of(at + (1 - mine) * half, 16)
                rows = self.parts[part][1]
                room = self.room + 2 * (rows - (rows >> level)) + part * half
                copy = self.launch(
                    grads.at[pl.ds(other, half)], rbuf.at[room : room + half], part, level, bit
                )
                self.open.append((copy, room, half))

        def scatter_end(self, level):
            for part in range(2):
                copy, room, half = self.open[part]
                copy.wait_recv()
                at, size = self.bounds(part, level + 1)
                mine = pl.ds(pl.multiple_of(at, 16), half)
                grads[mine, :] = (grads[mine, :].astype(F32) + rbuf[room : room + half, :].astype(F32)).astype(BF)

        def widen(self):
            for i, bit in enumerate(bits):
                for part in range(2):
                    at, size = self.bounds(part, 3)
                    rows = self.parts[part][1]
                    mine = pl.ds(pl.multiple_of(at, 16), size)
                    room = self.room + 2 * (rows - rows // 8) + (2 * i + part) * size
                    copy = self.launch(grads.at[mine], rbuf.at[room : room + size], part, 6 + i, bit)
                    copy.wait_recv()
                    grads[mine, :] = (
                        grads[mine, :].astype(F32) + rbuf[room : room + size, :].astype(F32)
                    ).astype(BF)

        def gather_start(self, level):
            self.open = []
            source = grads if level == 2 else grads_o
            if level == 1:
                for copy in self.own:
                    copy.wait()
            for part in range(2):
                at, size = self.bounds(part, level + 1)
                bit = self.parts[part][2][level]
                mine = pl.ds(pl.multiple_of(at, 16), size)
                self.open.append(
                    self.launch(source.at[mine], grads_o.at[mine], part, 3 + (2 - level), bit)
                )
                if level == 2:
                    copy = pltpu.make_async_copy(grads.at[mine], grads_o.at[mine], osem.at[self.index, part])
                    copy.start()
                    self.own.append(copy)

        def gather_end(self):
            for copy in self.open:
                copy.wait_recv()

    mid0 = place["cross_out"][0]
    mid1 = place["attn_out"][0]
    total_rows = grads.shape[0]
    extra = 2 * len(bits)
    rooms, at = [], 0
    for rows in (mid0, mid1 - mid0, total_rows - mid1):
        rooms.append(at)
        at += rows - rows // 8 + extra * (rows // 16)
    reduce_mlp = Reduce(0, 0, mid0, rooms[0])
    reduce_cross = Reduce(1, mid0, mid1 - mid0, rooms[1])
    reduce_self = Reduce(2, mid1, total_rows - mid1, rooms[2])

    def put(name, values):
        at, rows = place[name]
        grads[at : at + rows, :] = values.astype(BF)

    put("up", dot_tn(mlp_in[...], dpre[...]))
    put("down", dot_tn(act[...], dbm[...]))
    reduce_mlp.scatter_start(0)
    dm[5] = item_sums(every, og[...].reshape(T, D).astype(F32) * dot_nn(act[...], wdn[...]))

    reduce_mlp.scatter_end(0)
    reduce_mlp.scatter_start(1)
    for copy in rs_first.values():
        copy.wait_send()
    rs_second = to_owners(rs_send, rs_recv, 5, halves[1])
    pending.extend(rs_second.values())

    def stream_grad(chunk, copies):
        rows = halves[chunk]
        d_mlp = rs_send[0, rows].astype(F32)
        for k in (1, 3, 2):
            copies[TP - k].wait_recv()
            d_mlp = d_mlp + rs_recv[k - 1, rows].astype(F32)
        grad_c = og[0, rows].astype(F32) + normalize_back(
            d_mlp * (1.0 + per_frame(4, rows)), nm_own[rows, :], invm_own[rows, :]
        )
        gc_own[rows, :] = grad_c
        gc[0, rows] = grad_c.astype(BF)
        gc_chain.start(chunk)
        return d_mlp

    first = stream_grad(0, rs_first)
    reduce_mlp.scatter_end(1)
    reduce_mlp.scatter_start(2)
    gc_chain.step(0, 0)
    second = stream_grad(1, rs_second)
    gc_chain.step(1, 0)
    reduce_mlp.scatter_end(2)
    reduce_mlp.widen()
    reduce_mlp.gather_start(2)
    d_mlp = jnp.concatenate([first, second], axis=0)
    dm[3] = item_sums(own, d_mlp)
    dm[4] = item_sums(own, d_mlp * nm_own[...])
    gc_chain.step(2, 0)

    gc_chain.step(0, 1)
    gc_chain.step(1, 1)
    reduce_mlp.gather_end()
    reduce_mlp.gather_start(1)
    gc_chain.step(2, 1)
    gc_flat = gc[...].reshape(T, D)
    dcT[...] = dot_nt(full(2), gc_flat).astype(BF)

    def cross_backward(g, carry):
        d_probs_all = dot_nn(vblk[g], dcT[span(g * quad, quad, quad), :])
        for j in range(4):
            h = 4 * g + j
            hr = span(h * DH, DH, DH)
            kr, vr = span(h * 2 * DH, DH, DH), span(h * 2 * DH + DH, DH, DH)
            probs = pcross[h]
            d_probs = d_probs_all[j * TK : (j + 1) * TK]
            d_scores = (probs * (d_probs - jnp.sum(probs * d_probs, axis=0, keepdims=True))).astype(BF)
            dcqT[hr, :] = (dot_nn(ckvT[kr, :], d_scores) * scale).astype(BF)
            dckvT[kr, :] = (dot_nt(cqT[hr, :], d_scores) * scale).astype(BF)
            dckvT[vr, :] = dot_nt(dcT[hr, :], probs.astype(BF)).astype(BF)
        return carry

    lax.fori_loop(0, HEADS // 4, cross_backward, 0)
    d_cross = dot_tn(dcqT[...], full(1))
    back = normalize_back(d_cross, cross_in[...].astype(F32), inv_c[...])
    grad = gc_own[...] + back[:R]
    grad_own[...] = grad
    gate = per_frame(2, every)
    dba[own, :] = (grad * gate[:R]).astype(BF)
    rest = slice(R, T)
    dba[rest, :] = ((gc_flat[R:].astype(F32) + back[R:]) * gate[R:]).astype(BF)
    dOT[...] = dot_nt(wfull[0, 0], dba[...]).astype(BF)

    put("cross_out", dot_nn(catT[0:HW, :], gc_flat))
    put("cross_q", dot_nn(dcqT[0:HW, :], cross_in[...]))
    put("cross_kv", dot_nn(dckvT[0 : 2 * HW, :], text_flat))
    put("attn_out", dot_nn(att[0], dba[...]))
    reduce_cross.scatter_start(0)
    early[4:5, :] = dot_nn(onehot[...], gc_flat)[items : items + 1, :]
    early[5:6, :] = dot_nn(onehot[...], dba[...])[items : items + 1, :]
    eall[dp] = early[...]

    def dp_send(src, dst, index):
        def one(k, carry):
            peer = lax.rem(dp + k, dp_count)
            remote(
                src, dst, esem_s.at[index, k], esem_r.at[index, dp_count - k], {"dp": peer}
            ).start()
            return carry

        lax.fori_loop(1, dp_count, one, 0)

    def dp_wait(src, dst, index):
        def one(k, carry):
            remote(
                src, dst, esem_s.at[index, k], esem_r.at[index, k], {"dp": lax.rem(dp + k, dp_count)}
            ).wait()
            return carry

        lax.fori_loop(1, dp_count, one, 0)

    dp_send(eall.at[dp], eall.at[dp], 0)

    for h in range(HL):
        q0 = h * 3 * DH
        hr = slice(h * DH, (h + 1) * DH)
        probs = pself[h]
        d_probs = dot_nn(kvx[2 * h + 1], dOT[hr, :])
        d_scores = (probs * (d_probs - jnp.sum(probs * d_probs, axis=0, keepdims=True))).astype(BF)
        dqkvT[q0 : q0 + DH, :] = (dot_nn(qkvT[q0 + DH : q0 + 2 * DH, :], d_scores) * scale).astype(BF)
        dqkvT[q0 + DH : q0 + 2 * DH, :] = (dot_nt(qkvT[q0 : q0 + DH, :], d_scores) * scale).astype(BF)
        dqkvT[q0 + 2 * DH : q0 + 3 * DH, :] = dot_nt(dOT[hr, :], probs.astype(BF)).astype(BF)

    put("qkv", dot_nn(dqkvT[...], attn_in[...]))
    reduce_self.scatter_start(0)
    reduce_cross.scatter_end(0)
    reduce_cross.scatter_start(1)

    part = dot_tn(dqkvT[...], wqkvT[...])
    rs2_send[...] = part.astype(BF).reshape(TP, R, D)
    input_grad = rs2_send[...].reshape(T, D)
    dm[0] = dot_nn(onehot[...], input_grad)
    dm[1] = item_sums(every, input_grad.astype(F32) * na[...].astype(F32))
    dm[2] = item_sums(own, grad_own[...] * branch_own[...])

    for j in range(6):
        lo, hi = j * D, (j + 1) * D
        at = lo
        while at < hi:
            block = at // MB
            end = min(hi, (block + 1) * MB)
            dmp[block, :, at - block * MB : end - block * MB] = dm[j, 0:8, at - lo : end - lo]
            at = end
    dm_copies = direct(
        3, lambda k: dmp.at[lax.rem(tp + k, TP), 0:items], lambda k: dmr.at[TP - 1 - k, 0:items]
    )
    rs2_copies = to_owners(rs2_send, rs2_recv, 2, own)
    pending.extend(rs2_copies.values())
    reduce_self.scatter_end(0)
    reduce_self.scatter_start(1)
    reduce_mlp.gather_end()
    reduce_mlp.gather_start(0)

    dtext_o[...] = dot_tn(dckvT[:, 0:TL], wfull[:, 3:5].reshape(TP * 2 * HW, D)).astype(BF)
    reduce_cross.scatter_end(1)
    reduce_cross.scatter_start(2)

    d_mod = dmp[tp, 0:items]
    for k in range(1, TP):
        arrived(dm_copies, k)
        d_mod = d_mod + dmr[k - 1, 0:items]
    low = d_mod.astype(BF)
    lall[dp, 0:items] = low.astype(F32)
    dsil[0:items, :] = dot_nt(low, wmod[...])
    ds_copies = direct(4, lambda k: dsil.at[0:items], lambda k: dsr.at[TP - 1 - k, 0:items])

    reduce_self.scatter_end(1)
    reduce_self.scatter_start(2)
    dp_send(lall.at[dp, 0:items], lall.at[dp, 0:items], 1)
    reduce_cross.scatter_end(2)
    reduce_cross.widen()
    reduce_cross.gather_start(2)
    reduce_self.scatter_end(2)
    reduce_self.widen()
    reduce_self.gather_start(2)
    reduce_mlp.gather_end()
    reduce_cross.gather_end()
    reduce_cross.gather_start(1)
    reduce_self.gather_end()
    reduce_self.gather_start(1)

    d_in = rs2_send[0].astype(F32)
    for k in (1, 3, 2):
        rs2_copies[TP - k].wait_recv()
        d_in = d_in + rs2_recv[k - 1].astype(F32)
    normed, inverse = normalize(tok[0].astype(F32))
    dtok_o[...] = (
        grad_own[...] + normalize_back(d_in * (1.0 + per_frame(1, own)), normed, inverse)
    ).astype(BF)
    reduce_cross.gather_end()
    reduce_cross.gather_start(0)

    d_silu = dsil[0:items, :]
    for k in range(1, TP):
        arrived(ds_copies, k)
        d_silu = d_silu + dsr[k - 1, 0:items]
    for item in range(items):
        value = time_ref[item]
        gate = 1.0 / (1.0 + jnp.exp(-value))
        dtime_o[item] = d_silu[item : item + 1, :] * (gate * (1.0 + value * (1.0 - gate)))
    dp_wait(eall.at[dp], eall.at[dp], 0)
    dp_wait(lall.at[dp, 0:items], lall.at[dp, 0:items], 1)
    out_copies = [
        pltpu.make_async_copy(eall, early_o, osem.at[3, 0]),
        pltpu.make_async_copy(lall, late_o, osem.at[3, 1]),
    ]
    for copy in out_copies:
        copy.start()
    reduce_self.gather_end()
    reduce_self.gather_start(0)
    for chain in chains:
        chain.finish()
    reduce_cross.gather_end()
    reduce_self.gather_end()
    for copy in pending:
        copy.wait_send()
    for copy in out_copies:
        copy.wait()


def finish_kernel(
    place, items, grads_h, early_h, late_h, dtok_h, dtime_h, dtext_h,
    dtok_o, dtime_o, dtext_o, qkv_o, attn_out_o, cross_q_o, cross_kv_o, cross_out_o, up_o, down_o, mod_o,
    gb_attn_o, gb_cross_o, gb_up_o, gb_mod_o,
    low, full_v, kv_v, mod_v, early_v, late_v, isem, osem, ssem,
):
    names = ("up", "down", "qkv", "cross_kv", "attn_out", "cross_out", "cross_q")
    outs = {
        "up": up_o, "down": down_o, "qkv": qkv_o, "attn_out": attn_out_o, "cross_out": cross_out_o,
        "cross_q": cross_q_o, "cross_kv": cross_kv_o,
    }
    unit = 384
    chunks = []
    for name in names:
        at, rows = place[name]
        step = rows if name == "cross_kv" else math.gcd(rows, unit)
        chunks += [(name, at + i, step, i) for i in range(0, rows, step)]
    small = [
        pltpu.make_async_copy(early_h, early_v, ssem.at[0]),
        pltpu.make_async_copy(late_h, late_v, ssem.at[1]),
    ]
    stores = [
        pltpu.make_async_copy(dtok_h, dtok_o, ssem.at[2]),
        pltpu.make_async_copy(dtime_h, dtime_o, ssem.at[3]),
        pltpu.make_async_copy(dtext_h, dtext_o, ssem.at[4]),
    ]
    loads = [
        pltpu.make_async_copy(grads_h.at[at : at + step], low.at[at : at + step], isem.at[i])
        for i, (_, at, step, _) in enumerate(chunks)
    ]
    for copy in small + stores + loads:
        copy.start()

    def store(src, dst, sem):
        copy = pltpu.make_async_copy(src, dst, sem)
        copy.start()
        stores.append(copy)

    for i, (name, at, step, offset) in enumerate(chunks):
        loads[i].wait()
        if name == "cross_kv":
            ident = (
                lax.broadcasted_iota(jnp.int32, (step, step), 0)
                == lax.broadcasted_iota(jnp.int32, (step, step), 1)
            ).astype(F32).astype(BF)
            kv_v[...] = dot_tn(low[at : at + step, :], ident)
            store(kv_v, outs[name], osem.at[i])
        else:
            full_v[at : at + step, :] = low[at : at + step, :].astype(F32)
            store(full_v.at[at : at + step], outs[name].at[offset : offset + step], osem.at[i])
    for copy in small:
        copy.wait()
    dp_count, slots, D = early_v.shape
    MB = late_v.shape[2]
    keep = lax.rem(lax.broadcasted_iota(jnp.int32, (dp_count * slots, MB), 0), slots) < items
    late = jnp.where(keep, late_v[...].reshape(dp_count * slots, MB), 0.0)
    early = early_v[...]
    left, right = early.reshape(dp_count * slots, D).astype(BF), late.astype(BF)
    parts = 3
    rows = D // parts
    for i in range(parts):
        piece = slice(i * rows, (i + 1) * rows)
        mod_v[piece, :] = dot_tn(left[:, piece], right)
        store(mod_v.at[piece], mod_o.at[piece], ssem.at[5 + i])
    gb_mod_o[...] = jnp.sum(late, axis=0)
    sums = jnp.sum(early, axis=0)
    gb_up_o[...] = sums[3]
    gb_cross_o[...] = sums[4]
    gb_attn_o[...] = sums[5]
    for copy in stores:
        copy.wait()


def body(
    dp_count,
    tokens,
    seg_ids,
    time_embed,
    text_states,
    text_lengths,
    out_grad,
    w_qkv,
    w_attn_out,
    b_attn_out,
    w_cross_q,
    w_cross_kv,
    w_cross_out,
    b_cross_out,
    w_up,
    b_up,
    w_down,
    w_mod,
    b_mod,
):
    _, R, D = tokens.shape
    T = R * TP
    items = time_embed.shape[1]
    shard_txt = text_states.shape[2]
    TL = items * shard_txt
    TK = TP * TL
    HW = w_cross_q.shape[1]
    HL = HW // DH
    HEADS = TP * HL
    FF = w_up.shape[1]
    MB = w_mod.shape[1]
    place, total_rows = bucket_rows(FF, HW)
    text = text_states[0].reshape(TL, D)

    extra = 0
    step = 8
    while step < dp_count:
        extra += 1
        step *= 2
    room = total_rows - total_rows // 8 + 2 * extra * (total_rows // 16)

    hbm = pl.BlockSpec(memory_space=pl.ANY)
    vmem = pl.BlockSpec(memory_space=pltpu.VMEM)
    smem = pl.BlockSpec(memory_space=pltpu.SMEM)
    V = pltpu.VMEM
    DMA = pltpu.SemaphoreType.DMA
    chunks = max(HL, 5)
    scratch = [
        V((TP, R, D), BF), V((TP, R, D), BF), V((TP, TL, D), BF), V((TP, HW, T), BF), V((TP, R, D), BF),
        V((3 * HW, D), BF), V((D, 2 * HW), BF), V((TP, 5, HW, D), BF),
        V((D, FF), BF), V((FF, D), BF), V((D, MB), BF),
        V((TP, 8, MB), F32), V((6, 8, D), F32), V((1, T), F32), V((T, 1), F32), V((16, T), BF), V((TK, 1), F32),
        V((T, D), BF), V((T, D), BF), V((3 * HW, T), BF), V((2 * HL, T, DH), BF), V((HL, T, T), F32),
        V((T, D), F32), V((T, 1), F32), V((T, D), BF), V((TP * HW, T), BF), V((TP * 2 * HW, TK), BF),
        V((HEADS // 4, 4 * TK, 4 * DH), BF), V((HEADS // 4, 4 * TK, 4 * DH), BF), V((HEADS, TK, T), F32), V((TP * HW, T), BF), V((R, D), F32),
        V((T, D), BF), V((R, D), F32), V((R, 1), F32), V((T, FF), BF), V((T, FF), F32), V((T, FF), BF), V((T, D), BF),
        V((TP, R, D), BF), V((TP - 1, R, D), BF),
        V((R, D), F32), V((TP * HW, T), BF), V((TP * HW, T), BF),
        V((TP * 2 * HW, TK), BF), V((R, D), F32), V((T, D), BF), V((HW, T), BF), V((3 * HW, T), BF),
        V((TP, R, D), BF), V((TP - 1, R, D), BF),
        V((6, 16, D), F32), V((TP, 8, MB), F32), V((TP - 1, 8, MB), F32), V((8, D), F32), V((TP - 1, 8, D), F32),
        V((8, D), F32), V((dp_count, 8, D), F32), V((dp_count, 8, MB), F32),
        V((total_rows, D), BF), V((room, D), BF),
        DMA((11,)), DMA((6, TP)), DMA((6, TP)), DMA((6, 5, chunks)), DMA((6, TP, chunks)), DMA((5, 3)), DMA((5, 3)),
        DMA((3, 2, 6 + extra)), DMA((3, 2, 6 + extra)), DMA((2, dp_count)), DMA((2, dp_count)), DMA((4, 2)),
    ]
    d_tokens, d_time, d_text, grads, early, late = pl.pallas_call(
        functools.partial(layer_kernel, (dp_count, place, items)),
        out_shape=(
            jax.ShapeDtypeStruct((R, D), BF),
            jax.ShapeDtypeStruct((items, 1, D), F32),
            jax.ShapeDtypeStruct((TL, D), BF),
            jax.ShapeDtypeStruct((total_rows, D), BF),
            jax.ShapeDtypeStruct((dp_count, 8, D), F32),
            jax.ShapeDtypeStruct((dp_count, 8, MB), F32),
        ),
        in_specs=[hbm] * 11 + [vmem] * 6 + [smem],
        out_specs=(vmem, vmem, vmem, hbm, hbm, hbm),
        scratch_shapes=scratch,
        name="layer",
        compiler_params=pltpu.CompilerParams(
            collective_id=0, has_side_effects=True, vmem_limit_bytes=63 * 1024 * 1024
        ),
    )(
        tokens[0], out_grad[0], text, w_qkv.T, w_attn_out, w_cross_q.T, w_cross_kv, w_cross_out,
        w_up, w_down, w_mod, seg_ids, jnp.transpose(time_embed, (1, 0, 2)),
        b_attn_out, b_cross_out, b_up, b_mod, text_lengths,
    )

    f32 = lambda *shape: jax.ShapeDtypeStruct(shape, F32)
    d_tokens, d_time, d_text, g_qkv, g_attn, g_cq, g_ckv, g_co, g_up, g_down, g_mod, gb_attn, gb_cross, gb_up, gb_mod = pl.pallas_call(
        functools.partial(finish_kernel, place, items),
        out_shape=(
            jax.ShapeDtypeStruct((R, D), BF), f32(items, 1, D), jax.ShapeDtypeStruct((TL, D), BF),
            f32(3 * HW, D), f32(HW, D), f32(HW, D), f32(D, 2 * HW), f32(HW, D), f32(FF, D), f32(FF, D),
            f32(D, MB), f32(D), f32(D), f32(FF), f32(MB),
        ),
        in_specs=[hbm] * 6,
        out_specs=(hbm,) * 11 + (vmem,) * 4,
        scratch_shapes=[
            V((total_rows, D), BF), V((total_rows, D), F32), V((D, 2 * HW), F32), V((D, MB), F32),
            V((dp_count, 8, D), F32), V((dp_count, 8, MB), F32), DMA((16,)), DMA((16,)), DMA((8,)),
        ],
        name="finish",
        compiler_params=pltpu.CompilerParams(vmem_limit_bytes=63 * 1024 * 1024),
    )(grads, early, late, d_tokens, d_time, d_text)
    return (
        d_tokens[None],
        jnp.transpose(d_time, (1, 0, 2)),
        d_text.reshape(1, items, shard_txt, D),
        g_qkv.T,
        g_attn,
        gb_attn,
        g_cq.T,
        g_ckv,
        g_co,
        gb_cross,
        g_up,
        gb_up,
        g_down,
        g_mod,
        gb_mod,
    )


def solution(mesh):
    placed = (
        P("dp", "tp", None),
        P("dp", None),
        P("dp", None, None),
        P("dp", None, "tp", None),
        P("dp", None),
        P("dp", "tp", None),
        P(None, "tp"),
        P("tp", None),
        P(),
        P(None, "tp"),
        P(None, "tp"),
        P("tp", None),
        P(),
        P(None, "tp"),
        P("tp"),
        P("tp", None),
        P(None, "tp"),
        P("tp"),
    )
    return jax.shard_map(
        functools.partial(body, mesh.shape["dp"]),
        mesh=mesh,
        in_specs=placed,
        out_specs=(
            P("dp", "tp", None),
            P("dp", None, None),
            P("dp", None, "tp", None),
            P(None, "tp"),
            P("tp", None),
            P(),
            P(None, "tp"),
            P(None, "tp"),
            P("tp", None),
            P(),
            P(None, "tp"),
            P("tp"),
            P("tp", None),
            P(None, "tp"),
            P("tp"),
        ),
        check_vma=False,
    )
```

```python
import functools
import math

import jax
import jax.numpy as jnp
from jax import lax
from jax.experimental import pallas as pl
from jax.experimental.pallas import tpu as pltpu
from jax.sharding import PartitionSpec as P

DH = 64
TP = 4
MESH = pl.DeviceIdType.MESH
BF = jnp.bfloat16
F32 = jnp.float32
GELU_C = math.sqrt(2.0 / math.pi)


def dot_nn(left, right):
    return jnp.dot(left, right, preferred_element_type=F32)


def dot_tn(left, right):
    return lax.dot_general(left, right, (((0,), (0,)), ((), ())), preferred_element_type=F32)


def dot_nt(left, right):
    return lax.dot_general(left, right, (((1,), (1,)), ((), ())), preferred_element_type=F32)


def normalize(values):
    center = values - jnp.mean(values, axis=-1, keepdims=True)
    inverse = lax.rsqrt(jnp.mean(center * center, axis=-1, keepdims=True) + 1e-06)
    return center * inverse, inverse


def normalize_back(grad, normed, inverse):
    return inverse * (
        grad
        - jnp.mean(grad, axis=-1, keepdims=True)
        - normed * jnp.mean(grad * normed, axis=-1, keepdims=True)
    )


def bucket_rows(hidden, heads_width):
    sizes = [
        ("up", hidden),
        ("down", hidden),
        ("cross_out", heads_width),
        ("cross_q", heads_width),
        ("cross_kv", 2 * heads_width),
        ("attn_out", heads_width),
        ("qkv", 3 * heads_width),
    ]
    at, place = 0, {}
    for name, rows in sizes:
        place[name] = (at, rows)
        at += rows
    return place, at


def layer_kernel(
    dims,
    tok_h, og_h, text_h, wqkvT_h, wo_h, wcqT_h, wckv_h, wco_h, wup_h, wdn_h, wmod_h,
    seg_ref, time_ref, b_attn_out_ref, b_cross_out_ref, b_up_ref, b_mod_ref, tlen_ref,
    dtok_o, dtime_o, dtext_o, grads_o, early_o, late_o,
    tok, og, text, att, gc,
    wqkvT, wckv, wfull, wup, wdn, wmod,
    modbuf, mods, segrow, segcol, onehot, ktag,
    attn_in, na, qkvT, kvx, pself,
    stream_a, inv_c, cross_in, cqT, ckvT, kblk, vblk, pcross, catT, branch_own,
    mlp_in, nm_own, invm_own, act, slope, dpre, dbm, rs_send, rs_recv,
    gc_own, dcT, dcqT, dckvT, grad_own, dba, dOT, dqkvT,
    rs2_send, rs2_recv, dm, dmp, dmr, dsil, dsr, early, eall, lall,
    grads, rbuf,
    lsem, ssem, rsem, csem_s, csem_r, wsem_s, wsem_r, gsem_s, gsem_r, esem_s, esem_r, osem,
):
    dp_count, place, items = dims
    tp = lax.axis_index("tp")
    dp = lax.axis_index("dp")
    R = tok.shape[1]
    D = tok.shape[2]
    T = TP * R
    HW = att.shape[1]
    HL = HW // DH
    TK = TP * text.shape[1]
    TL = text.shape[1]
    HEADS = TP * HL
    MB = modbuf.shape[2]
    scale = 1.0 / math.sqrt(DH)
    sub = lax.rem(dp, 8)
    base8 = dp - sub
    core = lax.rem(sub, 2)
    chip = sub // 2

    def tp_peer(k):
        return {"tp": lax.rem(tp + k, TP)}

    def remote(src, dst, send, recv, peer):
        return pltpu.make_async_remote_copy(
            src_ref=src, dst_ref=dst, send_sem=send, recv_sem=recv, device_id=peer, device_id_type=MESH
        )

    def span(at, size, unit):
        return pl.ds(pl.multiple_of(at, unit), size)

    loads = [
        (wckv_h, wckv),
        (wo_h, wfull.at[0, 0]),
        (wcqT_h, wfull.at[0, 1]),
        (wco_h, wfull.at[0, 2]),
        (tok_h, tok.at[0]),
        (wmod_h, wmod),
        (wqkvT_h, wqkvT),
        (text_h, text.at[0]),
        (og_h, og.at[0]),
        (wup_h, wup),
        (wdn_h, wdn),
    ]
    local = [pltpu.make_async_copy(src, dst, lsem.at[i]) for i, (src, dst) in enumerate(loads)]
    for copy in local:
        copy.start()

    barrier = pltpu.get_barrier_semaphore()
    for k in range(1, TP):
        pl.semaphore_signal(barrier, inc=1, device_id=tp_peer(k), device_id_type=MESH)

    def greet(k, carry):
        pl.semaphore_signal(
            barrier, inc=1, device_id={"dp": lax.rem(dp + k, dp_count)}, device_id_type=MESH
        )
        return carry

    lax.fori_loop(1, dp_count, greet, 0)

    early[...] = jnp.zeros(early.shape, F32)
    for item in range(items):
        early[item : item + 1, :] = time_ref[item]
    time = early[...]
    sig = 1.0 / (1.0 + jnp.exp(-time))
    silu_low = (time * sig).astype(BF)
    early[...] = silu_low.astype(F32)
    local[5].wait()
    modbuf[tp] = dot_nn(silu_low, wmod[...]) + b_mod_ref[...].astype(F32).reshape(1, MB)
    local[0].wait()
    ident = (
        lax.broadcasted_iota(jnp.int32, (D, D), 0) == lax.broadcasted_iota(jnp.int32, (D, D), 1)
    ).astype(F32).astype(BF)
    wckvT = dot_tn(wckv[...], ident).astype(BF)
    wfull[0, 3] = wckvT[:HW]
    wfull[0, 4] = wckvT[HW:]
    for copy in local[1:5]:
        copy.wait()

    pl.semaphore_wait(barrier, TP - 1 + dp_count - 1)

    pending, chains = [], []
    inner = (tp > 0) & (tp < TP - 1)
    slot_a = jnp.where(tp == 3, 3, 1)
    slot_b = jnp.where((tp == 0) | (tp == 3), 2, 3)
    slot_c = jnp.where(tp == 0, 3, jnp.where(tp == 3, 1, 2))
    right, left = {"tp": lax.rem(tp + 1, TP)}, {"tp": lax.rem(tp + TP - 1, TP)}
    onward = {"tp": jnp.where(tp == 1, 0, TP - 1)}
    onward_slot = jnp.where(tp == 1, 3, 1)

    class Chain:
        def __init__(self, index, view):
            self.index, self.view, self.started = index, view, []
            chains.append(self)

        def copy(self, src, dst, send, chunk, peer):
            return remote(
                self.view(src, chunk), self.view(dst, chunk),
                csem_s.at[self.index, send, chunk], csem_r.at[self.index, dst, chunk], peer,
            )

        def start(self, chunk):
            self.started.append(chunk)

            @pl.when(tp < TP - 1)
            def _():
                self.copy(0, 3, 0, chunk, right).start()

            @pl.when(tp > 0)
            def _():
                self.copy(0, 1, 1, chunk, left).start()

        def step(self, which, chunk):
            slot = (slot_a, slot_b, slot_c)[which]
            self.copy(slot, slot, 2 + which, chunk, right).wait_recv()

            @pl.when(inner)
            def _():
                if which == 0:
                    self.copy(slot, 2, 2, chunk, left).start()
                elif which == 1:
                    self.copy(slot, 2, 3, chunk, right).start()
                else:
                    self.copy(slot, onward_slot, 4, chunk, onward).start()

        def finish(self):
            for chunk in self.started:

                @pl.when(tp < TP - 1)
                def _():
                    self.copy(0, 3, 0, chunk, right).wait_send()

                @pl.when(tp > 0)
                def _():
                    self.copy(0, 1, 1, chunk, left).wait_send()

                @pl.when(inner)
                def _():
                    self.copy(slot_a, 2, 2, chunk, left).wait_send()
                    self.copy(slot_b, 2, 3, chunk, right).wait_send()
                    self.copy(slot_c, onward_slot, 4, chunk, onward).wait_send()

    half = R // 2
    tok_chain = Chain(0, lambda slot, c: tok.at[slot, c * half : (c + 1) * half])
    text_chain = Chain(1, lambda slot, c: text.at[slot])
    WR, WC = HW // 4, D // 2
    wcol = pl.multiple_of(core * WC, 128)
    mats = (3, 4, 0, 1, 2)
    swapped = lax.rem(chip, 2) * 2 + chip // 2
    places = (chip, swapped, chip, swapped, chip)
    w_chain = Chain(2, lambda slot, c: wfull.at[slot, mats[c], span(places[c] * WR, WR, 16), pl.ds(wcol, WC)])
    att_chain = Chain(3, lambda slot, c: att.at[slot, c * DH : (c + 1) * DH])
    og_chain = Chain(4, lambda slot, c: og.at[slot, c * half : (c + 1) * half])
    split = R * 5 // 8
    gc_chain = Chain(5, lambda slot, c: gc.at[slot, c * split : R if c else split])

    class Plane:
        def __init__(self, index, bits):
            self.index, self.bits, self.open = index, bits, None

        def send(self, step, rows, bit):
            at = wfull.at[1:TP, mats[self.index], rows, pl.ds(wcol, WC)]
            copy = remote(
                at, at, wsem_s.at[self.index, step], wsem_r.at[self.index, step],
                {"dp": base8 + jnp.bitwise_xor(sub, bit)},
            )
            copy.start()
            pending.append(copy)
            self.open = copy

        def step(self, step):
            if step:
                self.open.wait_recv()
            place = places[self.index]
            if step == 0:
                self.send(0, span(place * WR, WR, 16), self.bits[0])
            elif step == 1:
                self.send(1, span(place // 2 * (2 * WR), 2 * WR, 16), self.bits[1])
            elif step == 2:
                self.send(2, slice(0, HW), 1)

    planes = [Plane(i, (4, 2) if i % 2 else (2, 4)) for i in range(5)]

    def direct(tag, src_of, dst_of):
        copies = []
        for k in range(1, TP):
            copy = remote(src_of(k), dst_of(k), ssem.at[tag, k], rsem.at[tag, TP - k], tp_peer(k))
            copy.start()
            copies.append(copy)
        pending.extend(copies)
        return copies

    def arrived(copies, slot):
        copies[TP - 1 - slot].wait_recv()

    w_chain.start(0)
    w_chain.start(1)
    tok_chain.start(0)
    tok_chain.start(1)
    mod_copies = direct(0, lambda k: modbuf.at[tp, 0:items], lambda k: modbuf.at[tp, 0:items])

    eye = lax.broadcasted_iota(jnp.int32, (R, R), 0) == lax.broadcasted_iota(jnp.int32, (R, R), 1)
    for slot in range(TP):
        owner = lax.rem(tp + slot, TP)
        row = seg_ref[:, pl.ds(pl.multiple_of(owner * R, R), R)].astype(F32)
        segrow[:, slot * R : (slot + 1) * R] = row
        col = jnp.sum(jnp.where(eye, row, 0.0), axis=1, keepdims=True)
        segcol[slot * R : (slot + 1) * R, :] = col
    kinds = lax.broadcasted_iota(jnp.int32, (16, T), 0)
    matches = (segrow[...] == kinds.astype(F32)) & (kinds < items)
    onehot[...] = jnp.where(matches | (kinds == items), 1.0, 0.0).astype(BF)
    key_at = lax.broadcasted_iota(jnp.int32, (TK, 1), 0)
    key_slot = key_at // TL
    key_item = lax.rem(key_at, TL) // (TL // items)
    key_pos = lax.rem(key_slot + tp, TP) * (TL // items) + lax.rem(key_at, TL // items)
    tag = jnp.full((TK, 1), -1.0, F32)
    for item in range(items):
        inside = (key_item == item) & (key_pos < tlen_ref[0, item])
        tag = jnp.where(inside, float(item), tag)
    ktag[...] = tag

    for k in range(1, TP):
        arrived(mod_copies, k)
    for j in range(6):
        lo, hi = j * D, (j + 1) * D
        at = lo
        while at < hi:
            block = at // MB
            end = min(hi, (block + 1) * MB)
            mods[j, 0:items, at - lo : end - lo] = modbuf[block, 0:items, at - block * MB : end - block * MB]
            at = end

    def per_frame(j, rows):
        col = segcol[rows, :]
        out = mods[j, items - 1 : items, :]
        for item in range(items - 2, -1, -1):
            out = jnp.where(col == float(item), mods[j, item : item + 1, :], out)
        return out

    def item_sums(rows, values):
        return dot_nn(onehot[:, rows], values.astype(BF))

    own, every = slice(0, R), slice(0, T)
    local[6].wait()

    def project(slot):
        rows = span(slot * R, R, R)
        normed, inverse = normalize(tok[slot].astype(F32))
        na[rows, :] = normed.astype(BF)
        x = (normed * (1.0 + per_frame(1, rows)) + per_frame(0, rows)).astype(BF)
        attn_in[rows, :] = x
        qkvT[:, rows] = dot_nt(wqkvT[...], x).astype(BF)

    def w_step(which, *chunks):
        for chunk in chunks:
            w_chain.step(which, chunk)
            if which == 2:
                planes[chunk].step(0)

    project(0)
    w_step(0, 0, 1)
    tok_chain.step(0, 0)
    tok_chain.step(0, 1)
    for chunk in (2, 3, 4):
        w_chain.start(chunk)
    local[7].wait()
    text_chain.start(0)
    w_step(1, 0, 1)
    tok_chain.step(1, 0)
    tok_chain.step(1, 1)
    w_step(2, 0, 1)
    project(slot_a)
    w_step(0, 2, 3, 4)
    planes[0].step(1)
    planes[1].step(1)
    project(slot_b)
    tok_chain.step(2, 0)
    tok_chain.step(2, 1)
    text_chain.step(0, 0)
    w_step(1, 2, 3, 4)
    project(slot_c)
    planes[0].step(2)
    planes[1].step(2)

    for h in range(HL):
        q0 = h * 3 * DH
        kvx[2 * h] = (qkvT[q0 + DH : q0 + 2 * DH, :].astype(F32).T * scale).astype(BF)
        kvx[2 * h + 1] = qkvT[q0 + 2 * DH : q0 + 3 * DH, :].astype(F32).T.astype(BF)
        scores = dot_nn(kvx[2 * h], qkvT[q0 : q0 + DH, :])
        scores = jnp.where(segcol[...] == segrow[...], scores, -1000000000.0)
        peak = jnp.max(scores, axis=0, keepdims=True)
        exponent = jnp.exp(scores - peak)
        probs = exponent * (1.0 / jnp.sum(exponent, axis=0, keepdims=True))
        pself[h] = probs
        att[0, h * DH : (h + 1) * DH, :] = dot_nn(qkvT[q0 + 2 * DH : q0 + 3 * DH, :], probs.astype(BF)).astype(BF)

    for h in range(HL):
        att_chain.start(h)
    w_step(2, 2, 3, 4)
    text_chain.step(1, 0)
    text_chain.step(2, 0)
    planes[0].step(3)
    planes[1].step(3)
    planes[2].step(1)
    planes[3].step(1)

    def full(i):
        return wfull[:, i].reshape(TP * HW, D)

    text_flat = text[...].reshape(TK, D)
    for s in range(TP):
        for part in range(2):
            ckvT[(2 * s + part) * HW : (2 * s + part + 1) * HW, :] = dot_nt(wfull[s, 3 + part], text_flat).astype(BF)
    quad = 4 * DH
    lane_head = lax.broadcasted_iota(jnp.int32, (TK, quad), 1) // DH
    for g in range(HEADS // 4):
        heads_at = [(4 * g + j) * 2 * DH for j in range(4)]
        for blocks, offset, factor in ((kblk, 0, scale), (vblk, DH, 1.0)):
            turned = jnp.concatenate(
                [ckvT[at + offset : at + offset + DH, :] for at in heads_at], axis=0
            ).astype(F32).T * factor
            for j in range(4):
                blocks[g, j * TK : (j + 1) * TK, :] = jnp.where(lane_head == j, turned, 0.0).astype(BF)
    planes[4].step(1)
    for h in range(HL):
        att_chain.step(0, h)
    planes[2].step(2)
    planes[3].step(2)
    for h in range(HL):
        att_chain.step(1, h)
    local[8].wait()
    og_chain.start(0)
    og_chain.start(1)
    planes[4].step(2)
    for h in range(HL):
        att_chain.step(2, h)
    for plane in planes[2:]:
        plane.step(3)
    og_chain.step(0, 0)
    og_chain.step(0, 1)

    b_attn_out = b_attn_out_ref[...].astype(F32).reshape(1, D)
    b_cross_out = b_cross_out_ref[...].astype(F32).reshape(1, D)
    b_up = b_up_ref[...].astype(F32).reshape(1, wup.shape[1])

    gathered = jnp.concatenate(
        [
            jnp.concatenate([att[k, :, (b - k) % TP * R : ((b - k) % TP + 1) * R] for b in range(TP)], axis=1)
            for k in range(TP)
        ],
        axis=0,
    )
    stream_a[...] = dot_tn(gathered, full(0)) + b_attn_out
    branch_own[...] = stream_a[own, :]
    stream_a[...] = tok[...].reshape(T, D).astype(F32) + per_frame(2, every) * stream_a[...]
    normed, inverse = normalize(stream_a[...])
    inv_c[...] = inverse
    cross_in[...] = normed.astype(BF)
    cqT[...] = dot_nt(full(1), cross_in[...]).astype(BF)
    allowed = ktag[...] == segrow[...]
    og_chain.step(1, 0)
    og_chain.step(1, 1)

    def cross_forward(g, carry):
        scores_all = dot_nn(kblk[g], cqT[span(g * quad, quad, quad), :])
        for j in range(4):
            h = 4 * g + j
            scores = jnp.where(allowed, scores_all[j * TK : (j + 1) * TK], -1000000000.0)
            peak = jnp.max(scores, axis=0, keepdims=True)
            exponent = jnp.exp(scores - peak)
            probs = exponent * (1.0 / jnp.sum(exponent, axis=0, keepdims=True))
            pcross[h] = probs
            vT = ckvT[span(h * 2 * DH + DH, DH, DH), :]
            catT[span(h * DH, DH, DH), :] = dot_nn(vT, probs.astype(BF)).astype(BF)
        return carry

    lax.fori_loop(0, HEADS // 4, cross_forward, 0)
    og_chain.step(2, 0)
    og_chain.step(2, 1)
    normed, inverse = normalize(stream_a[...] + dot_tn(catT[...], full(2)) + b_cross_out)
    nm_own[...] = normed[:R]
    invm_own[...] = inverse[:R]
    mlp_in[...] = (normed * (1.0 + per_frame(4, every)) + per_frame(3, every)).astype(BF)

    local[9].wait()
    local[10].wait()
    pre = dot_nn(mlp_in[...], wup[...]) + b_up
    square = pre * pre
    bend = jnp.tanh(GELU_C * pre * (1.0 + 0.044715 * square))
    act[...] = (0.5 * pre * (1.0 + bend)).astype(BF)
    slope[...] = 0.5 * (1.0 + bend) + 0.5 * pre * (1.0 - bend * bend) * (
        GELU_C * (1.0 + 3.0 * 0.044715 * square)
    )
    dbm[...] = (og[...].reshape(T, D).astype(F32) * per_frame(5, every)).astype(BF)
    dpre[...] = (dot_nt(dbm[...], wdn[...]) * slope[...]).astype(BF)
    rs_send[...] = dot_nt(dpre[...], wup[...]).astype(BF).reshape(TP, R, D)

    def to_owners(source, target, tag, rows):
        copies = {}
        for b in (2, 1, 3):
            copies[b] = remote(
                source.at[b, rows], target.at[TP - 1 - b, rows], ssem.at[tag, b], rsem.at[tag, TP - b], tp_peer(b)
            )
            copies[b].start()
        return copies

    halves = (slice(0, split), slice(split, R))
    rs_first = to_owners(rs_send, rs_recv, 1, halves[0])
    early[3:4, :] = dot_nn(onehot[...], dpre[...])[items : items + 1, :]

    bits = []
    step = 8
    while step < dp_count:
        bits.append(step)
        step *= 2

    class Reduce:
        def __init__(self, index, start, rows, room):
            self.parts = []
            half = rows // 2
            for part in range(2):
                chain = (1, 2, 4) if part == 0 else (1, 4, 2)
                self.parts.append((start + part * half, half, chain, part * half))
            self.index, self.room = index, room
            self.open, self.own = [], []

        def sem(self, part, step):
            return gsem_s.at[self.index, part, step], gsem_r.at[self.index, part, step]

        def launch(self, src, dst, part, step, bit):
            send, recv = self.sem(part, step)
            copy = remote(src, dst, send, recv, {"dp": jnp.bitwise_xor(dp, bit)})
            copy.start()
            pending.append(copy)
            return copy

        def bounds(self, part, level):
            start, rows, chain, _ = self.parts[part]
            at, size = start, rows
            for bit in chain[:level]:
                size //= 2
                at = at + jnp.bitwise_and(dp // bit, 1) * size
            return at, size

        def scatter_start(self, level):
            self.open = []
            for part in range(2):
                at, size = self.bounds(part, level)
                bit = self.parts[part][2][level]
                half = size // 2
                mine = jnp.bitwise_and(dp // bit, 1)
                other = pl.multiple_of(at + (1 - mine) * half, 16)
                rows = self.parts[part][1]
                room = self.room + 2 * (rows - (rows >> level)) + part * half
                copy = self.launch(
                    grads.at[pl.ds(other, half)], rbuf.at[room : room + half], part, level, bit
                )
                self.open.append((copy, room, half))

        def scatter_end(self, level):
            for part in range(2):
                copy, room, half = self.open[part]
                copy.wait_recv()
                at, size = self.bounds(part, level + 1)
                mine = pl.ds(pl.multiple_of(at, 16), half)
                grads[mine, :] = (grads[mine, :].astype(F32) + rbuf[room : room + half, :].astype(F32)).astype(BF)

        def widen(self):
            for i, bit in enumerate(bits):
                for part in range(2):
                    at, size = self.bounds(part, 3)
                    rows = self.parts[part][1]
                    mine = pl.ds(pl.multiple_of(at, 16), size)
                    room = self.room + 2 * (rows - rows // 8) + (2 * i + part) * size
                    copy = self.launch(grads.at[mine], rbuf.at[room : room + size], part, 6 + i, bit)
                    copy.wait_recv()
                    grads[mine, :] = (
                        grads[mine, :].astype(F32) + rbuf[room : room + size, :].astype(F32)
                    ).astype(BF)

        def gather_start(self, level):
            self.open = []
            source = grads if level == 2 else grads_o
            if level == 1:
                for copy in self.own:
                    copy.wait()
            for part in range(2):
                at, size = self.bounds(part, level + 1)
                bit = self.parts[part][2][level]
                mine = pl.ds(pl.multiple_of(at, 16), size)
                self.open.append(
                    self.launch(source.at[mine], grads_o.at[mine], part, 3 + (2 - level), bit)
                )
                if level == 2:
                    copy = pltpu.make_async_copy(grads.at[mine], grads_o.at[mine], osem.at[self.index, part])
                    copy.start()
                    self.own.append(copy)

        def gather_end(self):
            for copy in self.open:
                copy.wait_recv()

    mid0 = place["cross_out"][0]
    mid1 = place["attn_out"][0]
    total_rows = grads.shape[0]
    extra = 2 * len(bits)
    rooms, at = [], 0
    for rows in (mid0, mid1 - mid0, total_rows - mid1):
        rooms.append(at)
        at += rows - rows // 8 + extra * (rows // 16)
    reduce_mlp = Reduce(0, 0, mid0, rooms[0])
    reduce_cross = Reduce(1, mid0, mid1 - mid0, rooms[1])
    reduce_self = Reduce(2, mid1, total_rows - mid1, rooms[2])

    def put(name, values):
        at, rows = place[name]
        grads[at : at + rows, :] = values.astype(BF)

    put("up", dot_tn(mlp_in[...], dpre[...]))
    put("down", dot_tn(act[...], dbm[...]))
    reduce_mlp.scatter_start(0)
    dm[5] = item_sums(every, og[...].reshape(T, D).astype(F32) * dot_nn(act[...], wdn[...]))

    reduce_mlp.scatter_end(0)
    reduce_mlp.scatter_start(1)
    for copy in rs_first.values():
        copy.wait_send()
    rs_second = to_owners(rs_send, rs_recv, 5, halves[1])
    pending.extend(rs_second.values())

    def stream_grad(chunk, copies):
        rows = halves[chunk]
        d_mlp = rs_send[0, rows].astype(F32)
        for k in (1, 3, 2):
            copies[TP - k].wait_recv()
            d_mlp = d_mlp + rs_recv[k - 1, rows].astype(F32)
        grad_c = og[0, rows].astype(F32) + normalize_back(
            d_mlp * (1.0 + per_frame(4, rows)), nm_own[rows, :], invm_own[rows, :]
        )
        gc_own[rows, :] = grad_c
        gc[0, rows] = grad_c.astype(BF)
        gc_chain.start(chunk)
        return d_mlp

    first = stream_grad(0, rs_first)
    reduce_mlp.scatter_end(1)
    reduce_mlp.scatter_start(2)
    gc_chain.step(0, 0)
    second = stream_grad(1, rs_second)
    gc_chain.step(1, 0)
    reduce_mlp.scatter_end(2)
    reduce_mlp.widen()
    reduce_mlp.gather_start(2)
    d_mlp = jnp.concatenate([first, second], axis=0)
    dm[3] = item_sums(own, d_mlp)
    dm[4] = item_sums(own, d_mlp * nm_own[...])
    gc_chain.step(2, 0)

    gc_chain.step(0, 1)
    gc_chain.step(1, 1)
    reduce_mlp.gather_end()
    reduce_mlp.gather_start(1)
    gc_chain.step(2, 1)
    gc_flat = gc[...].reshape(T, D)
    dcT[...] = dot_nt(full(2), gc_flat).astype(BF)

    def cross_backward(g, carry):
        d_probs_all = dot_nn(vblk[g], dcT[span(g * quad, quad, quad), :])
        for j in range(4):
            h = 4 * g + j
            hr = span(h * DH, DH, DH)
            kr, vr = span(h * 2 * DH, DH, DH), span(h * 2 * DH + DH, DH, DH)
            probs = pcross[h]
            d_probs = d_probs_all[j * TK : (j + 1) * TK]
            d_scores = (probs * (d_probs - jnp.sum(probs * d_probs, axis=0, keepdims=True))).astype(BF)
            dcqT[hr, :] = (dot_nn(ckvT[kr, :], d_scores) * scale).astype(BF)
            dckvT[kr, :] = (dot_nt(cqT[hr, :], d_scores) * scale).astype(BF)
            dckvT[vr, :] = dot_nt(dcT[hr, :], probs.astype(BF)).astype(BF)
        return carry

    cross_backward(0, 0)
    put("cross_out", dot_nn(catT[0:HW, :], gc_flat))
    put("cross_q", dot_nn(dcqT[0:HW, :], cross_in[...]))
    put("cross_kv", dot_nn(dckvT[0 : 2 * HW, :], text_flat))
    reduce_cross.scatter_start(0)
    lax.fori_loop(1, HEADS // 4, cross_backward, 0)
    d_cross = dot_tn(dcqT[...], full(1))
    back = normalize_back(d_cross, cross_in[...].astype(F32), inv_c[...])
    grad = gc_own[...] + back[:R]
    grad_own[...] = grad
    gate = per_frame(2, every)
    dba[own, :] = (grad * gate[:R]).astype(BF)
    rest = slice(R, T)
    dba[rest, :] = ((gc_flat[R:].astype(F32) + back[R:]) * gate[R:]).astype(BF)
    dOT[...] = dot_nt(wfull[0, 0], dba[...]).astype(BF)
    reduce_cross.scatter_end(0)
    reduce_cross.scatter_start(1)

    put("attn_out", dot_nn(att[0], dba[...]))
    early[4:5, :] = dot_nn(onehot[...], gc_flat)[items : items + 1, :]
    early[5:6, :] = dot_nn(onehot[...], dba[...])[items : items + 1, :]
    eall[dp] = early[...]

    def dp_send(src, dst, index):
        def one(k, carry):
            peer = lax.rem(dp + k, dp_count)
            remote(
                src, dst, esem_s.at[index, k], esem_r.at[index, dp_count - k], {"dp": peer}
            ).start()
            return carry

        lax.fori_loop(1, dp_count, one, 0)

    def dp_wait(src, dst, index):
        def one(k, carry):
            remote(
                src, dst, esem_s.at[index, k], esem_r.at[index, k], {"dp": lax.rem(dp + k, dp_count)}
            ).wait()
            return carry

        lax.fori_loop(1, dp_count, one, 0)

    dp_send(eall.at[dp], eall.at[dp], 0)

    for h in range(HL):
        q0 = h * 3 * DH
        hr = slice(h * DH, (h + 1) * DH)
        probs = pself[h]
        d_probs = dot_nn(kvx[2 * h + 1], dOT[hr, :])
        d_scores = (probs * (d_probs - jnp.sum(probs * d_probs, axis=0, keepdims=True))).astype(BF)
        dqkvT[q0 : q0 + DH, :] = (dot_nn(qkvT[q0 + DH : q0 + 2 * DH, :], d_scores) * scale).astype(BF)
        dqkvT[q0 + DH : q0 + 2 * DH, :] = (dot_nt(qkvT[q0 : q0 + DH, :], d_scores) * scale).astype(BF)
        dqkvT[q0 + 2 * DH : q0 + 3 * DH, :] = dot_nt(dOT[hr, :], probs.astype(BF)).astype(BF)

    put("qkv", dot_nn(dqkvT[...], attn_in[...]))
    reduce_self.scatter_start(0)

    part = dot_tn(dqkvT[...], wqkvT[...])
    rs2_send[...] = part.astype(BF).reshape(TP, R, D)
    reduce_self.scatter_end(0)
    reduce_self.scatter_start(1)
    input_grad = rs2_send[...].reshape(T, D)
    dm[0] = dot_nn(onehot[...], input_grad)
    dm[1] = item_sums(every, input_grad.astype(F32) * na[...].astype(F32))
    dm[2] = item_sums(own, grad_own[...] * branch_own[...])

    for j in range(6):
        lo, hi = j * D, (j + 1) * D
        at = lo
        while at < hi:
            block = at // MB
            end = min(hi, (block + 1) * MB)
            dmp[block, :, at - block * MB : end - block * MB] = dm[j, 0:8, at - lo : end - lo]
            at = end
    dm_copies = direct(
        3, lambda k: dmp.at[lax.rem(tp + k, TP), 0:items], lambda k: dmr.at[TP - 1 - k, 0:items]
    )
    rs2_copies = to_owners(rs2_send, rs2_recv, 2, own)
    pending.extend(rs2_copies.values())
    reduce_cross.scatter_end(1)
    reduce_cross.scatter_start(2)
    reduce_mlp.gather_end()
    reduce_mlp.gather_start(0)

    dtext_o[...] = dot_tn(dckvT[:, 0:TL], wfull[:, 3:5].reshape(TP * 2 * HW, D)).astype(BF)
    reduce_self.scatter_end(1)
    reduce_self.scatter_start(2)
    reduce_cross.scatter_end(2)
    reduce_cross.widen()
    reduce_cross.gather_start(2)

    d_mod = dmp[tp, 0:items]
    for k in range(1, TP):
        arrived(dm_copies, k)
        d_mod = d_mod + dmr[k - 1, 0:items]
    low = d_mod.astype(BF)
    lall[dp, 0:items] = low.astype(F32)
    dsil[0:items, :] = dot_nt(low, wmod[...])
    ds_copies = direct(4, lambda k: dsil.at[0:items], lambda k: dsr.at[TP - 1 - k, 0:items])

    dp_send(lall.at[dp, 0:items], lall.at[dp, 0:items], 1)
    reduce_self.scatter_end(2)
    reduce_self.widen()
    reduce_self.gather_start(2)
    reduce_cross.gather_end()
    reduce_cross.gather_start(1)
    reduce_mlp.gather_end()
    dp_wait(eall.at[dp], eall.at[dp], 0)
    out_copies = [
        pltpu.make_async_copy(eall, early_o, osem.at[3, 0]),
        pltpu.make_async_copy(lall, late_o, osem.at[3, 1]),
    ]
    out_copies[0].start()
    reduce_self.gather_end()
    reduce_self.gather_start(1)
    reduce_cross.gather_end()
    reduce_cross.gather_start(0)
    d_silu = dsil[0:items, :]
    for k in range(1, TP):
        arrived(ds_copies, k)
        d_silu = d_silu + dsr[k - 1, 0:items]
    for item in range(items):
        value = time_ref[item]
        gate = 1.0 / (1.0 + jnp.exp(-value))
        dtime_o[item] = d_silu[item : item + 1, :] * (gate * (1.0 + value * (1.0 - gate)))
    dp_wait(lall.at[dp, 0:items], lall.at[dp, 0:items], 1)
    out_copies[1].start()
    normed, inverse = normalize(tok[0].astype(F32))
    reduce_self.gather_end()
    reduce_self.gather_start(0)

    d_in = rs2_send[0].astype(F32)
    for k in (1, 3, 2):
        rs2_copies[TP - k].wait_recv()
        d_in = d_in + rs2_recv[k - 1].astype(F32)
    dtok_o[...] = (
        grad_own[...] + normalize_back(d_in * (1.0 + per_frame(1, own)), normed, inverse)
    ).astype(BF)
    for chain in chains:
        chain.finish()
    reduce_cross.gather_end()
    reduce_self.gather_end()
    for copy in pending:
        copy.wait_send()
    for copy in out_copies:
        copy.wait()


def finish_kernel(
    place, items, grads_h, early_h, late_h, dtok_h, dtime_h, dtext_h,
    dtok_o, dtime_o, dtext_o, qkv_o, attn_out_o, cross_q_o, cross_kv_o, cross_out_o, up_o, down_o, mod_o,
    gb_attn_o, gb_cross_o, gb_up_o, gb_mod_o,
    low, full_v, kv_v, mod_v, early_v, late_v, dtok_v, dtime_v, dtext_v, isem, osem, ssem,
):
    names = ("up", "down", "qkv", "cross_kv", "attn_out", "cross_out", "cross_q")
    outs = {
        "up": up_o, "down": down_o, "qkv": qkv_o, "attn_out": attn_out_o, "cross_out": cross_out_o,
        "cross_q": cross_q_o, "cross_kv": cross_kv_o,
    }
    unit = 384
    chunks = []
    for name in names:
        at, rows = place[name]
        step = rows if name == "cross_kv" else math.gcd(rows, unit)
        chunks += [(name, at + i, step, i) for i in range(0, rows, step)]
    small = [
        pltpu.make_async_copy(early_h, early_v, ssem.at[0]),
        pltpu.make_async_copy(late_h, late_v, ssem.at[1]),
    ]
    through = [(dtok_h, dtok_v, dtok_o), (dtime_h, dtime_v, dtime_o), (dtext_h, dtext_v, dtext_o)]
    passed = [pltpu.make_async_copy(src, mid, ssem.at[2 + i]) for i, (src, mid, _) in enumerate(through)]
    stores = []
    loads = [
        pltpu.make_async_copy(grads_h.at[at : at + step], low.at[at : at + step], isem.at[i])
        for i, (_, at, step, _) in enumerate(chunks)
    ]
    for copy in small + passed + loads:
        copy.start()

    def store(src, dst, sem):
        copy = pltpu.make_async_copy(src, dst, sem)
        copy.start()
        stores.append(copy)

    for i, (name, at, step, offset) in enumerate(chunks):
        loads[i].wait()
        if name == "cross_kv":
            ident = (
                lax.broadcasted_iota(jnp.int32, (step, step), 0)
                == lax.broadcasted_iota(jnp.int32, (step, step), 1)
            ).astype(F32).astype(BF)
            kv_v[...] = dot_tn(low[at : at + step, :], ident)
            store(kv_v, outs[name], osem.at[i])
        else:
            full_v[at : at + step, :] = low[at : at + step, :].astype(F32)
            store(full_v.at[at : at + step], outs[name].at[offset : offset + step], osem.at[i])
    for copy in small + passed:
        copy.wait()
    for i, (_, mid, dst) in enumerate(through):
        store(mid, dst, ssem.at[8 + i])
    dp_count, slots, D = early_v.shape
    MB = late_v.shape[2]
    keep = lax.rem(lax.broadcasted_iota(jnp.int32, (dp_count * slots, MB), 0), slots) < items
    late = jnp.where(keep, late_v[...].reshape(dp_count * slots, MB), 0.0)
    early = early_v[...]
    left, right = early.reshape(dp_count * slots, D).astype(BF), late.astype(BF)
    parts = 3
    rows = D // parts
    for i in range(parts):
        piece = slice(i * rows, (i + 1) * rows)
        mod_v[piece, :] = dot_tn(left[:, piece], right)
        store(mod_v.at[piece], mod_o.at[piece], ssem.at[5 + i])
    gb_mod_o[...] = jnp.sum(late, axis=0)
    sums = jnp.sum(early, axis=0)
    gb_up_o[...] = sums[3]
    gb_cross_o[...] = sums[4]
    gb_attn_o[...] = sums[5]
    for copy in stores:
        copy.wait()


def body(
    dp_count,
    tokens,
    seg_ids,
    time_embed,
    text_states,
    text_lengths,
    out_grad,
    w_qkv,
    w_attn_out,
    b_attn_out,
    w_cross_q,
    w_cross_kv,
    w_cross_out,
    b_cross_out,
    w_up,
    b_up,
    w_down,
    w_mod,
    b_mod,
):
    _, R, D = tokens.shape
    T = R * TP
    items = time_embed.shape[1]
    shard_txt = text_states.shape[2]
    TL = items * shard_txt
    TK = TP * TL
    HW = w_cross_q.shape[1]
    HL = HW // DH
    HEADS = TP * HL
    FF = w_up.shape[1]
    MB = w_mod.shape[1]
    place, total_rows = bucket_rows(FF, HW)
    text = text_states[0].reshape(TL, D)

    extra = 0
    step = 8
    while step < dp_count:
        extra += 1
        step *= 2
    room = total_rows - total_rows // 8 + 2 * extra * (total_rows // 16)

    hbm = pl.BlockSpec(memory_space=pl.ANY)
    vmem = pl.BlockSpec(memory_space=pltpu.VMEM)
    smem = pl.BlockSpec(memory_space=pltpu.SMEM)
    V = pltpu.VMEM
    DMA = pltpu.SemaphoreType.DMA
    chunks = max(HL, 5)
    scratch = [
        V((TP, R, D), BF), V((TP, R, D), BF), V((TP, TL, D), BF), V((TP, HW, T), BF), V((TP, R, D), BF),
        V((3 * HW, D), BF), V((D, 2 * HW), BF), V((TP, 5, HW, D), BF),
        V((D, FF), BF), V((FF, D), BF), V((D, MB), BF),
        V((TP, 8, MB), F32), V((6, 8, D), F32), V((1, T), F32), V((T, 1), F32), V((16, T), BF), V((TK, 1), F32),
        V((T, D), BF), V((T, D), BF), V((3 * HW, T), BF), V((2 * HL, T, DH), BF), V((HL, T, T), F32),
        V((T, D), F32), V((T, 1), F32), V((T, D), BF), V((TP * HW, T), BF), V((TP * 2 * HW, TK), BF),
        V((HEADS // 4, 4 * TK, 4 * DH), BF), V((HEADS // 4, 4 * TK, 4 * DH), BF), V((HEADS, TK, T), F32), V((TP * HW, T), BF), V((R, D), F32),
        V((T, D), BF), V((R, D), F32), V((R, 1), F32), V((T, FF), BF), V((T, FF), F32), V((T, FF), BF), V((T, D), BF),
        V((TP, R, D), BF), V((TP - 1, R, D), BF),
        V((R, D), F32), V((TP * HW, T), BF), V((TP * HW, T), BF),
        V((TP * 2 * HW, TK), BF), V((R, D), F32), V((T, D), BF), V((HW, T), BF), V((3 * HW, T), BF),
        V((TP, R, D), BF), V((TP - 1, R, D), BF),
        V((6, 16, D), F32), V((TP, 8, MB), F32), V((TP - 1, 8, MB), F32), V((8, D), F32), V((TP - 1, 8, D), F32),
        V((8, D), F32), V((dp_count, 8, D), F32), V((dp_count, 8, MB), F32),
        V((total_rows, D), BF), V((room, D), BF),
        DMA((11,)), DMA((6, TP)), DMA((6, TP)), DMA((6, 5, chunks)), DMA((6, TP, chunks)), DMA((5, 3)), DMA((5, 3)),
        DMA((3, 2, 6 + extra)), DMA((3, 2, 6 + extra)), DMA((2, dp_count)), DMA((2, dp_count)), DMA((4, 2)),
    ]
    d_tokens, d_time, d_text, grads, early, late = pl.pallas_call(
        functools.partial(layer_kernel, (dp_count, place, items)),
        out_shape=(
            jax.ShapeDtypeStruct((R, D), BF),
            jax.ShapeDtypeStruct((items, 1, D), F32),
            jax.ShapeDtypeStruct((TL, D), BF),
            jax.ShapeDtypeStruct((total_rows, D), BF),
            jax.ShapeDtypeStruct((dp_count, 8, D), F32),
            jax.ShapeDtypeStruct((dp_count, 8, MB), F32),
        ),
        in_specs=[hbm] * 11 + [vmem] * 6 + [smem],
        out_specs=(vmem, vmem, vmem, hbm, hbm, hbm),
        scratch_shapes=scratch,
        name="layer",
        compiler_params=pltpu.CompilerParams(
            collective_id=0, has_side_effects=True, vmem_limit_bytes=63 * 1024 * 1024
        ),
    )(
        tokens[0], out_grad[0], text, w_qkv.T, w_attn_out, w_cross_q.T, w_cross_kv, w_cross_out,
        w_up, w_down, w_mod, seg_ids, jnp.transpose(time_embed, (1, 0, 2)),
        b_attn_out, b_cross_out, b_up, b_mod, text_lengths,
    )

    f32 = lambda *shape: jax.ShapeDtypeStruct(shape, F32)
    d_tokens, d_time, d_text, g_qkv, g_attn, g_cq, g_ckv, g_co, g_up, g_down, g_mod, gb_attn, gb_cross, gb_up, gb_mod = pl.pallas_call(
        functools.partial(finish_kernel, place, items),
        out_shape=(
            jax.ShapeDtypeStruct((R, D), BF), f32(items, 1, D), jax.ShapeDtypeStruct((TL, D), BF),
            f32(3 * HW, D), f32(HW, D), f32(HW, D), f32(D, 2 * HW), f32(HW, D), f32(FF, D), f32(FF, D),
            f32(D, MB), f32(D), f32(D), f32(FF), f32(MB),
        ),
        in_specs=[hbm] * 6,
        out_specs=(hbm,) * 11 + (vmem,) * 4,
        scratch_shapes=[
            V((total_rows, D), BF), V((total_rows, D), F32), V((D, 2 * HW), F32), V((D, MB), F32),
            V((dp_count, 8, D), F32), V((dp_count, 8, MB), F32), V((R, D), BF), V((items, 1, D), F32), V((TL, D), BF),
            DMA((16,)), DMA((16,)), DMA((11,)),
        ],
        name="finish",
        compiler_params=pltpu.CompilerParams(vmem_limit_bytes=63 * 1024 * 1024),
    )(grads, early, late, d_tokens, d_time, d_text)
    return (
        d_tokens[None],
        jnp.transpose(d_time, (1, 0, 2)),
        d_text.reshape(1, items, shard_txt, D),
        g_qkv.T,
        g_attn,
        gb_attn,
        g_cq.T,
        g_ckv,
        g_co,
        gb_cross,
        g_up,
        gb_up,
        g_down,
        g_mod,
        gb_mod,
    )


def solution(mesh):
    placed = (
        P("dp", "tp", None),
        P("dp", None),
        P("dp", None, None),
        P("dp", None, "tp", None),
        P("dp", None),
        P("dp", "tp", None),
        P(None, "tp"),
        P("tp", None),
        P(),
        P(None, "tp"),
        P(None, "tp"),
        P("tp", None),
        P(),
        P(None, "tp"),
        P("tp"),
        P("tp", None),
        P(None, "tp"),
        P("tp"),
    )
    return jax.shard_map(
        functools.partial(body, mesh.shape["dp"]),
        mesh=mesh,
        in_specs=placed,
        out_specs=(
            P("dp", "tp", None),
            P("dp", None, None),
            P("dp", None, "tp", None),
            P(None, "tp"),
            P("tp", None),
            P(),
            P(None, "tp"),
            P(None, "tp"),
            P("tp", None),
            P(),
            P(None, "tp"),
            P("tp"),
            P("tp", None),
            P(None, "tp"),
            P("tp"),
        ),
        check_vma=False,
    )
```

```python
import functools
import math

import jax
import jax.numpy as jnp
from jax import lax
from jax.experimental import pallas as pl
from jax.experimental.pallas import tpu as pltpu
from jax.sharding import PartitionSpec as P

DH = 64
TP = 4
MESH = pl.DeviceIdType.MESH
BF = jnp.bfloat16
F32 = jnp.float32
GELU_C = math.sqrt(2.0 / math.pi)


def dot_nn(left, right):
    return jnp.dot(left, right, preferred_element_type=F32)


def dot_tn(left, right):
    return lax.dot_general(left, right, (((0,), (0,)), ((), ())), preferred_element_type=F32)


def dot_nt(left, right):
    return lax.dot_general(left, right, (((1,), (1,)), ((), ())), preferred_element_type=F32)


def normalize(values):
    center = values - jnp.mean(values, axis=-1, keepdims=True)
    inverse = lax.rsqrt(jnp.mean(center * center, axis=-1, keepdims=True) + 1e-06)
    return center * inverse, inverse


def normalize_back(grad, normed, inverse):
    return inverse * (
        grad
        - jnp.mean(grad, axis=-1, keepdims=True)
        - normed * jnp.mean(grad * normed, axis=-1, keepdims=True)
    )


def bucket_rows(hidden, heads_width):
    sizes = [
        ("up", hidden),
        ("down", hidden),
        ("cross_out", heads_width),
        ("cross_q", heads_width),
        ("cross_kv", 2 * heads_width),
        ("attn_out", heads_width),
        ("qkv", 3 * heads_width),
    ]
    at, place = 0, {}
    for name, rows in sizes:
        place[name] = (at, rows)
        at += rows
    return place, at


def layer_kernel(
    dims,
    tok_h, og_h, text_h, wqkvT_h, wo_h, wcqT_h, wckv_h, wco_h, wup_h, wdn_h, wmod_h,
    seg_ref, time_ref, b_attn_out_ref, b_cross_out_ref, b_up_ref, b_mod_ref, tlen_ref,
    dtok_o, dtime_o, dtext_o, grads_o, early_o, late_o,
    tok, og, text, att, gc,
    wqkvT, wckv, wfull, wup, wdn, wmod,
    modbuf, mods, segrow, segcol, onehot, ktag,
    attn_in, na, qkvT, kvx, pself,
    stream_a, inv_c, cross_in, cqT, ckvT, kblk, vblk, pcross, catT, branch_own,
    mlp_in, nm_own, invm_own, act, slope, dpre, dbm, rs_send, rs_recv,
    gc_own, dcT, dcqT, dckvT, grad_own, dba, dOT, dqkvT,
    rs2_send, rs2_recv, dm, dmp, dmr, dsil, dsr, early, eall, lall,
    grads, rbuf,
    lsem, ssem, rsem, csem_s, csem_r, wsem_s, wsem_r, gsem_s, gsem_r, esem_s, esem_r, osem,
):
    dp_count, place, items = dims
    tp = lax.axis_index("tp")
    dp = lax.axis_index("dp")
    R = tok.shape[1]
    D = tok.shape[2]
    T = TP * R
    HW = att.shape[1]
    HL = HW // DH
    TK = TP * text.shape[1]
    TL = text.shape[1]
    HEADS = TP * HL
    MB = modbuf.shape[2]
    scale = 1.0 / math.sqrt(DH)
    sub = lax.rem(dp, 8)
    base8 = dp - sub
    core = lax.rem(sub, 2)
    chip = sub // 2

    def tp_peer(k):
        return {"tp": lax.rem(tp + k, TP)}

    def remote(src, dst, send, recv, peer):
        return pltpu.make_async_remote_copy(
            src_ref=src, dst_ref=dst, send_sem=send, recv_sem=recv, device_id=peer, device_id_type=MESH
        )

    def span(at, size, unit):
        return pl.ds(pl.multiple_of(at, unit), size)

    loads = [
        (wckv_h, wckv),
        (wo_h, wfull.at[0, 0]),
        (wcqT_h, wfull.at[0, 1]),
        (wco_h, wfull.at[0, 2]),
        (tok_h, tok.at[0]),
        (wmod_h, wmod),
        (wqkvT_h, wqkvT),
        (text_h, text.at[0]),
        (og_h, og.at[0]),
        (wup_h, wup),
        (wdn_h, wdn),
    ]
    local = [pltpu.make_async_copy(src, dst, lsem.at[i]) for i, (src, dst) in enumerate(loads)]
    for copy in local:
        copy.start()

    barrier = pltpu.get_barrier_semaphore()
    for k in range(1, TP):
        pl.semaphore_signal(barrier, inc=1, device_id=tp_peer(k), device_id_type=MESH)

    def greet(k, carry):
        pl.semaphore_signal(
            barrier, inc=1, device_id={"dp": lax.rem(dp + k, dp_count)}, device_id_type=MESH
        )
        return carry

    lax.fori_loop(1, dp_count, greet, 0)

    early[...] = jnp.zeros(early.shape, F32)
    for item in range(items):
        early[item : item + 1, :] = time_ref[item]
    time = early[...]
    sig = 1.0 / (1.0 + jnp.exp(-time))
    silu_low = (time * sig).astype(BF)
    early[...] = silu_low.astype(F32)
    local[5].wait()
    modbuf[tp] = dot_nn(silu_low, wmod[...]) + b_mod_ref[...].astype(F32).reshape(1, MB)
    local[0].wait()
    ident = (
        lax.broadcasted_iota(jnp.int32, (D, D), 0) == lax.broadcasted_iota(jnp.int32, (D, D), 1)
    ).astype(F32).astype(BF)
    wckvT = dot_tn(wckv[...], ident).astype(BF)
    wfull[0, 3] = wckvT[:HW]
    wfull[0, 4] = wckvT[HW:]
    for copy in local[1:5]:
        copy.wait()

    pl.semaphore_wait(barrier, TP - 1 + dp_count - 1)

    pending, chains = [], []
    inner = (tp > 0) & (tp < TP - 1)
    slot_a = jnp.where(tp == 3, 3, 1)
    slot_b = jnp.where((tp == 0) | (tp == 3), 2, 3)
    slot_c = jnp.where(tp == 0, 3, jnp.where(tp == 3, 1, 2))
    right, left = {"tp": lax.rem(tp + 1, TP)}, {"tp": lax.rem(tp + TP - 1, TP)}
    onward = {"tp": jnp.where(tp == 1, 0, TP - 1)}
    onward_slot = jnp.where(tp == 1, 3, 1)

    class Chain:
        def __init__(self, index, view):
            self.index, self.view, self.started = index, view, []
            chains.append(self)

        def copy(self, src, dst, send, chunk, peer):
            return remote(
                self.view(src, chunk), self.view(dst, chunk),
                csem_s.at[self.index, send, chunk], csem_r.at[self.index, dst, chunk], peer,
            )

        def start(self, chunk):
            self.started.append(chunk)

            @pl.when(tp < TP - 1)
            def _():
                self.copy(0, 3, 0, chunk, right).start()

            @pl.when(tp > 0)
            def _():
                self.copy(0, 1, 1, chunk, left).start()

        def step(self, which, chunk):
            slot = (slot_a, slot_b, slot_c)[which]
            self.copy(slot, slot, 2 + which, chunk, right).wait_recv()

            @pl.when(inner)
            def _():
                if which == 0:
                    self.copy(slot, 2, 2, chunk, left).start()
                elif which == 1:
                    self.copy(slot, 2, 3, chunk, right).start()
                else:
                    self.copy(slot, onward_slot, 4, chunk, onward).start()

        def finish(self):
            for chunk in self.started:

                @pl.when(tp < TP - 1)
                def _():
                    self.copy(0, 3, 0, chunk, right).wait_send()

                @pl.when(tp > 0)
                def _():
                    self.copy(0, 1, 1, chunk, left).wait_send()

                @pl.when(inner)
                def _():
                    self.copy(slot_a, 2, 2, chunk, left).wait_send()
                    self.copy(slot_b, 2, 3, chunk, right).wait_send()
                    self.copy(slot_c, onward_slot, 4, chunk, onward).wait_send()

    half = R // 2
    tok_chain = Chain(0, lambda slot, c: tok.at[slot, c * half : (c + 1) * half])
    text_chain = Chain(1, lambda slot, c: text.at[slot])
    WR, WC = HW // 4, D // 2
    wcol = pl.multiple_of(core * WC, 128)
    mats = (3, 4, 0, 1, 2)
    swapped = lax.rem(chip, 2) * 2 + chip // 2
    places = (chip, swapped, chip, swapped, chip)
    w_chain = Chain(2, lambda slot, c: wfull.at[slot, mats[c], span(places[c] * WR, WR, 16), pl.ds(wcol, WC)])
    att_chain = Chain(3, lambda slot, c: att.at[slot, c * DH : (c + 1) * DH])
    og_chain = Chain(4, lambda slot, c: og.at[slot, c * half : (c + 1) * half])
    split = R * 5 // 8
    gc_chain = Chain(5, lambda slot, c: gc.at[slot, c * split : R if c else split])

    class Plane:
        def __init__(self, index, bits):
            self.index, self.bits, self.open = index, bits, None

        def send(self, step, rows, bit):
            at = wfull.at[1:TP, mats[self.index], rows, pl.ds(wcol, WC)]
            copy = remote(
                at, at, wsem_s.at[self.index, step], wsem_r.at[self.index, step],
                {"dp": base8 + jnp.bitwise_xor(sub, bit)},
            )
            copy.start()
            pending.append(copy)
            self.open = copy

        def step(self, step):
            if step:
                self.open.wait_recv()
            place = places[self.index]
            if step == 0:
                self.send(0, span(place * WR, WR, 16), self.bits[0])
            elif step == 1:
                self.send(1, span(place // 2 * (2 * WR), 2 * WR, 16), self.bits[1])
            elif step == 2:
                self.send(2, slice(0, HW), 1)

    planes = [Plane(i, (4, 2) if i % 2 else (2, 4)) for i in range(5)]

    def direct(tag, src_of, dst_of):
        copies = []
        for k in range(1, TP):
            copy = remote(src_of(k), dst_of(k), ssem.at[tag, k], rsem.at[tag, TP - k], tp_peer(k))
            copy.start()
            copies.append(copy)
        pending.extend(copies)
        return copies

    def arrived(copies, slot):
        copies[TP - 1 - slot].wait_recv()

    w_chain.start(0)
    w_chain.start(1)
    tok_chain.start(0)
    tok_chain.start(1)
    mod_copies = direct(0, lambda k: modbuf.at[tp, 0:items], lambda k: modbuf.at[tp, 0:items])

    eye = lax.broadcasted_iota(jnp.int32, (R, R), 0) == lax.broadcasted_iota(jnp.int32, (R, R), 1)
    for slot in range(TP):
        owner = lax.rem(tp + slot, TP)
        row = seg_ref[:, pl.ds(pl.multiple_of(owner * R, R), R)].astype(F32)
        segrow[:, slot * R : (slot + 1) * R] = row
        col = jnp.sum(jnp.where(eye, row, 0.0), axis=1, keepdims=True)
        segcol[slot * R : (slot + 1) * R, :] = col
    kinds = lax.broadcasted_iota(jnp.int32, (16, T), 0)
    matches = (segrow[...] == kinds.astype(F32)) & (kinds < items)
    onehot[...] = jnp.where(matches | (kinds == items), 1.0, 0.0).astype(BF)
    key_at = lax.broadcasted_iota(jnp.int32, (TK, 1), 0)
    key_slot = key_at // TL
    key_item = lax.rem(key_at, TL) // (TL // items)
    key_pos = lax.rem(key_slot + tp, TP) * (TL // items) + lax.rem(key_at, TL // items)
    tag = jnp.full((TK, 1), -1.0, F32)
    for item in range(items):
        inside = (key_item == item) & (key_pos < tlen_ref[0, item])
        tag = jnp.where(inside, float(item), tag)
    ktag[...] = tag

    for k in range(1, TP):
        arrived(mod_copies, k)
    for j in range(6):
        lo, hi = j * D, (j + 1) * D
        at = lo
        while at < hi:
            block = at // MB
            end = min(hi, (block + 1) * MB)
            mods[j, 0:items, at - lo : end - lo] = modbuf[block, 0:items, at - block * MB : end - block * MB]
            at = end

    def per_frame(j, rows):
        col = segcol[rows, :]
        out = mods[j, items - 1 : items, :]
        for item in range(items - 2, -1, -1):
            out = jnp.where(col == float(item), mods[j, item : item + 1, :], out)
        return out

    def item_sums(rows, values):
        return dot_nn(onehot[:, rows], values.astype(BF))

    own, every = slice(0, R), slice(0, T)
    local[6].wait()

    def project(slot):
        rows = span(slot * R, R, R)
        normed, inverse = normalize(tok[slot].astype(F32))
        na[rows, :] = normed.astype(BF)
        x = (normed * (1.0 + per_frame(1, rows)) + per_frame(0, rows)).astype(BF)
        attn_in[rows, :] = x
        qkvT[:, rows] = dot_nt(wqkvT[...], x).astype(BF)

    def w_step(which, *chunks):
        for chunk in chunks:
            w_chain.step(which, chunk)
            if which == 2:
                planes[chunk].step(0)

    project(0)
    w_step(0, 0, 1)
    tok_chain.step(0, 0)
    tok_chain.step(0, 1)
    for chunk in (2, 3, 4):
        w_chain.start(chunk)
    local[7].wait()
    text_chain.start(0)
    w_step(1, 0, 1)
    tok_chain.step(1, 0)
    tok_chain.step(1, 1)
    w_step(2, 0, 1)
    project(slot_a)
    w_step(0, 2, 3, 4)
    planes[0].step(1)
    planes[1].step(1)
    project(slot_b)
    tok_chain.step(2, 0)
    tok_chain.step(2, 1)
    text_chain.step(0, 0)
    w_step(1, 2, 3, 4)
    project(slot_c)
    planes[0].step(2)
    planes[1].step(2)

    for h in range(HL):
        q0 = h * 3 * DH
        kvx[2 * h] = (qkvT[q0 + DH : q0 + 2 * DH, :].astype(F32).T * scale).astype(BF)
        kvx[2 * h + 1] = qkvT[q0 + 2 * DH : q0 + 3 * DH, :].astype(F32).T.astype(BF)
        scores = dot_nn(kvx[2 * h], qkvT[q0 : q0 + DH, :])
        scores = jnp.where(segcol[...] == segrow[...], scores, -1000000000.0)
        peak = jnp.max(scores, axis=0, keepdims=True)
        exponent = jnp.exp(scores - peak)
        probs = exponent * (1.0 / jnp.sum(exponent, axis=0, keepdims=True))
        pself[h] = probs
        att[0, h * DH : (h + 1) * DH, :] = dot_nn(qkvT[q0 + 2 * DH : q0 + 3 * DH, :], probs.astype(BF)).astype(BF)

    for h in range(HL):
        att_chain.start(h)
    w_step(2, 2, 3, 4)
    text_chain.step(1, 0)
    text_chain.step(2, 0)
    planes[0].step(3)
    planes[1].step(3)
    planes[2].step(1)
    planes[3].step(1)

    def full(i):
        return wfull[:, i].reshape(TP * HW, D)

    text_flat = text[...].reshape(TK, D)
    for s in range(TP):
        for part in range(2):
            ckvT[(2 * s + part) * HW : (2 * s + part + 1) * HW, :] = dot_nt(wfull[s, 3 + part], text_flat).astype(BF)
    quad = 4 * DH
    lane_head = lax.broadcasted_iota(jnp.int32, (TK, quad), 1) // DH
    for g in range(HEADS // 4):
        heads_at = [(4 * g + j) * 2 * DH for j in range(4)]
        for blocks, offset, factor in ((kblk, 0, scale), (vblk, DH, 1.0)):
            turned = jnp.concatenate(
                [ckvT[at + offset : at + offset + DH, :] for at in heads_at], axis=0
            ).astype(F32).T * factor
            for j in range(4):
                blocks[g, j * TK : (j + 1) * TK, :] = jnp.where(lane_head == j, turned, 0.0).astype(BF)
    planes[4].step(1)
    for h in range(HL):
        att_chain.step(0, h)
    planes[2].step(2)
    planes[3].step(2)
    for h in range(HL):
        att_chain.step(1, h)
    local[8].wait()
    og_chain.start(0)
    og_chain.start(1)
    planes[4].step(2)
    for h in range(HL):
        att_chain.step(2, h)
    for plane in planes[2:]:
        plane.step(3)
    og_chain.step(0, 0)
    og_chain.step(0, 1)

    b_attn_out = b_attn_out_ref[...].astype(F32).reshape(1, D)
    b_cross_out = b_cross_out_ref[...].astype(F32).reshape(1, D)
    b_up = b_up_ref[...].astype(F32).reshape(1, wup.shape[1])

    gathered = jnp.concatenate(
        [
            jnp.concatenate([att[k, :, (b - k) % TP * R : ((b - k) % TP + 1) * R] for b in range(TP)], axis=1)
            for k in range(TP)
        ],
        axis=0,
    )
    stream_a[...] = dot_tn(gathered, full(0)) + b_attn_out
    branch_own[...] = stream_a[own, :]
    stream_a[...] = tok[...].reshape(T, D).astype(F32) + per_frame(2, every) * stream_a[...]
    normed, inverse = normalize(stream_a[...])
    inv_c[...] = inverse
    cross_in[...] = normed.astype(BF)
    cqT[...] = dot_nt(full(1), cross_in[...]).astype(BF)
    allowed = ktag[...] == segrow[...]
    og_chain.step(1, 0)
    og_chain.step(1, 1)

    def cross_forward(g, carry):
        scores_all = dot_nn(kblk[g], cqT[span(g * quad, quad, quad), :])
        for j in range(4):
            h = 4 * g + j
            scores = jnp.where(allowed, scores_all[j * TK : (j + 1) * TK], -1000000000.0)
            peak = jnp.max(scores, axis=0, keepdims=True)
            exponent = jnp.exp(scores - peak)
            probs = exponent * (1.0 / jnp.sum(exponent, axis=0, keepdims=True))
            pcross[h] = probs
            vT = ckvT[span(h * 2 * DH + DH, DH, DH), :]
            catT[span(h * DH, DH, DH), :] = dot_nn(vT, probs.astype(BF)).astype(BF)
        return carry

    for g in range(HEADS // 4):
        cross_forward(g, 0)
    og_chain.step(2, 0)
    og_chain.step(2, 1)
    normed, inverse = normalize(stream_a[...] + dot_tn(catT[...], full(2)) + b_cross_out)
    nm_own[...] = normed[:R]
    invm_own[...] = inverse[:R]
    mlp_in[...] = (normed * (1.0 + per_frame(4, every)) + per_frame(3, every)).astype(BF)

    local[9].wait()
    local[10].wait()
    pre = dot_nn(mlp_in[...], wup[...]) + b_up
    square = pre * pre
    bend = jnp.tanh(GELU_C * pre * (1.0 + 0.044715 * square))
    act[...] = (0.5 * pre * (1.0 + bend)).astype(BF)
    slope[...] = 0.5 * (1.0 + bend) + 0.5 * pre * (1.0 - bend * bend) * (
        GELU_C * (1.0 + 3.0 * 0.044715 * square)
    )
    dbm[...] = (og[...].reshape(T, D).astype(F32) * per_frame(5, every)).astype(BF)
    dpre[...] = (dot_nt(dbm[...], wdn[...]) * slope[...]).astype(BF)
    rs_send[...] = dot_nt(dpre[...], wup[...]).astype(BF).reshape(TP, R, D)

    def to_owners(source, target, tag, rows):
        copies = {}
        for b in (2, 1, 3):
            copies[b] = remote(
                source.at[b, rows], target.at[TP - 1 - b, rows], ssem.at[tag, b], rsem.at[tag, TP - b], tp_peer(b)
            )
            copies[b].start()
        return copies

    halves = (slice(0, split), slice(split, R))
    rs_first = to_owners(rs_send, rs_recv, 1, halves[0])
    early[3:4, :] = dot_nn(onehot[...], dpre[...])[items : items + 1, :]

    bits = []
    step = 8
    while step < dp_count:
        bits.append(step)
        step *= 2

    class Reduce:
        def __init__(self, index, start, rows, room):
            self.parts = []
            half = rows // 2
            for part in range(2):
                chain = (1, 2, 4) if part == 0 else (1, 4, 2)
                self.parts.append((start + part * half, half, chain, part * half))
            self.index, self.room = index, room
            self.open, self.own = [], []

        def sem(self, part, step):
            return gsem_s.at[self.index, part, step], gsem_r.at[self.index, part, step]

        def launch(self, src, dst, part, step, bit):
            send, recv = self.sem(part, step)
            copy = remote(src, dst, send, recv, {"dp": jnp.bitwise_xor(dp, bit)})
            copy.start()
            pending.append(copy)
            return copy

        def bounds(self, part, level):
            start, rows, chain, _ = self.parts[part]
            at, size = start, rows
            for bit in chain[:level]:
                size //= 2
                at = at + jnp.bitwise_and(dp // bit, 1) * size
            return at, size

        def scatter_start(self, level):
            self.open = []
            for part in range(2):
                at, size = self.bounds(part, level)
                bit = self.parts[part][2][level]
                half = size // 2
                mine = jnp.bitwise_and(dp // bit, 1)
                other = pl.multiple_of(at + (1 - mine) * half, 16)
                rows = self.parts[part][1]
                room = self.room + 2 * (rows - (rows >> level)) + part * half
                copy = self.launch(
                    grads.at[pl.ds(other, half)], rbuf.at[room : room + half], part, level, bit
                )
                self.open.append((copy, room, half))

        def scatter_end(self, level):
            for part in range(2):
                copy, room, half = self.open[part]
                copy.wait_recv()
                at, size = self.bounds(part, level + 1)
                mine = pl.ds(pl.multiple_of(at, 16), half)
                grads[mine, :] = (grads[mine, :].astype(F32) + rbuf[room : room + half, :].astype(F32)).astype(BF)

        def widen(self):
            for i, bit in enumerate(bits):
                for part in range(2):
                    at, size = self.bounds(part, 3)
                    rows = self.parts[part][1]
                    mine = pl.ds(pl.multiple_of(at, 16), size)
                    room = self.room + 2 * (rows - rows // 8) + (2 * i + part) * size
                    copy = self.launch(grads.at[mine], rbuf.at[room : room + size], part, 6 + i, bit)
                    copy.wait_recv()
                    grads[mine, :] = (
                        grads[mine, :].astype(F32) + rbuf[room : room + size, :].astype(F32)
                    ).astype(BF)

        def gather_start(self, level):
            self.open = []
            source = grads if level == 2 else grads_o
            if level == 1:
                for copy in self.own:
                    copy.wait()
            for part in range(2):
                at, size = self.bounds(part, level + 1)
                bit = self.parts[part][2][level]
                mine = pl.ds(pl.multiple_of(at, 16), size)
                self.open.append(
                    self.launch(source.at[mine], grads_o.at[mine], part, 3 + (2 - level), bit)
                )
                if level == 2:
                    copy = pltpu.make_async_copy(grads.at[mine], grads_o.at[mine], osem.at[self.index, part])
                    copy.start()
                    self.own.append(copy)

        def gather_end(self):
            for copy in self.open:
                copy.wait_recv()

    mid0 = place["cross_out"][0]
    mid1 = place["attn_out"][0]
    total_rows = grads.shape[0]
    extra = 2 * len(bits)
    rooms, at = [], 0
    for rows in (mid0, mid1 - mid0, total_rows - mid1):
        rooms.append(at)
        at += rows - rows // 8 + extra * (rows // 16)
    reduce_mlp = Reduce(0, 0, mid0, rooms[0])
    reduce_cross = Reduce(1, mid0, mid1 - mid0, rooms[1])
    reduce_self = Reduce(2, mid1, total_rows - mid1, rooms[2])

    def put(name, values):
        at, rows = place[name]
        grads[at : at + rows, :] = values.astype(BF)

    put("up", dot_tn(mlp_in[...], dpre[...]))
    put("down", dot_tn(act[...], dbm[...]))
    reduce_mlp.scatter_start(0)
    dm[5] = item_sums(every, og[...].reshape(T, D).astype(F32) * dot_nn(act[...], wdn[...]))

    reduce_mlp.scatter_end(0)
    reduce_mlp.scatter_start(1)
    for copy in rs_first.values():
        copy.wait_send()
    rs_second = to_owners(rs_send, rs_recv, 5, halves[1])
    pending.extend(rs_second.values())

    def stream_grad(chunk, copies):
        rows = halves[chunk]
        d_mlp = rs_send[0, rows].astype(F32)
        for k in (1, 3, 2):
            copies[TP - k].wait_recv()
            d_mlp = d_mlp + rs_recv[k - 1, rows].astype(F32)
        grad_c = og[0, rows].astype(F32) + normalize_back(
            d_mlp * (1.0 + per_frame(4, rows)), nm_own[rows, :], invm_own[rows, :]
        )
        gc_own[rows, :] = grad_c
        gc[0, rows] = grad_c.astype(BF)
        gc_chain.start(chunk)
        return d_mlp

    first = stream_grad(0, rs_first)
    reduce_mlp.scatter_end(1)
    reduce_mlp.scatter_start(2)
    gc_chain.step(0, 0)
    second = stream_grad(1, rs_second)
    gc_chain.step(1, 0)
    reduce_mlp.scatter_end(2)
    reduce_mlp.widen()
    reduce_mlp.gather_start(2)
    d_mlp = jnp.concatenate([first, second], axis=0)
    dm[3] = item_sums(own, d_mlp)
    dm[4] = item_sums(own, d_mlp * nm_own[...])
    gc_chain.step(2, 0)

    gc_chain.step(0, 1)
    gc_chain.step(1, 1)
    reduce_mlp.gather_end()
    reduce_mlp.gather_start(1)
    gc_chain.step(2, 1)
    gc_flat = gc[...].reshape(T, D)
    dcT[...] = dot_nt(full(2), gc_flat).astype(BF)

    def cross_backward(g, carry):
        d_probs_all = dot_nn(vblk[g], dcT[span(g * quad, quad, quad), :])
        for j in range(4):
            h = 4 * g + j
            hr = span(h * DH, DH, DH)
            kr, vr = span(h * 2 * DH, DH, DH), span(h * 2 * DH + DH, DH, DH)
            probs = pcross[h]
            d_probs = d_probs_all[j * TK : (j + 1) * TK]
            d_scores = (probs * (d_probs - jnp.sum(probs * d_probs, axis=0, keepdims=True))).astype(BF)
            dcqT[hr, :] = (dot_nn(ckvT[kr, :], d_scores) * scale).astype(BF)
            dckvT[kr, :] = (dot_nt(cqT[hr, :], d_scores) * scale).astype(BF)
            dckvT[vr, :] = dot_nt(dcT[hr, :], probs.astype(BF)).astype(BF)
        return carry

    cross_backward(0, 0)
    put("cross_out", dot_nn(catT[0:HW, :], gc_flat))
    put("cross_q", dot_nn(dcqT[0:HW, :], cross_in[...]))
    put("cross_kv", dot_nn(dckvT[0 : 2 * HW, :], text_flat))
    reduce_cross.scatter_start(0)
    lax.fori_loop(1, HEADS // 4, cross_backward, 0)
    d_cross = dot_tn(dcqT[...], full(1))
    back = normalize_back(d_cross, cross_in[...].astype(F32), inv_c[...])
    grad = gc_own[...] + back[:R]
    grad_own[...] = grad
    gate = per_frame(2, every)
    dba[own, :] = (grad * gate[:R]).astype(BF)
    rest = slice(R, T)
    dba[rest, :] = ((gc_flat[R:].astype(F32) + back[R:]) * gate[R:]).astype(BF)
    dOT[...] = dot_nt(wfull[0, 0], dba[...]).astype(BF)
    reduce_cross.scatter_end(0)
    reduce_cross.scatter_start(1)

    put("attn_out", dot_nn(att[0], dba[...]))
    early[4:5, :] = dot_nn(onehot[...], gc_flat)[items : items + 1, :]
    early[5:6, :] = dot_nn(onehot[...], dba[...])[items : items + 1, :]
    eall[dp] = early[...]

    def dp_send(src, dst, index):
        def one(k, carry):
            peer = lax.rem(dp + k, dp_count)
            remote(
                src, dst, esem_s.at[index, k], esem_r.at[index, dp_count - k], {"dp": peer}
            ).start()
            return carry

        lax.fori_loop(1, dp_count, one, 0)

    def dp_wait(src, dst, index):
        def one(k, carry):
            remote(
                src, dst, esem_s.at[index, k], esem_r.at[index, k], {"dp": lax.rem(dp + k, dp_count)}
            ).wait()
            return carry

        lax.fori_loop(1, dp_count, one, 0)

    dp_send(eall.at[dp], eall.at[dp], 0)

    reduce_mlp.gather_end()
    reduce_mlp.gather_start(0)

    for h in range(HL):
        q0 = h * 3 * DH
        hr = slice(h * DH, (h + 1) * DH)
        probs = pself[h]
        d_probs = dot_nn(kvx[2 * h + 1], dOT[hr, :])
        d_scores = (probs * (d_probs - jnp.sum(probs * d_probs, axis=0, keepdims=True))).astype(BF)
        dqkvT[q0 : q0 + DH, :] = (dot_nn(qkvT[q0 + DH : q0 + 2 * DH, :], d_scores) * scale).astype(BF)
        dqkvT[q0 + DH : q0 + 2 * DH, :] = (dot_nt(qkvT[q0 : q0 + DH, :], d_scores) * scale).astype(BF)
        dqkvT[q0 + 2 * DH : q0 + 3 * DH, :] = dot_nt(dOT[hr, :], probs.astype(BF)).astype(BF)

    put("qkv", dot_nn(dqkvT[...], attn_in[...]))
    reduce_self.scatter_start(0)

    part = dot_tn(dqkvT[...], wqkvT[...])
    rs2_send[...] = part.astype(BF).reshape(TP, R, D)
    reduce_self.scatter_end(0)
    reduce_self.scatter_start(1)
    input_grad = rs2_send[...].reshape(T, D)
    dm[0] = dot_nn(onehot[...], input_grad)
    dm[1] = item_sums(every, input_grad.astype(F32) * na[...].astype(F32))
    dm[2] = item_sums(own, grad_own[...] * branch_own[...])

    for j in range(6):
        lo, hi = j * D, (j + 1) * D
        at = lo
        while at < hi:
            block = at // MB
            end = min(hi, (block + 1) * MB)
            dmp[block, :, at - block * MB : end - block * MB] = dm[j, 0:8, at - lo : end - lo]
            at = end
    dm_copies = direct(
        3, lambda k: dmp.at[lax.rem(tp + k, TP), 0:items], lambda k: dmr.at[TP - 1 - k, 0:items]
    )
    rs2_copies = to_owners(rs2_send, rs2_recv, 2, own)
    pending.extend(rs2_copies.values())
    reduce_cross.scatter_end(1)
    reduce_cross.scatter_start(2)

    dtext_o[...] = dot_tn(dckvT[:, 0:TL], wfull[:, 3:5].reshape(TP * 2 * HW, D)).astype(BF)
    reduce_self.scatter_end(1)
    reduce_self.scatter_start(2)
    reduce_cross.scatter_end(2)
    reduce_cross.widen()
    reduce_cross.gather_start(2)

    d_mod = dmp[tp, 0:items]
    for k in range(1, TP):
        arrived(dm_copies, k)
        d_mod = d_mod + dmr[k - 1, 0:items]
    low = d_mod.astype(BF)
    lall[dp, 0:items] = low.astype(F32)
    dsil[0:items, :] = dot_nt(low, wmod[...])
    ds_copies = direct(4, lambda k: dsil.at[0:items], lambda k: dsr.at[TP - 1 - k, 0:items])

    dp_send(lall.at[dp, 0:items], lall.at[dp, 0:items], 1)
    reduce_self.scatter_end(2)
    reduce_self.widen()
    reduce_self.gather_start(2)
    reduce_cross.gather_end()
    reduce_cross.gather_start(1)
    reduce_mlp.gather_end()
    dp_wait(eall.at[dp], eall.at[dp], 0)
    out_copies = [
        pltpu.make_async_copy(eall, early_o, osem.at[3, 0]),
        pltpu.make_async_copy(lall, late_o, osem.at[3, 1]),
    ]
    out_copies[0].start()
    reduce_self.gather_end()
    reduce_self.gather_start(1)
    reduce_cross.gather_end()
    reduce_cross.gather_start(0)
    dp_wait(lall.at[dp, 0:items], lall.at[dp, 0:items], 1)
    out_copies[1].start()
    normed, inverse = normalize(tok[0].astype(F32))
    reduce_self.gather_end()
    reduce_self.gather_start(0)

    d_in = rs2_send[0].astype(F32)
    for k in (1, 3, 2):
        rs2_copies[TP - k].wait_recv()
        d_in = d_in + rs2_recv[k - 1].astype(F32)
    dtok_o[...] = (
        grad_own[...] + normalize_back(d_in * (1.0 + per_frame(1, own)), normed, inverse)
    ).astype(BF)
    d_silu = dsil[0:items, :]
    for k in range(1, TP):
        arrived(ds_copies, k)
        d_silu = d_silu + dsr[k - 1, 0:items]
    for item in range(items):
        value = time_ref[item]
        gate = 1.0 / (1.0 + jnp.exp(-value))
        dtime_o[item] = d_silu[item : item + 1, :] * (gate * (1.0 + value * (1.0 - gate)))
    for chain in chains:
        chain.finish()
    reduce_cross.gather_end()
    reduce_self.gather_end()
    for copy in pending:
        copy.wait_send()
    for copy in out_copies:
        copy.wait()


def finish_kernel(
    place, items, grads_h, early_h, late_h, dtok_h, dtime_h, dtext_h,
    dtok_o, dtime_o, dtext_o, qkv_o, attn_out_o, cross_q_o, cross_kv_o, cross_out_o, up_o, down_o, mod_o,
    gb_attn_o, gb_cross_o, gb_up_o, gb_mod_o,
    low, full_v, kv_v, mod_v, early_v, late_v, dtok_v, dtime_v, dtext_v, isem, osem, ssem,
):
    names = ("up", "down", "qkv", "cross_kv", "attn_out", "cross_out", "cross_q")
    outs = {
        "up": up_o, "down": down_o, "qkv": qkv_o, "attn_out": attn_out_o, "cross_out": cross_out_o,
        "cross_q": cross_q_o, "cross_kv": cross_kv_o,
    }
    unit = 384
    chunks = []
    for name in names:
        at, rows = place[name]
        step = rows if name == "cross_kv" else math.gcd(rows, unit)
        chunks += [(name, at + i, step, i) for i in range(0, rows, step)]
    small = [
        pltpu.make_async_copy(early_h, early_v, ssem.at[0]),
        pltpu.make_async_copy(late_h, late_v, ssem.at[1]),
    ]
    through = [(dtok_h, dtok_v, dtok_o), (dtime_h, dtime_v, dtime_o), (dtext_h, dtext_v, dtext_o)]
    passed = [pltpu.make_async_copy(src, mid, ssem.at[2 + i]) for i, (src, mid, _) in enumerate(through)]
    stores = []
    loads = [
        pltpu.make_async_copy(grads_h.at[at : at + step], low.at[at : at + step], isem.at[i])
        for i, (_, at, step, _) in enumerate(chunks)
    ]
    for copy in small + passed + loads:
        copy.start()

    def store(src, dst, sem):
        copy = pltpu.make_async_copy(src, dst, sem)
        copy.start()
        stores.append(copy)

    for i, (name, at, step, offset) in enumerate(chunks):
        loads[i].wait()
        if name == "cross_kv":
            ident = (
                lax.broadcasted_iota(jnp.int32, (step, step), 0)
                == lax.broadcasted_iota(jnp.int32, (step, step), 1)
            ).astype(F32).astype(BF)
            kv_v[...] = dot_tn(low[at : at + step, :], ident)
            store(kv_v, outs[name], osem.at[i])
        else:
            full_v[at : at + step, :] = low[at : at + step, :].astype(F32)
            store(full_v.at[at : at + step], outs[name].at[offset : offset + step], osem.at[i])
    for copy in small + passed:
        copy.wait()
    for i, (_, mid, dst) in enumerate(through):
        store(mid, dst, ssem.at[8 + i])
    dp_count, slots, D = early_v.shape
    MB = late_v.shape[2]
    keep = lax.rem(lax.broadcasted_iota(jnp.int32, (dp_count * slots, MB), 0), slots) < items
    late = jnp.where(keep, late_v[...].reshape(dp_count * slots, MB), 0.0)
    early = early_v[...]
    left, right = early.reshape(dp_count * slots, D).astype(BF), late.astype(BF)
    parts = 3
    rows = D // parts
    for i in range(parts):
        piece = slice(i * rows, (i + 1) * rows)
        mod_v[piece, :] = dot_tn(left[:, piece], right)
        store(mod_v.at[piece], mod_o.at[piece], ssem.at[5 + i])
    gb_mod_o[...] = jnp.sum(late, axis=0)
    sums = jnp.sum(early, axis=0)
    gb_up_o[...] = sums[3]
    gb_cross_o[...] = sums[4]
    gb_attn_o[...] = sums[5]
    for copy in stores:
        copy.wait()


def body(
    dp_count,
    tokens,
    seg_ids,
    time_embed,
    text_states,
    text_lengths,
    out_grad,
    w_qkv,
    w_attn_out,
    b_attn_out,
    w_cross_q,
    w_cross_kv,
    w_cross_out,
    b_cross_out,
    w_up,
    b_up,
    w_down,
    w_mod,
    b_mod,
):
    _, R, D = tokens.shape
    T = R * TP
    items = time_embed.shape[1]
    shard_txt = text_states.shape[2]
    TL = items * shard_txt
    TK = TP * TL
    HW = w_cross_q.shape[1]
    HL = HW // DH
    HEADS = TP * HL
    FF = w_up.shape[1]
    MB = w_mod.shape[1]
    place, total_rows = bucket_rows(FF, HW)
    text = text_states[0].reshape(TL, D)

    extra = 0
    step = 8
    while step < dp_count:
        extra += 1
        step *= 2
    room = total_rows - total_rows // 8 + 2 * extra * (total_rows // 16)

    hbm = pl.BlockSpec(memory_space=pl.ANY)
    vmem = pl.BlockSpec(memory_space=pltpu.VMEM)
    smem = pl.BlockSpec(memory_space=pltpu.SMEM)
    V = pltpu.VMEM
    DMA = pltpu.SemaphoreType.DMA
    chunks = max(HL, 5)
    scratch = [
        V((TP, R, D), BF), V((TP, R, D), BF), V((TP, TL, D), BF), V((TP, HW, T), BF), V((TP, R, D), BF),
        V((3 * HW, D), BF), V((D, 2 * HW), BF), V((TP, 5, HW, D), BF),
        V((D, FF), BF), V((FF, D), BF), V((D, MB), BF),
        V((TP, 8, MB), F32), V((6, 8, D), F32), V((1, T), F32), V((T, 1), F32), V((16, T), BF), V((TK, 1), F32),
        V((T, D), BF), V((T, D), BF), V((3 * HW, T), BF), V((2 * HL, T, DH), BF), V((HL, T, T), F32),
        V((T, D), F32), V((T, 1), F32), V((T, D), BF), V((TP * HW, T), BF), V((TP * 2 * HW, TK), BF),
        V((HEADS // 4, 4 * TK, 4 * DH), BF), V((HEADS // 4, 4 * TK, 4 * DH), BF), V((HEADS, TK, T), F32), V((TP * HW, T), BF), V((R, D), F32),
        V((T, D), BF), V((R, D), F32), V((R, 1), F32), V((T, FF), BF), V((T, FF), F32), V((T, FF), BF), V((T, D), BF),
        V((TP, R, D), BF), V((TP - 1, R, D), BF),
        V((R, D), F32), V((TP * HW, T), BF), V((TP * HW, T), BF),
        V((TP * 2 * HW, TK), BF), V((R, D), F32), V((T, D), BF), V((HW, T), BF), V((3 * HW, T), BF),
        V((TP, R, D), BF), V((TP - 1, R, D), BF),
        V((6, 16, D), F32), V((TP, 8, MB), F32), V((TP - 1, 8, MB), F32), V((8, D), F32), V((TP - 1, 8, D), F32),
        V((8, D), F32), V((dp_count, 8, D), F32), V((dp_count, 8, MB), F32),
        V((total_rows, D), BF), V((room, D), BF),
        DMA((11,)), DMA((6, TP)), DMA((6, TP)), DMA((6, 5, chunks)), DMA((6, TP, chunks)), DMA((5, 3)), DMA((5, 3)),
        DMA((3, 2, 6 + extra)), DMA((3, 2, 6 + extra)), DMA((2, dp_count)), DMA((2, dp_count)), DMA((4, 2)),
    ]
    d_tokens, d_time, d_text, grads, early, late = pl.pallas_call(
        functools.partial(layer_kernel, (dp_count, place, items)),
        out_shape=(
            jax.ShapeDtypeStruct((R, D), BF),
            jax.ShapeDtypeStruct((items, 1, D), F32),
            jax.ShapeDtypeStruct((TL, D), BF),
            jax.ShapeDtypeStruct((total_rows, D), BF),
            jax.ShapeDtypeStruct((dp_count, 8, D), F32),
            jax.ShapeDtypeStruct((dp_count, 8, MB), F32),
        ),
        in_specs=[hbm] * 11 + [vmem] * 6 + [smem],
        out_specs=(vmem, vmem, vmem, hbm, hbm, hbm),
        scratch_shapes=scratch,
        name="layer",
        compiler_params=pltpu.CompilerParams(
            collective_id=0, has_side_effects=True, vmem_limit_bytes=63 * 1024 * 1024
        ),
    )(
        tokens[0], out_grad[0], text, w_qkv.T, w_attn_out, w_cross_q.T, w_cross_kv, w_cross_out,
        w_up, w_down, w_mod, seg_ids, jnp.transpose(time_embed, (1, 0, 2)),
        b_attn_out, b_cross_out, b_up, b_mod, text_lengths,
    )

    f32 = lambda *shape: jax.ShapeDtypeStruct(shape, F32)
    d_tokens, d_time, d_text, g_qkv, g_attn, g_cq, g_ckv, g_co, g_up, g_down, g_mod, gb_attn, gb_cross, gb_up, gb_mod = pl.pallas_call(
        functools.partial(finish_kernel, place, items),
        out_shape=(
            jax.ShapeDtypeStruct((R, D), BF), f32(items, 1, D), jax.ShapeDtypeStruct((TL, D), BF),
            f32(3 * HW, D), f32(HW, D), f32(HW, D), f32(D, 2 * HW), f32(HW, D), f32(FF, D), f32(FF, D),
            f32(D, MB), f32(D), f32(D), f32(FF), f32(MB),
        ),
        in_specs=[hbm] * 6,
        out_specs=(hbm,) * 11 + (vmem,) * 4,
        scratch_shapes=[
            V((total_rows, D), BF), V((total_rows, D), F32), V((D, 2 * HW), F32), V((D, MB), F32),
            V((dp_count, 8, D), F32), V((dp_count, 8, MB), F32), V((R, D), BF), V((items, 1, D), F32), V((TL, D), BF),
            DMA((16,)), DMA((16,)), DMA((11,)),
        ],
        name="finish",
        compiler_params=pltpu.CompilerParams(vmem_limit_bytes=63 * 1024 * 1024),
    )(grads, early, late, d_tokens, d_time, d_text)
    return (
        d_tokens[None],
        jnp.transpose(d_time, (1, 0, 2)),
        d_text.reshape(1, items, shard_txt, D),
        g_qkv.T,
        g_attn,
        gb_attn,
        g_cq.T,
        g_ckv,
        g_co,
        gb_cross,
        g_up,
        gb_up,
        g_down,
        g_mod,
        gb_mod,
    )


def solution(mesh):
    placed = (
        P("dp", "tp", None),
        P("dp", None),
        P("dp", None, None),
        P("dp", None, "tp", None),
        P("dp", None),
        P("dp", "tp", None),
        P(None, "tp"),
        P("tp", None),
        P(),
        P(None, "tp"),
        P(None, "tp"),
        P("tp", None),
        P(),
        P(None, "tp"),
        P("tp"),
        P("tp", None),
        P(None, "tp"),
        P("tp"),
    )
    return jax.shard_map(
        functools.partial(body, mesh.shape["dp"]),
        mesh=mesh,
        in_specs=placed,
        out_specs=(
            P("dp", "tp", None),
            P("dp", None, None),
            P("dp", None, "tp", None),
            P(None, "tp"),
            P("tp", None),
            P(),
            P(None, "tp"),
            P(None, "tp"),
            P("tp", None),
            P(),
            P(None, "tp"),
            P("tp"),
            P("tp", None),
            P(None, "tp"),
            P("tp"),
        ),
        check_vma=False,
    )
```
